32 devices in a mesh: patch: 4 (over y, x), curve: 8 (over z, core).
Axes of the slice: x: 2, y: 2, z: 4, core: 2. Of those that a mesh axis runs over, the one named last changes fastest.
Arguments:
- points: bfloat16 [8, 4, 256, 512], P('curve', 'patch'), may hold values from -6 to 6
- norm_gain_one: float32 [512], replicated, may hold values from 0.4 to 2.5, as said below
- qkv_one: bfloat16 [512, 1536], replicated, may hold values from -0.25 to 0.25
- out_one: bfloat16 [512, 512], replicated, may hold values from -0.25 to 0.25
- hilbert_pos: int32 [8, 4, 256], P('curve', 'patch'), may hold values from 0 to 2047, as said below
- norm_gain_two: float32 [512], replicated, may hold values from 0.4 to 2.5, as said below
- qkv_two: bfloat16 [512, 1536], replicated, may hold values from -0.25 to 0.25
- out_two: bfloat16 [512, 512], replicated, may hold values from -0.25 to 0.25
- hilbert_seg: int32 [4, 8, 256], P('patch', 'curve'), may hold values from 0 to 7, never falling along the last dimension, each value on 1 to 128 neighbouring positions
- out_grad: bfloat16 [4, 8, 256, 512], P('patch', 'curve'), may hold values from -6 to 6
Outputs:
- point_grad: bfloat16 [8, 4, 256, 512], P('curve', 'patch')
The draws below stay inside these ranges and needn't reach their ends.
Inputs may be any that keep to these rules, and one draw needn't show every extreme that they name: `hilbert_pos`: for each index p of the second dimension, the values over all c and i form a permutation of 0 to 2047. From the points of one device at most 64 have q // 256 equal to any one value, and in every draw some device sends exactly 64 to some owner. `hilbert_seg`: within one device's slots the numbers never fall; a patch holds at most 128 slots. `norm_gain_one`: positive gains. `norm_gain_two`: positive gains.
All inputs are finite; a program needn't handle non-finite values.
Results may differ from the reference program's by a relative error of at most 0.02.
Values may be sent and summed in bfloat16 or wider, within the bound.
No kernel may reach another device: no remote copies, remote signals or barrier semaphores. Data moves between devices by JAX's collectives and lax.ppermute only.
A program may use at most 64 MiB of HBM per device.

```python
import math
import jax
import jax.numpy as jnp
import numpy as np
from jax import lax

D = 512
HEADS = 16
ROWS = 256
SEG_COUNT = 8
SEG_MOST = 128
PATCH = 1024
N_PATCH = 4
N_CURVE = 8


def pair_counts(key):
    base = ROWS // N_CURVE
    half = N_CURVE // 2
    extra = jax.random.randint(jax.random.fold_in(key, 1), (half,), 0, base + 1)
    extra = extra.at[0].set(base)
    counts = jnp.concatenate([base + extra, base - extra])
    counts = counts[jax.random.permutation(jax.random.fold_in(key, 2), N_CURVE)]
    labels = jax.random.permutation(jax.random.fold_in(key, 3), N_CURVE)
    return counts[(labels[None, :] - labels[:, None]) % N_CURVE]


def group_positions(key):
    pairs = pair_counts(key)
    slots = jnp.arange(ROWS)

    def one_source(counts_row, source_key):
        ends = jnp.cumsum(counts_row)
        starts = ends - counts_row
        owner = jnp.repeat(jnp.arange(N_CURVE), counts_row, total_repeat_length=ROWS)
        ranking = slots - starts[owner]
        shuffle = jax.random.permutation(source_key, ROWS)
        return (owner[shuffle], ranking[shuffle])
    source_keys = jax.random.split(jax.random.fold_in(key, 4), N_CURVE)
    owner, ranking = jax.vmap(one_source)(pairs, source_keys)
    incoming_base = jnp.cumsum(pairs, axis=0) - pairs
    incoming = incoming_base[jnp.arange(N_CURVE)[:, None], owner] + ranking
    dest_keys = jax.random.split(jax.random.fold_in(key, 5), N_CURVE)
    shuffles = jax.vmap(lambda dest_key: jax.random.permutation(dest_key, ROWS))(dest_keys)
    offset = shuffles[owner, incoming]
    return owner * ROWS + offset


def draw_hilbert_pos(key, part):
    groups = [group_positions(jax.random.fold_in(key, 100 + index)) for index in range(N_PATCH)]
    return jnp.stack(groups, axis=1).astype(jnp.int32)


def gain_values(key):
    return jnp.exp(jax.random.uniform(key, (D,), jnp.float32, math.log(0.5), math.log(2.0)))


def draw_norm_gain_one(key, part):
    return gain_values(jax.random.fold_in(key, 7))


def draw_norm_gain_two(key, part):
    return gain_values(jax.random.fold_in(key, 8))


def shard_levels(rng, extent, cuts, smallest, top_value):
    factor_of = 1.0
    for position, blocks in cuts:
        draws = jax.random.uniform(jax.random.fold_in(jax.random.fold_in(rng, 6), position), (blocks,), jnp.float32, smallest / len(cuts), top_value / len(cuts))
        factor_of = factor_of * jnp.repeat(jnp.exp(draws), extent[position] // blocks).reshape((-1,) + (1,) * (len(extent) - 1 - position))
    return factor_of


def split_up(number_of, total, limit, skew):
    loads = [(1 << 20) // math.isqrt(grade ** skew) + 1 for grade in range(2, number_of + 1)]
    spare, given = total - limit - (number_of - 1), [1] * (number_of - 1)
    while spare > 0:
        movable = [i for i in range(number_of - 1) if given[i] < limit]
        mass, left = sum([loads[i] for i in movable]), spare
        for i in movable:
            addition = min(limit - given[i], max(1, left * loads[i] // mass), spare)
            given[i] = given[i] + addition
            spare = spare - addition
    return np.array([limit] + given)


def uneven(own_key, count, total, reach, slope):
    if count == 2:
        one = jax.random.randint(own_key, (), max(1, total - reach), min(reach, total - 1) + 1)
        return jnp.stack([one, total - one])
    lengths = jnp.asarray(split_up(count, total, reach, slope), jnp.int32)
    twos = (count - 1) // 2
    source_of, sink = lengths[1:1 + 2 * twos:2], lengths[2:2 + 2 * twos:2]
    room = jnp.minimum(source_of - 1, reach - sink)
    passed = jax.random.randint(jax.random.fold_in(own_key, 1), (twos,), 0, 1 << 20) % (room + 1)
    lengths = lengths.at[1:1 + 2 * twos:2].set(source_of - passed).at[2:2 + 2 * twos:2].set(sink + passed)
    return lengths[jax.random.permutation(jax.random.fold_in(own_key, 2), count)]


def bell_draw(own_key, extent, deviation, bound, cuts=(), dtype=jnp.bfloat16):
    drawn = jax.random.normal(own_key, extent, jnp.float32) * deviation
    if len(cuts) > 0:
        drawn = shard_levels(own_key, extent, cuts, -0.22, 0.18) * drawn
    return jnp.clip(drawn, min=-bound, max=bound).astype(dtype)


def setup_inputs(seed: int = 0) -> dict:
    seeds = jax.random.split(jax.random.key(seed), 11)
    points = bell_draw(seeds[0], (N_CURVE, N_PATCH, ROWS, D), 1.0, 6.0, ((0, 8), (1, 4)))
    norm_gain_one = draw_norm_gain_one(jax.random.fold_in(seeds[10], 71), 0)
    qkv_one = bell_draw(seeds[2], (D, 3 * D), D ** -0.5, 0.25)
    out_one = bell_draw(seeds[3], (D, D), D ** -0.5, 0.25)
    hilbert_pos = draw_hilbert_pos(jax.random.fold_in(seeds[10], 71), 0)
    norm_gain_two = draw_norm_gain_two(jax.random.fold_in(seeds[10], 71), 0)
    qkv_two = bell_draw(seeds[6], (D, 3 * D), D ** -0.5, 0.25)
    out_two = bell_draw(seeds[7], (D, D), D ** -0.5, 0.25)
    hilbert_seg = jax.vmap(lambda own: jnp.searchsorted(jnp.cumsum(uneven(own, SEG_COUNT, ROWS, SEG_MOST, 2)), jnp.arange(ROWS), side="right"))(jax.random.split(seeds[8], N_PATCH * N_CURVE)).reshape((N_PATCH, N_CURVE, ROWS)).astype(jnp.int32)
    out_grad = bell_draw(seeds[9], (N_PATCH, N_CURVE, ROWS, D), 1.0, 6.0, ((0, 4), (1, 8)))
    return dict(points=points, norm_gain_one=norm_gain_one, qkv_one=qkv_one, out_one=out_one, hilbert_pos=hilbert_pos, norm_gain_two=norm_gain_two, qkv_two=qkv_two, out_two=out_two, hilbert_seg=hilbert_seg, out_grad=out_grad)


EPS = 1e-06

def prepare(source_rows, gain, w_qkv):
    wide = source_rows.astype(jnp.float32)
    power = lax.optimization_barrier(jnp.mean(wide * wide, axis=-1, keepdims=True))
    normed = (wide * lax.rsqrt(power + EPS) * gain).astype(jnp.bfloat16)
    return jnp.dot(normed, w_qkv, preferred_element_type=jnp.float32).astype(jnp.bfloat16)

def finish(source_rows, mixed, w_out):
    total = source_rows.astype(jnp.float32) + jnp.dot(mixed, w_out, preferred_element_type=jnp.float32)
    return total.astype(jnp.bfloat16)

def attend(queries, keys, values, allowed):
    count, width = queries.shape
    depth = width // HEADS
    q_heads = queries.astype(jnp.float32).reshape(count, HEADS, depth)
    k_heads = keys.astype(jnp.float32).reshape(-1, HEADS, depth)
    v_heads = values.astype(jnp.float32).reshape(-1, HEADS, depth)
    scores = jnp.einsum('rhe,khe->hrk', q_heads, k_heads) * depth ** (-0.5)
    if allowed is not None:
        scores = jnp.where(allowed[None], scores, -1e+30)
    weights = jax.nn.softmax(scores, axis=-1)
    rounded = lax.optimization_barrier(weights.astype(jnp.bfloat16))
    mixed = jnp.einsum('hrk,khe->rhe', rounded.astype(jnp.float32), v_heads)
    return mixed.reshape(count, width).astype(jnp.bfloat16)

def device_block(source_rows, segment, gain, w_qkv, w_out):
    width = source_rows.shape[1]
    packed = prepare(source_rows, gain, w_qkv)
    allowed = segment[:, None] == segment[None, :]
    mixed = attend(packed[:, :width], packed[:, width:2 * width], packed[:, 2 * width:], allowed)
    return finish(source_rows, mixed, w_out)

def reference(points, norm_gain_one, qkv_one, out_one, hilbert_pos, norm_gain_two, qkv_two, out_two, hilbert_seg, out_grad):
    width = points.shape[-1]

    def patch_block(patch_rows):
        packed = prepare(patch_rows, norm_gain_one, qkv_one)
        mixed = attend(packed[:, :width], packed[:, width:2 * width], packed[:, 2 * width:], None)
        return finish(patch_rows, mixed, out_one)

    def second_block(pair):
        return device_block(pair[0], pair[1], norm_gain_two, qkv_two, out_two)

    def forward(source):
        patches = source.reshape(N_CURVE, PATCH, width)
        moved = lax.map(jax.checkpoint(patch_block), patches)
        grouped = moved.reshape(N_CURVE, N_PATCH, ROWS, width).transpose(1, 0, 2, 3).reshape(N_PATCH, N_CURVE * ROWS, width)
        order = hilbert_pos.transpose(1, 0, 2).reshape(N_PATCH, N_CURVE * ROWS)
        placed = jax.vmap(lambda src, where_to: jnp.zeros_like(src).at[where_to].set(src))(grouped, order)
        blocks = placed.reshape(N_PATCH * N_CURVE, ROWS, width)
        segments = hilbert_seg.reshape(N_PATCH * N_CURVE, ROWS)
        done = lax.map(jax.checkpoint(second_block), (blocks, segments))
        return done.reshape(N_PATCH, N_CURVE, ROWS, width)
    _, pull = jax.vjp(forward, points)
    return pull(out_grad)[0]
```

```python
import functools
import math

import jax
import jax.numpy as jnp
from jax import lax
from jax.experimental import pallas as pl
from jax.experimental.pallas import tpu as pltpu
from jax.sharding import PartitionSpec as P

HEADS = 16
EPS = 1e-06
LANES = 128
MASKED = -1e30
F32 = jnp.float32
BF16 = jnp.bfloat16
LOG2E = math.log2(math.e)


def dot_nn(left, right):
    return lax.dot_general(left, right, (((1,), (0,)), ((), ())), preferred_element_type=F32)


def dot_nt(left, right):
    return lax.dot_general(left, right, (((1,), (1,)), ((), ())), preferred_element_type=F32)


def dot_tn(left, right):
    return lax.dot_general(left, right, (((0,), (0,)), ((), ())), preferred_element_type=F32)


def norm_rows(rows, gain):
    wide = rows.astype(F32)
    power = jnp.mean(wide * wide, axis=-1, keepdims=True)
    return (wide * lax.rsqrt(power + EPS) * gain).astype(BF16)


def norm_pull(rows, gain, cotangent):
    wide = rows.astype(F32)
    power = jnp.mean(wide * wide, axis=-1, keepdims=True)
    inverse = lax.rsqrt(power + EPS)
    scaled = cotangent.astype(F32) * gain
    along = jnp.mean(scaled * wide, axis=-1, keepdims=True)
    return (inverse * scaled - wide * (inverse * inverse * inverse * along)).astype(BF16)


def head_mask(rows, index, depth):
    return lax.broadcasted_iota(jnp.int32, (rows, LANES), 1) // depth == index


def only(mask, tile):
    return jnp.where(mask, tile, jnp.zeros_like(tile))


def tile_at(t):
    return pl.ds(pl.multiple_of(t * LANES, LANES), LANES)


def vmem_call(body, outs, scratch=(), name=None, flops=0, moved=0, **more):
    params = pltpu.CompilerParams(vmem_limit_bytes=56 << 20, **more.pop("params", {}))
    return pl.pallas_call(
        body,
        out_shape=outs,
        scratch_shapes=scratch,
        compiler_params=params,
        name=name,
        cost_estimate=pl.CostEstimate(flops=flops, bytes_accessed=moved, transcendentals=0),
        **more,
    )


def prep_body(x_ref, gain_ref, w_ref, q_ref, k_ref, v_ref):
    width = x_ref.shape[1]
    normed = norm_rows(x_ref[...], gain_ref[...])
    q_ref[...] = dot_nn(normed, w_ref[:, :width]).astype(BF16)
    k_ref[...] = dot_nn(normed, w_ref[:, width : 2 * width]).astype(BF16)
    v_ref[...] = dot_nn(normed, w_ref[:, 2 * width :]).astype(BF16)


def forward_body(peers, chunks, depth, *refs):
    x_ref, q_ref, k_ref, v_ref, gain_ref, w_ref, out_w_ref, slot_ref = refs[:8]
    others = refs[8 : 8 + peers]
    keys_ref, values_ref, mixed_ref, lse_ref, lse_rows_ref = refs[8 + peers : 13 + peers]
    sends = refs[13 + peers : 13 + peers + chunks]
    count, width = x_ref.shape
    scale = depth ** (-0.5) * LOG2E
    keys_ref[:count] = k_ref[...]
    values_ref[:count] = v_ref[...]
    for index, other in enumerate(others):
        rows = slice((index + 1) * count, (index + 2) * count)
        normed = norm_rows(other[...], gain_ref[...])
        keys_ref[rows] = dot_nn(normed, w_ref[:, width : 2 * width]).astype(BF16)
        values_ref[rows] = dot_nn(normed, w_ref[:, 2 * width :]).astype(BF16)
    total = keys_ref.shape[0]

    def tile_step(t, carry):
        at = tile_at(t)
        q_tile = q_ref[:, at]
        k_tile = keys_ref[:, at]
        v_tile = values_ref[:, at]
        acc = jnp.zeros((count, 2 * LANES), F32)
        tops = jnp.zeros((count, LANES), F32)
        for j in range(LANES // depth):
            mask = head_mask(count, j, depth)
            scores = dot_nt(only(mask, q_tile), k_tile)
            top = jnp.max(scores, axis=-1, keepdims=True) * scale
            shifted = jnp.exp2(scores * scale - top).astype(BF16)
            wide_mask = head_mask(total, j, depth)
            ones = jnp.where(wide_mask, 1.0, 0.0).astype(BF16)
            acc += dot_nn(shifted, jnp.concatenate([only(wide_mask, v_tile), ones], axis=1))
            tops = jnp.where(mask, top, tops)
        sums = acc[:, LANES:]
        mixed_ref[:, at] = (acc[:, :LANES] / sums).astype(BF16)
        lse = tops + jnp.log(sums) * LOG2E
        lse_ref[:, at] = lse
        flipped = jnp.transpose(lse)
        for j in range(LANES // depth):
            lse_rows_ref[pl.ds(t * (LANES // depth) + j, 1)] = flipped[j * depth : j * depth + 1]
        return carry

    lax.fori_loop(0, width // LANES, tile_step, 0)
    moved = (x_ref[...].astype(F32) + dot_nn(mixed_ref[...], out_w_ref[...])).astype(BF16)
    slots = 2 * count
    picked = (lax.broadcasted_iota(jnp.int32, (slots, count), 0) == slot_ref[...]).astype(F32)
    outgoing = dot_nn(picked.astype(BF16), moved).astype(BF16)
    size = slots // chunks
    for index, send in enumerate(sends):
        send[...] = outgoing[index * size : (index + 1) * size]


def second_body(chunks, depth, *refs):
    land_row_ref, land_col_ref, seg_row_ref, seg_col_ref = refs[:4]
    gain_ref, w_ref, out_w_ref, grad_ref = refs[4:8]
    arrived = refs[8 : 8 + chunks]
    sends = refs[8 + chunks : 8 + 2 * chunks]
    staged, packed, packed_grad, mixed_grad, bias = refs[8 + 2 * chunks :]
    count, width = grad_ref.shape
    slots = staged.shape[0]
    size = slots // chunks
    for index, piece in enumerate(arrived):
        staged[index * size : (index + 1) * size] = piece[...]
    place = (lax.broadcasted_iota(jnp.int32, (count, slots), 0) == land_row_ref[...]).astype(F32)
    hilbert = dot_nn(place.astype(BF16), staged[...]).astype(BF16)
    normed = norm_rows(hilbert, gain_ref[...])
    packed[...] = dot_nn(normed, w_ref[...]).astype(BF16)
    mixed_grad[...] = dot_nt(grad_ref[...], out_w_ref[...]).astype(BF16)
    bias[...] = jnp.where(seg_col_ref[...] == seg_row_ref[...], 0.0, MASKED)
    scale = depth ** (-0.5)

    def tile_step(t, carry):
        at = tile_at(t)
        k_at = tile_at(t + width // LANES)
        v_at = tile_at(t + 2 * (width // LANES))
        q_tile = packed[:, at]
        k_tile = packed[:, k_at]
        v_tile = packed[:, v_at]
        g_tile = mixed_grad[:, at]
        dq = jnp.zeros((count, LANES), F32)
        dk = jnp.zeros((count, LANES), F32)
        dv = jnp.zeros((count, LANES), F32)
        for j in range(LANES // depth):
            mask = head_mask(count, j, depth)
            q_one = only(mask, q_tile)
            g_one = only(mask, g_tile)
            scores = dot_nt(q_one, k_tile) * (scale * LOG2E) + bias[...]
            top = jnp.max(scores, axis=-1, keepdims=True)
            shifted = jnp.exp2(scores - top)
            sums = jnp.sum(shifted, axis=-1, keepdims=True)
            weights = shifted * (1.0 / sums)
            weight_grad = dot_nt(g_one, v_tile)
            carried = jnp.sum(weights * weight_grad, axis=-1, keepdims=True)
            score_grad = (weights * (weight_grad - carried)).astype(BF16)
            dq += dot_nn(score_grad, only(mask, k_tile))
            dk += dot_tn(score_grad, q_one)
            dv += dot_tn(weights.astype(BF16), g_one)
        packed_grad[:, at] = (dq * scale).astype(BF16)
        packed_grad[:, k_at] = (dk * scale).astype(BF16)
        packed_grad[:, v_at] = dv.astype(BF16)
        return carry

    lax.fori_loop(0, width // LANES, tile_step, 0)
    normed_grad = dot_nt(packed_grad[...], w_ref[...]).astype(BF16)
    total = grad_ref[...].astype(F32) + norm_pull(hilbert, gain_ref[...], normed_grad).astype(F32)
    back = (lax.broadcasted_iota(jnp.int32, (slots, count), 1) == land_col_ref[...]).astype(F32)
    returning = dot_nn(back.astype(BF16), total.astype(BF16)).astype(BF16)
    for index, send in enumerate(sends):
        send[...] = returning[index * size : (index + 1) * size]


def queries_body(peers, *refs):
    gain_ref, w_ref, q_ref = refs[:3]
    out_ref = refs[3 + peers]
    count, width = q_ref.shape
    out_ref[:count] = q_ref[...]
    for index, other in enumerate(refs[3 : 3 + peers]):
        rows = slice((index + 1) * count, (index + 2) * count)
        normed = norm_rows(other[...], gain_ref[...])
        out_ref[rows] = dot_nn(normed, w_ref[:, :width]).astype(BF16)


def weights_body(depth, q_ref, keys_ref, lse_ref, out_ref):
    scale = depth ** (-0.5) * LOG2E
    for j in range(LANES // depth):
        mask = head_mask(q_ref.shape[0], j, depth)
        scores = dot_nt(only(mask, q_ref[...]), keys_ref[...])
        out_ref[j] = jnp.exp2(scores * scale - lse_ref[:, j * depth : j * depth + 1]).astype(BF16)


def weights_flipped_body(depth, k_ref, queries_ref, lse_ref, out_ref):
    scale = depth ** (-0.5) * LOG2E
    for j in range(LANES // depth):
        mask = head_mask(k_ref.shape[0], j, depth)
        scores = dot_nt(only(mask, k_ref[...]), queries_ref[...])
        out_ref[j] = jnp.exp2(scores * scale - lse_ref[0, j : j + 1]).astype(BF16)


def home_body(chunks, depth, *refs):
    slot_ref, mixed_ref, out_w_ref = refs[:3]
    home = refs[3 : 3 + chunks]
    moved_ref, grad_ref, delta_ref = refs[3 + chunks : 6 + chunks]
    staged = refs[6 + chunks]
    count, width = moved_ref.shape
    slots = staged.shape[0]
    size = slots // chunks
    for index, piece in enumerate(home):
        staged[index * size : (index + 1) * size] = piece[...]
    take = (lax.broadcasted_iota(jnp.int32, (count, slots), 1) == slot_ref[...]).astype(F32)
    moved = dot_nn(take.astype(BF16), staged[...]).astype(BF16)
    moved_ref[...] = moved
    grad = dot_nt(moved, out_w_ref[...]).astype(BF16)
    product = grad.astype(F32) * mixed_ref[...].astype(F32)
    high = product.astype(BF16)
    low = (product - high.astype(F32)).astype(BF16)
    same = lax.broadcasted_iota(jnp.int32, (width, width), 0) // depth == (
        lax.broadcasted_iota(jnp.int32, (width, width), 1) // depth
    )
    same = same.astype(F32).astype(BF16)
    delta_ref[...] = dot_nn(high, same) + dot_nn(low, same)
    heads = width // depth
    pick = lax.broadcasted_iota(jnp.int32, (heads, width), 1) // depth == (
        lax.broadcasted_iota(jnp.int32, (heads, width), 0)
    )
    pick = pick.astype(F32).astype(BF16)
    rows = dot_nt(pick, high) + dot_nt(pick, low)
    rows_high = rows.astype(BF16)
    rows_low = (rows - rows_high.astype(F32)).astype(BF16)
    grad_ref[:count] = grad
    grad_ref[count:, :count] = rows_high
    grad_ref[count:, count:] = rows_low


def query_grad_body(depth, weights_ref, grad_ref, delta_ref, keys_ref, values_ref, out_ref):
    count = grad_ref.shape[0]
    total = keys_ref.shape[0]
    acc = jnp.zeros((count, LANES), F32)
    for j in range(LANES // depth):
        weight_grad = dot_nt(only(head_mask(count, j, depth), grad_ref[...]), values_ref[...])
        delta = delta_ref[:, j * depth : j * depth + 1]
        score_grad = (weights_ref[j].astype(F32) * (weight_grad - delta)).astype(BF16)
        acc += dot_nn(score_grad, only(head_mask(total, j, depth), keys_ref[...]))
    out_ref[...] = (acc * depth ** (-0.5)).astype(BF16)


def key_grad_body(peers, depth, *refs):
    weights_ref, k_ref, v_ref, queries_ref, dq_ref, x_ref, gain_ref, w_ref, moved_ref = refs[:9]
    grads = refs[9 : 10 + peers]
    out_ref = refs[10 + peers]
    packed_grad = refs[11 + peers]
    t = pl.program_id(0)
    count, width = x_ref.shape
    heads = LANES // depth
    at = tile_at(t)
    k_tile = k_ref[:, at]
    v_tile = v_ref[:, at]
    dk = jnp.zeros((count, LANES), F32)
    dv = jnp.zeros((count, LANES), F32)
    for b in range(peers + 1):
        rows = slice(b * count, (b + 1) * count)
        g_tile = grads[b][:count, at]
        q_tile = queries_ref[rows, at]
        lines = grads[b][count:].astype(F32)
        lines = lines[:, :count] + lines[:, count:]
        for j in range(heads):
            mask = head_mask(count, j, depth)
            weights = weights_ref[j, :, rows]
            weight_grad = dot_nt(only(mask, v_tile), g_tile)
            index = lax.broadcasted_iota(jnp.int32, (HEADS, count), 0) == t * heads + j
            delta = jnp.sum(jnp.where(index, lines, 0.0), axis=0, keepdims=True)
            score_grad = (weights.astype(F32) * (weight_grad - delta)).astype(BF16)
            dv += dot_nn(weights, only(mask, g_tile))
            dk += dot_nn(score_grad, only(mask, q_tile))
    packed_grad[:, at] = dq_ref[:, at]
    packed_grad[:, tile_at(t + width // LANES)] = (dk * depth ** (-0.5)).astype(BF16)
    packed_grad[:, tile_at(t + 2 * (width // LANES))] = dv.astype(BF16)

    @pl.when(t == pl.num_programs(0) - 1)
    def _():
        normed_grad = dot_nt(packed_grad[...], w_ref[...]).astype(BF16)
        path = norm_pull(x_ref[...], gain_ref[...], normed_grad)
        out_ref[...] = (moved_ref[...].astype(F32) + path.astype(F32)).astype(BF16)


def full(shape):
    zeros = (0,) * len(shape)
    return pl.BlockSpec(shape, lambda t: zeros)


def by_xor(array, axis, step):
    size = lax.axis_size(axis)
    return lax.ppermute(array, axis, [(i, i ^ step) for i in range(size)])


def exchange(pieces, axis):
    if len(pieces) == 1:
        size = lax.axis_size(axis)
        stacked = pieces[0].reshape((size, -1) + pieces[0].shape[1:])
        got = lax.all_to_all(stacked, axis, split_axis=0, concat_axis=0, tiled=True)
        return [got.reshape(pieces[0].shape)]
    return [pieces[0]] + [by_xor(pieces[m], axis, m) for m in range(1, len(pieces))]


def shards(
    points, gain_one, qkv_one, out_one, hilbert_pos, gain_two, qkv_two, out_two, segments, out_grad
):
    count, width = points.shape[2:]
    depth = width // HEADS
    tiles = width // LANES
    per_tile = LANES // depth
    patch_size = lax.axis_size("patch")
    curve_size = lax.axis_size("curve")
    peers = patch_size - 1
    total = patch_size * count
    slots = 2 * count
    capacity = slots // curve_size
    chunks = curve_size if curve_size <= 16 else 1
    rows_bf16 = jax.ShapeDtypeStruct((count, width), BF16)
    all_bf16 = jax.ShapeDtypeStruct((total, width), BF16)
    chunk_bf16 = jax.ShapeDtypeStruct((slots // chunks, width), BF16)

    x = points.reshape(count, width)
    others = [by_xor(x, "patch", m) for m in range(1, patch_size)]
    gain_one = gain_one.reshape(1, width)
    gain_two = gain_two.reshape(1, width)

    target = hilbert_pos.reshape(count)
    owner = target // count
    offset = target % count
    lane = owner if chunks == 1 else owner ^ lax.axis_index("curve")
    i_row = lax.broadcasted_iota(jnp.int32, (count, count), 0)
    i_col = lax.broadcasted_iota(jnp.int32, (count, count), 1)
    ranking = jnp.sum(
        jnp.where((owner[:, None] == owner[None, :]) & (i_col < i_row), 1, 0), axis=1
    ).astype(jnp.int32)
    slot = lane * capacity + ranking
    hit = slot[None, :] == lax.broadcasted_iota(jnp.int32, (slots, count), 0)
    outgoing_at = jnp.min(jnp.where(hit, offset[None, :], count), axis=1).astype(jnp.int32)
    at_pieces = [outgoing_at[m * (slots // chunks) : (m + 1) * (slots // chunks)] for m in range(chunks)]
    landing = jnp.concatenate(exchange(at_pieces, "curve"))

    q, k, v = vmem_call(prep_body, (rows_bf16,) * 3, name="prep", flops=2 * count * width * 3 * width, moved=4 << 20)(
        x, gain_one, qkv_one
    )
    results = vmem_call(
        functools.partial(forward_body, peers, chunks, depth),
        (
            all_bf16,
            all_bf16,
            rows_bf16,
            jax.ShapeDtypeStruct((count, width), F32),
            jax.ShapeDtypeStruct((HEADS, count), F32),
        )
        + (chunk_bf16,) * chunks,
        name="forward",
        flops=8 << 30,
        moved=8 << 20,
    )(x, q, k, v, gain_one, qkv_one, out_one, slot.reshape(1, count), *others)
    keys_all, values_all, mixed, lse, lse_rows = results[:5]
    arrived = exchange(results[5:], "curve")
    lse_rows = lse_rows.reshape(tiles, per_tile, count)
    lse_all = jnp.concatenate(
        [lse_rows] + [by_xor(lse_rows, "patch", m) for m in range(1, patch_size)], axis=2
    )

    queries_all = vmem_call(
        functools.partial(queries_body, peers), all_bf16, name="queries", flops=1 << 29, moved=3 << 20
    )(gain_one, qkv_one, q, *others)
    stack = jax.ShapeDtypeStruct((HEADS, count, total), BF16)
    stack_spec = pl.BlockSpec((per_tile, count, total), lambda t: (t, 0, 0))
    own_spec = pl.BlockSpec((count, LANES), lambda t: (0, t))
    all_spec = pl.BlockSpec((total, LANES), lambda t: (0, t))
    weights = vmem_call(
        functools.partial(weights_body, depth),
        stack,
        name="weights",
        flops=4 << 30,
        moved=10 << 20,
        grid=(tiles,),
        in_specs=[own_spec, all_spec, own_spec],
        out_specs=stack_spec,
    )(q, keys_all, lse)
    weights_flipped = vmem_call(
        functools.partial(weights_flipped_body, depth),
        stack,
        name="weights_flipped",
        flops=4 << 30,
        moved=10 << 20,
        grid=(tiles,),
        in_specs=[own_spec, all_spec, pl.BlockSpec((1, per_tile, total), lambda t: (t, 0, 0))],
        out_specs=stack_spec,
    )(k, queries_all, lse_all)

    segment = segments.reshape(count)
    returning = vmem_call(
        functools.partial(second_body, chunks, depth),
        (chunk_bf16,) * chunks,
        [
            pltpu.VMEM((slots, width), BF16),
            pltpu.VMEM((count, 3 * width), BF16),
            pltpu.VMEM((count, 3 * width), BF16),
            pltpu.VMEM((count, width), BF16),
            pltpu.VMEM((count, count), F32),
        ],
        name="second",
        flops=8 << 30,
        moved=4 << 20,
    )(
        landing.reshape(1, slots),
        landing.reshape(slots, 1),
        segment.reshape(1, count),
        segment.reshape(count, 1),
        gain_two,
        qkv_two,
        out_two,
        out_grad.reshape(count, width),
        *arrived,
    )
    home = exchange(returning, "curve")

    moved_grad, grad_own, delta = vmem_call(
        functools.partial(home_body, chunks, depth),
        (
            rows_bf16,
            jax.ShapeDtypeStruct((count + HEADS, width), BF16),
            jax.ShapeDtypeStruct((count, width), F32),
        ),
        [pltpu.VMEM((slots, width), BF16)],
        name="home",
        flops=1 << 29,
        moved=2 << 20,
    )(slot.reshape(count, 1), mixed, out_one, *home)
    grads = [grad_own] + [by_xor(grad_own, "patch", m) for m in range(1, patch_size)]

    query_grad = vmem_call(
        functools.partial(query_grad_body, depth),
        rows_bf16,
        name="query_grad",
        flops=8 << 30,
        moved=10 << 20,
        grid=(tiles,),
        in_specs=[stack_spec, own_spec, own_spec, all_spec, all_spec],
        out_specs=own_spec,
    )(weights, grad_own, delta, keys_all, values_all)
    result = vmem_call(
        functools.partial(key_grad_body, peers, depth),
        rows_bf16,
        [pltpu.VMEM((count, 3 * width), BF16)],
        name="key_grad",
        flops=8 << 30,
        moved=14 << 20,
        grid=(tiles,),
        in_specs=[
            stack_spec,
            full((count, width)),
            full((count, width)),
            full((total, width)),
            full((count, width)),
            full((count, width)),
            full((1, width)),
            full(qkv_one.shape),
            full((count, width)),
        ]
        + [full((count + HEADS, width))] * patch_size,
        out_specs=full((count, width)),
    )(weights_flipped, k, v, queries_all, query_grad, x, gain_one, qkv_one, moved_grad, *grads)
    return result.reshape(points.shape)


def solution(mesh):
    in_specs = (
        P("curve", "patch", None, None),
        P(),
        P(),
        P(),
        P("curve", "patch", None),
        P(),
        P(),
        P(),
        P("patch", "curve", None),
        P("patch", "curve", None, None),
    )
    out_specs = P("curve", "patch", None, None)
    return jax.shard_map(shards, mesh=mesh, in_specs=in_specs, out_specs=out_specs, check_vma=False)
```

```python
import functools
import math

import jax
import jax.numpy as jnp
from jax import lax
from jax.experimental import pallas as pl
from jax.experimental.pallas import tpu as pltpu
from jax.sharding import PartitionSpec as P

HEADS = 16
EPS = 1e-06
LANES = 128
MASKED = -1e30
F32 = jnp.float32
BF16 = jnp.bfloat16
LOG2E = math.log2(math.e)


def dot_nn(left, right):
    return lax.dot_general(left, right, (((1,), (0,)), ((), ())), preferred_element_type=F32)


def dot_nt(left, right):
    return lax.dot_general(left, right, (((1,), (1,)), ((), ())), preferred_element_type=F32)


def dot_tn(left, right):
    return lax.dot_general(left, right, (((0,), (0,)), ((), ())), preferred_element_type=F32)


def norm_rows(rows, gain):
    wide = rows.astype(F32)
    power = jnp.mean(wide * wide, axis=-1, keepdims=True)
    return (wide * lax.rsqrt(power + EPS) * gain).astype(BF16)


def norm_pull(rows, gain, cotangent):
    wide = rows.astype(F32)
    power = jnp.mean(wide * wide, axis=-1, keepdims=True)
    inverse = lax.rsqrt(power + EPS)
    scaled = cotangent.astype(F32) * gain
    along = jnp.mean(scaled * wide, axis=-1, keepdims=True)
    return (inverse * scaled - wide * (inverse * inverse * inverse * along)).astype(BF16)


def head_mask(rows, index, depth):
    return lax.broadcasted_iota(jnp.int32, (rows, LANES), 1) // depth == index


def only(mask, tile):
    return jnp.where(mask, tile, jnp.zeros_like(tile))


def tile_at(t):
    return pl.ds(pl.multiple_of(t * LANES, LANES), LANES)


def vmem_call(body, outs, scratch=(), name=None, flops=0, moved=0, **more):
    params = pltpu.CompilerParams(vmem_limit_bytes=24 << 20, **more.pop("params", {}))
    return pl.pallas_call(
        body,
        out_shape=outs,
        scratch_shapes=scratch,
        compiler_params=params,
        name=name,
        cost_estimate=pl.CostEstimate(flops=flops, bytes_accessed=moved, transcendentals=0),
        **more,
    )


HBM_SPEC = pl.BlockSpec(memory_space=pltpu.MemorySpace.HBM)
VMEM_SPEC = pl.BlockSpec(memory_space=pltpu.MemorySpace.VMEM)
LOW, HIGH = 2.0**-60, 2.0**100


def column(row):
    return jnp.transpose(jnp.broadcast_to(row.astype(F32), (LANES, row.shape[1])))[:, :1]


def start_all(pairs, sems):
    copies = [pltpu.make_async_copy(src, dst, sems.at[i]) for i, (src, dst) in enumerate(pairs)]
    for copy in copies:
        copy.start()
    return copies


def with_ones(tile):
    return jnp.concatenate([tile, jnp.ones_like(tile)], axis=1)


def unshifted(depth, q_tile, k_tile, v_tile):
    count = q_tile.shape[0]
    scale = depth ** (-0.5) * LOG2E
    right = with_ones(v_tile)
    mixed = jnp.zeros((count, LANES), F32)
    sums = jnp.zeros((count, LANES), F32)
    for j in range(LANES // depth):
        mask = head_mask(count, j, depth)
        scores = dot_nt(only(mask, q_tile), k_tile)
        both = dot_nn(jnp.exp2(scores * scale).astype(BF16), right)
        mixed = jnp.where(mask, both[:, :LANES], mixed)
        sums = jnp.where(mask, both[:, LANES:], sums)
    return mixed, sums


def prep_body(depth, x_ref, gain_ref, w_ref, q_ref, k_ref, v_ref, mixed_ref, sums_ref):
    width = x_ref.shape[1]
    normed = norm_rows(x_ref[...], gain_ref[...])
    q_ref[...] = dot_nn(normed, w_ref[:, :width]).astype(BF16)
    k_ref[...] = dot_nn(normed, w_ref[:, width : 2 * width]).astype(BF16)
    v_ref[...] = dot_nn(normed, w_ref[:, 2 * width :]).astype(BF16)

    def tile_step(t, carry):
        at = tile_at(t)
        mixed_ref[:, at], sums_ref[:, at] = unshifted(depth, q_ref[:, at], k_ref[:, at], v_ref[:, at])
        return carry

    lax.fori_loop(0, width // LANES, tile_step, 0)


def forward_body(peers, chunks, depth, *refs):
    x_ref, q_ref, k_ref, v_ref, own_mixed_ref, own_sums_ref = refs[:6]
    gain_ref, w_ref, out_w_ref, slot_ref = refs[6:10]
    others = refs[10 : 10 + peers]
    keys_ref, values_ref, mixed_ref, lse_ref, lse_rows_ref = refs[10 + peers : 15 + peers]
    sends = refs[15 + peers : 15 + peers + chunks]
    landed, outgoing, in_sems, out_sems = refs[15 + peers + chunks :]
    count, width = x_ref.shape
    heads = LANES // depth
    arrivals = start_all([(other, landed.at[i]) for i, other in enumerate(others)], in_sems)
    keys_ref[:count] = k_ref[...]
    values_ref[:count] = v_ref[...]
    for index, copy in enumerate(arrivals):
        copy.wait()
        rows = slice((index + 1) * count, (index + 2) * count)
        normed = norm_rows(landed[index], gain_ref[...])
        keys_ref[rows] = dot_nn(normed, w_ref[:, width : 2 * width]).astype(BF16)
        values_ref[rows] = dot_nn(normed, w_ref[:, 2 * width :]).astype(BF16)
    total = keys_ref.shape[0]

    def finish_tile(t, at, mixed, sums, lse):
        mixed_ref[:, at] = (mixed / sums).astype(BF16)
        lse_ref[:, at] = lse
        flipped = jnp.transpose(lse)
        for j in range(heads):
            lse_rows_ref[pl.ds(t * heads + j, 1)] = flipped[j * depth : j * depth + 1]

    def fast_step(t, bad):
        at = tile_at(t)
        mixed, sums = unshifted(depth, q_ref[:, at], keys_ref[count:, at], values_ref[count:, at])
        mixed += own_mixed_ref[:, at]
        sums += own_sums_ref[:, at]
        finish_tile(t, at, mixed, sums, jnp.log(sums) * LOG2E)
        return jnp.where((sums >= LOW) & (sums <= HIGH), bad, 1.0)

    bad = lax.fori_loop(0, width // LANES, fast_step, jnp.zeros((count, LANES), F32))

    @pl.when(jnp.max(bad) > 0.0)
    def _():
        scale = depth ** (-0.5) * LOG2E

        def safe_step(t, carry):
            at = tile_at(t)
            right = with_ones(values_ref[:, at])
            mixed = jnp.zeros((count, LANES), F32)
            sums = jnp.ones((count, LANES), F32)
            tops = jnp.zeros((count, LANES), F32)
            for j in range(heads):
                mask = head_mask(count, j, depth)
                scores = dot_nt(only(mask, q_ref[:, at]), keys_ref[:, at])
                top = jnp.max(scores, axis=-1, keepdims=True) * scale
                both = dot_nn(jnp.exp2(scores * scale - top).astype(BF16), right)
                mixed = jnp.where(mask, both[:, :LANES], mixed)
                sums = jnp.where(mask, both[:, LANES:], sums)
                tops = jnp.where(mask, top, tops)
            finish_tile(t, at, mixed, sums, tops + jnp.log(sums) * LOG2E)
            return carry

        lax.fori_loop(0, width // LANES, safe_step, 0)

    moved = (x_ref[...].astype(F32) + dot_nn(mixed_ref[...], out_w_ref[...])).astype(BF16)
    slots = 2 * count
    picked = (lax.broadcasted_iota(jnp.int32, (slots, count), 0) == slot_ref[...]).astype(F32)
    outgoing[...] = dot_nn(picked.astype(BF16), moved).astype(BF16)
    size = slots // chunks
    pairs = [(outgoing.at[i * size : (i + 1) * size], send) for i, send in enumerate(sends)]
    for copy in start_all(pairs, out_sems):
        copy.wait()


def second_body(chunks, depth, *refs):
    land_ref, seg_ref, gain_ref, w_ref, out_w_ref, grad_ref = refs[:6]
    arrived = refs[6 : 6 + chunks]
    sends = refs[6 + chunks : 6 + 2 * chunks]
    staged, packed, packed_grad, mixed_grad, bias, in_sems, out_sems = refs[6 + 2 * chunks :]
    count, width = grad_ref.shape
    slots = staged.shape[0]
    size = slots // chunks
    parts = [slice(i * size, (i + 1) * size) for i in range(chunks)]
    copies = start_all([(piece, staged.at[parts[i]]) for i, piece in enumerate(arrived)], in_sems)
    mixed_grad[...] = dot_nt(grad_ref[...], out_w_ref[...]).astype(BF16)
    bias[...] = jnp.where(column(seg_ref[...]) == seg_ref[...].astype(F32), 0.0, MASKED)
    place = (lax.broadcasted_iota(jnp.int32, (count, slots), 0) == land_ref[...]).astype(F32)
    for copy in copies:
        copy.wait()
    hilbert = dot_nn(place.astype(BF16), staged[...]).astype(BF16)
    normed = norm_rows(hilbert, gain_ref[...])
    packed[...] = dot_nn(normed, w_ref[...]).astype(BF16)
    scale = depth ** (-0.5)

    def tile_step(t, carry):
        at = tile_at(t)
        k_at = tile_at(t + width // LANES)
        v_at = tile_at(t + 2 * (width // LANES))
        q_tile = packed[:, at]
        k_tile = packed[:, k_at]
        v_tile = packed[:, v_at]
        g_tile = mixed_grad[:, at]
        k_flipped = jnp.transpose(k_tile)
        dk = jnp.zeros((count, LANES), F32)
        dv = jnp.zeros((count, LANES), F32)
        dq = []
        for j in range(LANES // depth):
            mask = head_mask(count, j, depth)
            scores = dot_nt(only(mask, k_tile), q_tile) * (scale * LOG2E) + bias[...]
            shifted = jnp.exp2(scores - jnp.max(scores, axis=0, keepdims=True))
            weights = shifted * (1.0 / jnp.sum(shifted, axis=0, keepdims=True))
            weight_grad = dot_nt(only(mask, v_tile), g_tile)
            carried = jnp.sum(weights * weight_grad, axis=0, keepdims=True)
            score_grad = (weights * (weight_grad - carried)).astype(BF16)
            dk = jnp.where(mask, dot_nn(score_grad, q_tile), dk)
            dv = jnp.where(mask, dot_nn(weights.astype(BF16), g_tile), dv)
            dq.append(dot_nn(k_flipped[j * depth : (j + 1) * depth], score_grad))
        dq = jnp.transpose(jnp.concatenate(dq, axis=0))
        packed_grad[:, at] = (dq * scale).astype(BF16)
        packed_grad[:, k_at] = (dk * scale).astype(BF16)
        packed_grad[:, v_at] = dv.astype(BF16)
        return carry

    lax.fori_loop(0, width // LANES, tile_step, 0)
    normed_grad = dot_nt(packed_grad[...], w_ref[...]).astype(BF16)
    total = grad_ref[...].astype(F32) + norm_pull(hilbert, gain_ref[...], normed_grad).astype(F32)
    back = lax.broadcasted_iota(jnp.int32, (slots, count), 1).astype(F32) == column(land_ref[...])
    staged[...] = dot_nn(back.astype(F32).astype(BF16), total.astype(BF16)).astype(BF16)
    pairs = [(staged.at[parts[i]], send) for i, send in enumerate(sends)]
    for copy in start_all(pairs, out_sems):
        copy.wait()


def queries_body(peers, *refs):
    gain_ref, w_ref, q_ref = refs[:3]
    others = refs[3 : 3 + peers]
    out_ref, landed, sems = refs[3 + peers :]
    count, width = q_ref.shape
    copies = start_all([(other, landed.at[i]) for i, other in enumerate(others)], sems)
    out_ref[:count] = q_ref[...]
    for index, copy in enumerate(copies):
        copy.wait()
        rows = slice((index + 1) * count, (index + 2) * count)
        normed = norm_rows(landed[index], gain_ref[...])
        out_ref[rows] = dot_nn(normed, w_ref[:, :width]).astype(BF16)


def weights_body(depth, q_ref, keys_ref, lse_ref, out_ref):
    scale = depth ** (-0.5) * LOG2E
    heads = LANES // depth

    def tile_step(t, carry):
        at = tile_at(t)
        lse = lse_ref[:, at]
        for j in range(heads):
            mask = head_mask(q_ref.shape[0], j, depth)
            scores = dot_nt(only(mask, q_ref[:, at]), keys_ref[:, at])
            line = lse[:, j * depth : j * depth + 1]
            out_ref[t * heads + j] = jnp.exp2(scores * scale - line).astype(BF16)
        return carry

    lax.fori_loop(0, q_ref.shape[1] // LANES, tile_step, 0)


def weights_flipped_body(peers, depth, *refs):
    k_ref, queries_ref = refs[:2]
    lse_refs = refs[2 : 3 + peers]
    out_ref = refs[3 + peers]
    scale = depth ** (-0.5) * LOG2E
    heads = LANES // depth
    count = k_ref.shape[0]

    def tile_step(t, carry):
        at = tile_at(t)
        for j in range(heads):
            mask = head_mask(count, j, depth)
            scores = dot_nt(only(mask, k_ref[:, at]), queries_ref[:, at])
            h = t * heads + j
            line = jnp.concatenate([ref[pl.ds(h, 1)] for ref in lse_refs], axis=1)
            out_ref[h] = jnp.exp2(scores * scale - line).astype(BF16)
        return carry

    lax.fori_loop(0, k_ref.shape[1] // LANES, tile_step, 0)


def home_body(chunks, depth, *refs):
    slot_ref, mixed_ref, out_w_ref = refs[:3]
    home = refs[3 : 3 + chunks]
    moved_ref, grad_ref, delta_ref, send_ref = refs[3 + chunks : 7 + chunks]
    staged, sems, send_sem = refs[7 + chunks :]
    count, width = moved_ref.shape
    slots = staged.shape[0]
    size = slots // chunks
    pairs = [(piece, staged.at[i * size : (i + 1) * size]) for i, piece in enumerate(home)]
    copies = start_all(pairs, sems)
    take = lax.broadcasted_iota(jnp.int32, (count, slots), 1).astype(F32) == column(slot_ref[...])
    take = take.astype(F32).astype(BF16)
    for copy in copies:
        copy.wait()
    moved = dot_nn(take, staged[...]).astype(BF16)
    moved_ref[...] = moved
    grad = dot_nt(moved, out_w_ref[...]).astype(BF16)
    grad_ref[:count] = grad
    product = grad.astype(F32) * mixed_ref[...].astype(F32)
    high = product.astype(BF16)
    low = (product - high.astype(F32)).astype(BF16)
    heads = width // depth
    pick = lax.broadcasted_iota(jnp.int32, (heads, width), 1) // depth == (
        lax.broadcasted_iota(jnp.int32, (heads, width), 0)
    )
    pick = pick.astype(F32).astype(BF16)
    rows = dot_nt(pick, high) + dot_nt(pick, low)
    rows_high = rows.astype(BF16)
    grad_ref[count:, :count] = rows_high
    grad_ref[count:, count:] = (rows - rows_high.astype(F32)).astype(BF16)
    send = pltpu.make_async_copy(grad_ref, send_ref, send_sem)
    send.start()
    same = lax.broadcasted_iota(jnp.int32, (width, width), 0) // depth == (
        lax.broadcasted_iota(jnp.int32, (width, width), 1) // depth
    )
    same = same.astype(F32).astype(BF16)
    delta_ref[...] = dot_nn(high, same) + dot_nn(low, same)
    send.wait()


def key_tile(depth, t, at, v_ref, weights_ref, columns, queries, grads, deltas_ref):
    count = v_ref.shape[0]
    heads = LANES // depth
    v_tile = v_ref[:, at]
    dk = jnp.zeros((count, LANES), F32)
    dv = jnp.zeros((count, LANES), F32)
    for j in range(heads):
        h = t * heads + j
        mask = head_mask(count, j, depth)
        weights = weights_ref[h, :, columns]
        weight_grad = dot_nt(only(mask, v_tile), grads)
        delta = deltas_ref[pl.ds(h, 1)]
        score_grad = (weights.astype(F32) * (weight_grad - delta)).astype(BF16)
        dv = jnp.where(mask, dot_nn(weights, grads), dv)
        dk = jnp.where(mask, dot_nn(score_grad, queries), dk)
    return dk, dv


def unsplit(lines):
    half = lines.shape[1] // 2
    return lines[:, :half].astype(F32) + lines[:, half:].astype(F32)


def query_grad_body(depth, *refs):
    weights_ref, flipped_ref, grad_ref, delta_ref, keys_ref, values_ref, q_ref = refs[:7]
    out_ref, dk_ref, dv_ref, deltas = refs[7:]
    count, width = q_ref.shape
    heads = LANES // depth
    deltas[...] = unsplit(grad_ref[count:])

    def tile_step(t, carry):
        at = tile_at(t)
        g_tile = grad_ref[:count, at]
        delta_tile = delta_ref[:, at]
        dq = jnp.zeros((count, LANES), F32)
        for j in range(heads):
            mask = head_mask(count, j, depth)
            weight_grad = dot_nt(only(mask, g_tile), values_ref[:, at])
            delta = delta_tile[:, j * depth : j * depth + 1]
            weights = weights_ref[t * heads + j].astype(F32)
            score_grad = (weights * (weight_grad - delta)).astype(BF16)
            dq = jnp.where(mask, dot_nn(score_grad, keys_ref[:, at]), dq)
        out_ref[:, at] = (dq * depth ** (-0.5)).astype(BF16)
        own = slice(0, count)
        dk_ref[:, at], dv_ref[:, at] = key_tile(
            depth, t, at, values_ref.at[own], flipped_ref, own, q_ref[:, at], g_tile, deltas
        )
        return carry

    lax.fori_loop(0, width // LANES, tile_step, 0)


def key_grad_body(peers, depth, *refs):
    flipped_ref, v_ref, queries_ref, dq_ref, dk_ref, dv_ref = refs[:6]
    x_ref, gain_ref, w_ref, moved_ref = refs[6:10]
    others = refs[10 : 10 + peers]
    out_ref, packed_grad, landed, lines, deltas, sems = refs[10 + peers :]
    count, width = x_ref.shape
    pairs = []
    for i, other in enumerate(others):
        pairs.append((other.at[:count], landed.at[i * count : (i + 1) * count]))
        pairs.append((other.at[count:], lines.at[i]))
    copies = start_all(pairs, sems)
    packed_grad[:, :width] = dq_ref[...]
    for copy in copies:
        copy.wait()
    for i in range(peers):
        deltas[:, i * count : (i + 1) * count] = unsplit(lines[i])

    def tile_step(t, carry):
        at = tile_at(t)
        dk, dv = key_tile(
            depth,
            t,
            at,
            v_ref,
            flipped_ref,
            slice(count, (peers + 1) * count),
            queries_ref[count:, at],
            landed[:, at],
            deltas,
        )
        dk = (dk + dk_ref[:, at]) * depth ** (-0.5)
        packed_grad[:, tile_at(t + width // LANES)] = dk.astype(BF16)
        packed_grad[:, tile_at(t + 2 * (width // LANES))] = (dv + dv_ref[:, at]).astype(BF16)
        return carry

    lax.fori_loop(0, width // LANES, tile_step, 0)
    normed_grad = dot_nt(packed_grad[...], w_ref[...]).astype(BF16)
    path = norm_pull(x_ref[...], gain_ref[...], normed_grad)
    out_ref[...] = (moved_ref[...].astype(F32) + path.astype(F32)).astype(BF16)


def by_xor(array, axis, step):
    size = lax.axis_size(axis)
    return lax.ppermute(array, axis, [(i, i ^ step) for i in range(size)])


def exchange(pieces, axis):
    if len(pieces) == 1:
        size = lax.axis_size(axis)
        stacked = pieces[0].reshape((size, -1) + pieces[0].shape[1:])
        got = lax.all_to_all(stacked, axis, split_axis=0, concat_axis=0, tiled=True)
        return [got.reshape(pieces[0].shape)]
    return [pieces[0]] + [by_xor(pieces[m], axis, m) for m in range(1, len(pieces))]


def shards(
    points, gain_one, qkv_one, out_one, hilbert_pos, gain_two, qkv_two, out_two, segments, out_grad
):
    count, width = points.shape[2:]
    depth = width // HEADS
    tiles = width // LANES
    per_tile = LANES // depth
    patch_size = lax.axis_size("patch")
    curve_size = lax.axis_size("curve")
    peers = patch_size - 1
    total = patch_size * count
    slots = 2 * count
    capacity = slots // curve_size
    chunks = curve_size if curve_size <= 16 else 1
    rows_bf16 = jax.ShapeDtypeStruct((count, width), BF16)
    all_bf16 = jax.ShapeDtypeStruct((total, width), BF16)
    chunk_bf16 = jax.ShapeDtypeStruct((slots // chunks, width), BF16)

    x = points.reshape(count, width)
    others = [by_xor(x, "patch", m) for m in range(1, patch_size)]
    gain_one = gain_one.reshape(1, width)
    gain_two = gain_two.reshape(1, width)

    target = hilbert_pos.reshape(count)
    owner = target // count
    offset = target % count
    lane = owner if chunks == 1 else owner ^ lax.axis_index("curve")
    i_row = lax.broadcasted_iota(jnp.int32, (count, count), 0)
    i_col = lax.broadcasted_iota(jnp.int32, (count, count), 1)
    ranking = jnp.sum(
        jnp.where((owner[:, None] == owner[None, :]) & (i_row < i_col), 1, 0), axis=0
    ).astype(jnp.int32)
    slot = lane * capacity + ranking
    absolute = owner * capacity + ranking
    hit = absolute[None, :] == lax.broadcasted_iota(jnp.int32, (slots, count), 0)
    outgoing_at = jnp.min(jnp.where(hit, offset[None, :], count), axis=1).astype(jnp.int32)
    landing = lax.all_to_all(
        outgoing_at.reshape(curve_size, 1, capacity), "curve", split_axis=0, concat_axis=0, tiled=True
    )
    if chunks > 1:
        sources = jnp.arange(curve_size) ^ lax.axis_index("curve")
        landing = jnp.sum(
            jnp.where(
                sources[:, None, None] == jnp.arange(curve_size)[None, :, None], landing[:, 0][None], 0
            ),
            axis=1,
        )
    landing = landing.reshape(1, slots)
    slot = slot.reshape(1, count)

    rows_f32 = jax.ShapeDtypeStruct((count, width), F32)
    q, k, v, own_mixed, own_sums = vmem_call(
        functools.partial(prep_body, depth),
        (rows_bf16,) * 3 + (rows_f32,) * 2,
        name="prep",
        flops=2 << 30,
        moved=4 << 20,
    )(x, gain_one, qkv_one)
    dma = pltpu.SemaphoreType.DMA
    results = vmem_call(
        functools.partial(forward_body, peers, chunks, depth),
        (all_bf16, all_bf16, rows_bf16, rows_f32, jax.ShapeDtypeStruct((HEADS, count), F32))
        + (chunk_bf16,) * chunks,
        [
            pltpu.VMEM((peers, count, width), BF16),
            pltpu.VMEM((slots, width), BF16),
            dma((peers,)),
            dma((chunks,)),
        ],
        name="forward",
        flops=8 << 30,
        moved=8 << 20,
        in_specs=[VMEM_SPEC] * 10 + [HBM_SPEC] * peers,
        out_specs=(VMEM_SPEC,) * 5 + (HBM_SPEC,) * chunks,
    )(x, q, k, v, own_mixed, own_sums, gain_one, qkv_one, out_one, slot, *others)
    keys_all, values_all, mixed, lse, lse_rows = results[:5]
    arrived = exchange(results[5:], "curve")
    lse_all = [lse_rows] + [by_xor(lse_rows, "patch", m) for m in range(1, patch_size)]

    queries_all = vmem_call(
        functools.partial(queries_body, peers),
        all_bf16,
        [pltpu.VMEM((peers, count, width), BF16), dma((peers,))],
        name="queries",
        flops=1 << 29,
        moved=3 << 20,
        in_specs=[VMEM_SPEC] * 3 + [HBM_SPEC] * peers,
    )(gain_one, qkv_one, q, *others)
    stack = jax.ShapeDtypeStruct((HEADS, count, total), BF16)
    weights = vmem_call(
        functools.partial(weights_body, depth), stack, name="weights", flops=4 << 30, moved=10 << 20
    )(q, keys_all, lse)
    flipped = vmem_call(
        functools.partial(weights_flipped_body, peers, depth),
        stack,
        name="weights_flipped",
        flops=4 << 30,
        moved=10 << 20,
    )(k, queries_all, *lse_all)

    returning = vmem_call(
        functools.partial(second_body, chunks, depth),
        (chunk_bf16,) * chunks,
        [
            pltpu.VMEM((slots, width), BF16),
            pltpu.VMEM((count, 3 * width), BF16),
            pltpu.VMEM((count, 3 * width), BF16),
            pltpu.VMEM((count, width), BF16),
            pltpu.VMEM((count, count), F32),
            dma((chunks,)),
            dma((chunks,)),
        ],
        name="second",
        flops=8 << 30,
        moved=4 << 20,
        in_specs=[VMEM_SPEC] * 6 + [HBM_SPEC] * chunks,
        out_specs=(HBM_SPEC,) * chunks,
    )(
        landing,
        segments.reshape(1, count),
        gain_two,
        qkv_two,
        out_two,
        out_grad.reshape(count, width),
        *arrived,
    )
    home = exchange(returning, "curve")

    grad_shape = jax.ShapeDtypeStruct((count + HEADS, width), BF16)
    moved_grad, grad_own, delta, grad_send = vmem_call(
        functools.partial(home_body, chunks, depth),
        (rows_bf16, grad_shape, rows_f32, grad_shape),
        [pltpu.VMEM((slots, width), BF16), dma((chunks,)), dma(())],
        name="home",
        flops=1 << 29,
        moved=2 << 20,
        in_specs=[VMEM_SPEC] * 3 + [HBM_SPEC] * chunks,
        out_specs=(VMEM_SPEC,) * 3 + (HBM_SPEC,),
    )(slot, mixed, out_one, *home)
    grads = [by_xor(grad_send, "patch", m) for m in range(1, patch_size)]

    query_grad, key_own, value_own = vmem_call(
        functools.partial(query_grad_body, depth),
        (rows_bf16, rows_f32, rows_f32),
        [pltpu.VMEM((HEADS, count), F32)],
        name="query_grad",
        flops=8 << 30,
        moved=10 << 20,
    )(weights, flipped, grad_own, delta, keys_all, values_all, q)
    result = vmem_call(
        functools.partial(key_grad_body, peers, depth),
        rows_bf16,
        [
            pltpu.VMEM((count, 3 * width), BF16),
            pltpu.VMEM((peers * count, width), BF16),
            pltpu.VMEM((peers, HEADS, width), BF16),
            pltpu.VMEM((HEADS, peers * count), F32),
            dma((2 * peers,)),
        ],
        name="key_grad",
        flops=8 << 30,
        moved=14 << 20,
        in_specs=[VMEM_SPEC] * 10 + [HBM_SPEC] * peers,
    )(flipped, v, queries_all, query_grad, key_own, value_own, x, gain_one, qkv_one, moved_grad, *grads)
    return result.reshape(points.shape)


def solution(mesh):
    in_specs = (
        P("curve", "patch", None, None),
        P(),
        P(),
        P(),
        P("curve", "patch", None),
        P(),
        P(),
        P(),
        P("patch", "curve", None),
        P("patch", "curve", None, None),
    )
    out_specs = P("curve", "patch", None, None)
    return jax.shard_map(shards, mesh=mesh, in_specs=in_specs, out_specs=out_specs, check_vma=False)
```

```python
import functools
import math

import jax
import jax.numpy as jnp
from jax import lax
from jax.experimental import pallas as pl
from jax.experimental.pallas import tpu as pltpu
from jax.sharding import PartitionSpec as P

HEADS = 16
EPS = 1e-06
LANES = 128
MASKED = -1e30
F32 = jnp.float32
BF16 = jnp.bfloat16
LOG2E = math.log2(math.e)


def dot_nn(left, right):
    return lax.dot_general(left, right, (((1,), (0,)), ((), ())), preferred_element_type=F32)


def dot_nt(left, right):
    return lax.dot_general(left, right, (((1,), (1,)), ((), ())), preferred_element_type=F32)


def dot_tn(left, right):
    return lax.dot_general(left, right, (((0,), (0,)), ((), ())), preferred_element_type=F32)


def norm_rows(rows, gain):
    wide = rows.astype(F32)
    power = jnp.mean(wide * wide, axis=-1, keepdims=True)
    return (wide * lax.rsqrt(power + EPS) * gain).astype(BF16)


def norm_pull(rows, gain, cotangent):
    wide = rows.astype(F32)
    power = jnp.mean(wide * wide, axis=-1, keepdims=True)
    inverse = lax.rsqrt(power + EPS)
    scaled = cotangent.astype(F32) * gain
    along = jnp.mean(scaled * wide, axis=-1, keepdims=True)
    return (inverse * scaled - wide * (inverse * inverse * inverse * along)).astype(BF16)


def head_mask(rows, index, depth):
    return lax.broadcasted_iota(jnp.int32, (rows, LANES), 1) // depth == index


def only(mask, tile):
    return jnp.where(mask, tile, jnp.zeros_like(tile))


def tile_at(t):
    return pl.ds(pl.multiple_of(t * LANES, LANES), LANES)


def vmem_call(body, outs, scratch=(), name=None, flops=0, moved=0, **more):
    params = pltpu.CompilerParams(vmem_limit_bytes=24 << 20, **more.pop("params", {}))
    return pl.pallas_call(
        body,
        out_shape=outs,
        scratch_shapes=scratch,
        compiler_params=params,
        name=name,
        cost_estimate=pl.CostEstimate(flops=flops, bytes_accessed=moved, transcendentals=0),
        **more,
    )


HBM_SPEC = pl.BlockSpec(memory_space=pltpu.MemorySpace.HBM)
SMEM_SPEC = pl.BlockSpec(memory_space=pltpu.MemorySpace.SMEM)
VMEM_SPEC = pl.BlockSpec(memory_space=pltpu.MemorySpace.VMEM)
LOW, HIGH = 2.0**-60, 2.0**100


def column(row):
    return jnp.transpose(jnp.broadcast_to(row.astype(F32), (LANES, row.shape[1])))[:, :1]


def start_all(pairs, sems):
    copies = [pltpu.make_async_copy(src, dst, sems.at[i]) for i, (src, dst) in enumerate(pairs)]
    for copy in copies:
        copy.start()
    return copies


def flip_tile(tile):
    return jnp.transpose(tile)


def with_ones(tile):
    return jnp.concatenate([tile, jnp.ones_like(tile)], axis=1)


def unshifted(depth, t, q_tile, k_tile, v_tile, weights_ref, columns):
    count = q_tile.shape[0]
    scale = depth ** (-0.5) * LOG2E
    right = with_ones(v_tile)
    mixed = jnp.zeros((count, LANES), F32)
    sums = jnp.zeros((count, LANES), F32)
    for j in range(LANES // depth):
        mask = head_mask(count, j, depth)
        scores = dot_nt(only(mask, q_tile), k_tile)
        shifted = jnp.exp2(scores * scale).astype(BF16)
        weights_ref[t * (LANES // depth) + j, :, columns] = shifted
        both = dot_nn(shifted, right)
        mixed = jnp.where(mask, both[:, :LANES], mixed)
        sums = jnp.where(mask, both[:, LANES:], sums)
    return mixed, sums


def route_body(chunks, capacity, me_ref, target_ref, slot_ref, at_ref):
    count = target_ref.shape[1]
    slots = 2 * count
    target = target_ref[...]
    shift = count.bit_length() - 1
    owner = lax.shift_right_logical(target, jnp.full_like(target, shift))
    offset = target - lax.shift_left(owner, jnp.full_like(target, shift))
    same = column(owner) == owner.astype(F32)
    earlier = lax.broadcasted_iota(jnp.int32, (count, count), 0) < (
        lax.broadcasted_iota(jnp.int32, (count, count), 1)
    )
    ranking = jnp.sum(jnp.where(same & earlier, 1.0, 0.0), axis=0, keepdims=True).astype(jnp.int32)
    lane = owner if chunks == 1 else lax.bitwise_xor(owner, jnp.full_like(owner, me_ref[0]))
    slot_ref[...] = lane * capacity + ranking
    hit = column(owner * capacity + ranking) == (
        lax.broadcasted_iota(jnp.int32, (count, slots), 1).astype(F32)
    )
    at = jnp.sum(jnp.where(hit, column(offset) - count, 0.0), axis=0, keepdims=True) + count
    if chunks == 1:
        at_ref[...] = at.astype(jnp.int32)
    else:
        for m in range(chunks):
            at_ref[m] = at[:, m * capacity : (m + 1) * capacity].astype(jnp.int32)


def prep_body(depth, *refs):
    x_ref, gain_ref, w_ref = refs[:3]
    q_ref, k_ref, v_ref, weights_ref, mixed_ref, sums_ref = refs[3:]
    count, width = x_ref.shape
    normed = norm_rows(x_ref[...], gain_ref[...])
    q_ref[...] = dot_nn(normed, w_ref[:, :width]).astype(BF16)
    k_ref[...] = dot_nn(normed, w_ref[:, width : 2 * width]).astype(BF16)
    v_ref[...] = dot_nn(normed, w_ref[:, 2 * width :]).astype(BF16)

    def tile_step(t, carry):
        at = tile_at(t)
        mixed_ref[:, at], sums_ref[:, at] = unshifted(
            depth, t, q_ref[:, at], k_ref[:, at], v_ref[:, at], weights_ref, slice(0, count)
        )
        return carry

    lax.fori_loop(0, width // LANES, tile_step, 0)


def forward_body(peers, chunks, depth, *refs):
    x_ref, gain_ref, w_ref, out_w_ref, slot_ref = refs[:5]
    q_ref, k_ref, v_ref, own_weights_ref, own_mixed_ref, own_sums_ref = refs[5:11]
    others = refs[11 : 11 + peers]
    keys_ref, values_ref, weights_ref, mixed_ref, inverse_ref, lse_ref = refs[11 + peers : 17 + peers]
    sends = refs[17 + peers : 17 + peers + chunks]
    outgoing, out_sems = refs[17 + peers + chunks :]
    count, width = x_ref.shape
    heads = LANES // depth
    keys_ref[:count] = k_ref[...]
    values_ref[:count] = v_ref[...]
    for index, other in enumerate(others):
        rows = slice((index + 1) * count, (index + 2) * count)
        normed = norm_rows(other[...], gain_ref[...])
        keys_ref[rows] = dot_nn(normed, w_ref[:, width : 2 * width]).astype(BF16)
        values_ref[rows] = dot_nn(normed, w_ref[:, 2 * width :]).astype(BF16)
    total = keys_ref.shape[0]

    def finish_tile(t, at, mixed, sums, tops):
        inverse = 1.0 / sums
        mixed_ref[:, at] = (mixed * inverse).astype(BF16)
        inverse_ref[:, at] = inverse
        flipped = flip_tile(tops + jnp.log(sums) * LOG2E)
        for j in range(heads):
            lse_ref[pl.ds(t * heads + j, 1)] = flipped[j * depth : j * depth + 1]

    def fast_step(t, bad):
        at = tile_at(t)
        mixed, sums = unshifted(
            depth,
            t,
            q_ref[:, at],
            keys_ref[count:, at],
            values_ref[count:, at],
            weights_ref,
            slice(count, total),
        )
        for j in range(heads):
            weights_ref[t * heads + j, :, :count] = own_weights_ref[t * heads + j]
        mixed += own_mixed_ref[:, at]
        sums += own_sums_ref[:, at]
        finish_tile(t, at, mixed, sums, 0.0)
        return jnp.where((sums >= LOW) & (sums <= HIGH), bad, 1.0)

    bad = lax.fori_loop(0, width // LANES, fast_step, jnp.zeros((count, LANES), F32))

    @pl.when(jnp.max(bad) > 0.0)
    def _():
        scale = depth ** (-0.5) * LOG2E

        def safe_step(t, carry):
            at = tile_at(t)
            right = with_ones(values_ref[:, at])
            mixed = jnp.zeros((count, LANES), F32)
            sums = jnp.ones((count, LANES), F32)
            tops = jnp.zeros((count, LANES), F32)
            for j in range(heads):
                mask = head_mask(count, j, depth)
                scores = dot_nt(only(mask, q_ref[:, at]), keys_ref[:, at])
                top = jnp.max(scores, axis=-1, keepdims=True) * scale
                shifted = jnp.exp2(scores * scale - top).astype(BF16)
                weights_ref[t * heads + j] = shifted
                both = dot_nn(shifted, right)
                mixed = jnp.where(mask, both[:, :LANES], mixed)
                sums = jnp.where(mask, both[:, LANES:], sums)
                tops = jnp.where(mask, top, tops)
            finish_tile(t, at, mixed, sums, tops)
            return carry

        lax.fori_loop(0, width // LANES, safe_step, 0)

    moved = (x_ref[...].astype(F32) + dot_nn(mixed_ref[...], out_w_ref[...])).astype(BF16)
    slots = 2 * count
    picked = (lax.broadcasted_iota(jnp.int32, (slots, count), 0) == slot_ref[...]).astype(F32)
    outgoing[...] = dot_nn(picked.astype(BF16), moved).astype(BF16)
    size = slots // chunks
    pairs = [(outgoing.at[i * size : (i + 1) * size], send) for i, send in enumerate(sends)]
    for copy in start_all(pairs, out_sems):
        copy.wait()


def second_body(chunks, depth, *refs):
    me_ref, land_ref, seg_ref, gain_ref, w_ref, out_w_ref, grad_ref = refs[:7]
    arrived = refs[7 : 7 + chunks]
    sends = refs[7 + chunks : 7 + 2 * chunks]
    staged, packed, packed_grad, mixed_grad, bias, out_sems = refs[7 + 2 * chunks :]
    count, width = grad_ref.shape
    slots = staged.shape[0]
    size = slots // chunks
    parts = [slice(i * size, (i + 1) * size) for i in range(chunks)]
    mixed_grad[...] = dot_nt(grad_ref[...], out_w_ref[...]).astype(BF16)
    bias[...] = jnp.where(column(seg_ref[...]) == seg_ref[...].astype(F32), 0.0, MASKED)
    if chunks == 1:
        landing = land_ref[...]
    else:
        sources = [lax.bitwise_xor(me_ref[0], jnp.int32(m)) for m in range(chunks)]
        landing = jnp.concatenate([land_ref[source] for source in sources], axis=1)
    place = (lax.broadcasted_iota(jnp.int32, (count, slots), 0) == landing).astype(F32)
    rows = jnp.concatenate([piece[...] for piece in arrived], axis=0)
    hilbert = dot_nn(place.astype(BF16), rows).astype(BF16)
    normed = norm_rows(hilbert, gain_ref[...])
    packed[...] = dot_nn(normed, w_ref[...]).astype(BF16)
    scale = depth ** (-0.5)

    def tile_step(t, carry):
        at = tile_at(t)
        k_at = tile_at(t + width // LANES)
        v_at = tile_at(t + 2 * (width // LANES))
        q_tile = packed[:, at]
        k_tile = packed[:, k_at]
        v_tile = packed[:, v_at]
        g_tile = mixed_grad[:, at]
        k_flipped = flip_tile(k_tile)
        heads = LANES // depth
        masks = [head_mask(count, j, depth) for j in range(heads)]
        stacked = (heads, count, count)
        k_heads = jnp.concatenate([only(mask, k_tile) for mask in masks], axis=0)
        v_heads = jnp.concatenate([only(mask, v_tile) for mask in masks], axis=0)
        scores = dot_nt(k_heads, q_tile).reshape(stacked) * (scale * LOG2E) + bias[...][None]
        weight_grad = dot_nt(v_heads, g_tile).reshape(stacked)
        shifted = jnp.exp2(scores - jnp.max(scores, axis=1, keepdims=True))
        weights = shifted * (1.0 / jnp.sum(shifted, axis=1, keepdims=True))
        carried = jnp.sum(weights * weight_grad, axis=1, keepdims=True)
        score_grad = (weights * (weight_grad - carried)).astype(BF16)
        dk_heads = dot_nn(score_grad.reshape(heads * count, count), q_tile)
        dv_heads = dot_nn(weights.astype(BF16).reshape(heads * count, count), g_tile)
        dk, dv, dq = dk_heads[:count], dv_heads[:count], []
        for j in range(heads):
            part = slice(j * count, (j + 1) * count)
            dk = jnp.where(masks[j], dk_heads[part], dk)
            dv = jnp.where(masks[j], dv_heads[part], dv)
            dq.append(dot_nn(k_flipped[j * depth : (j + 1) * depth], score_grad[j]))
        dq = jnp.transpose(jnp.concatenate(dq, axis=0))
        packed_grad[:, at] = (dq * scale).astype(BF16)
        packed_grad[:, k_at] = (dk * scale).astype(BF16)
        packed_grad[:, v_at] = dv.astype(BF16)
        return carry

    lax.fori_loop(0, width // LANES, tile_step, 0)
    normed_grad = dot_nt(packed_grad[...], w_ref[...]).astype(BF16)
    total = grad_ref[...].astype(F32) + norm_pull(hilbert, gain_ref[...], normed_grad).astype(F32)
    back = lax.broadcasted_iota(jnp.int32, (slots, count), 1).astype(F32) == column(landing)
    staged[...] = dot_nn(back.astype(F32).astype(BF16), total.astype(BF16)).astype(BF16)
    pairs = [(staged.at[parts[i]], send) for i, send in enumerate(sends)]
    for copy in start_all(pairs, out_sems):
        copy.wait()


def queries_body(peers, *refs):
    gain_ref, w_ref, q_ref = refs[:3]
    others = refs[3 : 3 + peers]
    out_ref = refs[3 + peers]
    count, width = q_ref.shape
    out_ref[:count] = q_ref[...]
    for index, other in enumerate(others):
        rows = slice((index + 1) * count, (index + 2) * count)
        normed = norm_rows(other[...], gain_ref[...])
        out_ref[rows] = dot_nn(normed, w_ref[:, :width]).astype(BF16)


def spread(rows, width):
    heads = rows.shape[0]
    pick = lax.broadcasted_iota(jnp.int32, (heads, width), 1) // (width // heads) == (
        lax.broadcasted_iota(jnp.int32, (heads, width), 0)
    )
    return dot_tn(rows, pick.astype(F32).astype(BF16))


def weights_flipped_body(peers, depth, *refs):
    k_ref, queries_ref = refs[:2]
    lse_refs = refs[2 : 3 + peers]
    out_ref = refs[3 + peers]
    scale = depth ** (-0.5) * LOG2E
    heads = LANES // depth
    count = k_ref.shape[0]

    def tile_step(t, carry):
        at = tile_at(t)
        for j in range(heads):
            mask = head_mask(count, j, depth)
            scores = dot_nt(only(mask, k_ref[:, at]), queries_ref[:, at])
            h = t * heads + j
            line = jnp.concatenate([ref[pl.ds(h, 1)] for ref in lse_refs], axis=1)
            out_ref[h] = jnp.exp2(scores * scale - line).astype(BF16)
        return carry

    lax.fori_loop(0, k_ref.shape[1] // LANES, tile_step, 0)


def home_body(chunks, depth, *refs):
    slot_ref, mixed_ref, out_w_ref = refs[:3]
    home = refs[3 : 3 + chunks]
    moved_ref, grad_ref, send_ref, send_sem = refs[3 + chunks :]
    count, width = moved_ref.shape
    slots = 2 * count
    take = lax.broadcasted_iota(jnp.int32, (count, slots), 1).astype(F32) == column(slot_ref[...])
    take = take.astype(F32).astype(BF16)
    moved = dot_nn(take, jnp.concatenate([piece[...] for piece in home], axis=0)).astype(BF16)
    moved_ref[...] = moved
    grad = dot_nt(moved, out_w_ref[...]).astype(BF16)
    grad_ref[:count] = grad
    product = grad.astype(F32) * mixed_ref[...].astype(F32)
    high = product.astype(BF16)
    low = (product - high.astype(F32)).astype(BF16)
    heads = width // depth
    pick = lax.broadcasted_iota(jnp.int32, (heads, width), 1) // depth == (
        lax.broadcasted_iota(jnp.int32, (heads, width), 0)
    )
    pick = pick.astype(F32).astype(BF16)
    rows = dot_nt(pick, high) + dot_nt(pick, low)
    rows_high = rows.astype(BF16)
    grad_ref[count:, :count] = rows_high
    grad_ref[count:, count:] = (rows - rows_high.astype(F32)).astype(BF16)
    send = pltpu.make_async_copy(grad_ref, send_ref, send_sem)
    send.start()
    send.wait()


def key_tile(depth, t, v_tile, weights_ref, columns, queries, grads, deltas_ref):
    count = v_tile.shape[0]
    heads = LANES // depth
    dk = jnp.zeros((count, LANES), F32)
    dv = jnp.zeros((count, LANES), F32)
    for j in range(heads):
        h = t * heads + j
        mask = head_mask(count, j, depth)
        weights = weights_ref[h, :, columns]
        weight_grad = dot_nt(only(mask, v_tile), grads)
        delta = deltas_ref[pl.ds(h, 1)]
        score_grad = (weights.astype(F32) * (weight_grad - delta)).astype(BF16)
        dv = jnp.where(mask, dot_nn(weights, grads), dv)
        dk = jnp.where(mask, dot_nn(score_grad, queries), dk)
    return dk, dv


def halves(lines):
    half = lines.shape[1] // 2
    return lines[:, :half], lines[:, half:]


def query_grad_body(depth, *refs):
    weights_ref, inverse_ref, flipped_ref, grad_ref, keys_ref, values_ref, q_ref = refs[:7]
    out_ref, dk_ref, dv_ref, lines, wide = refs[7:]
    count, width = out_ref.shape
    heads = LANES // depth
    high, low = halves(grad_ref[count:])
    lines[...] = high.astype(F32) + low.astype(F32)
    wide[...] = spread(high, width) + spread(low, width)

    def tile_step(t, carry):
        at = tile_at(t)
        g_tile = grad_ref[:count, at]
        delta_tile = wide[:, at]
        dq = jnp.zeros((count, LANES), F32)
        for j in range(heads):
            mask = head_mask(count, j, depth)
            weight_grad = dot_nt(only(mask, g_tile), values_ref[:, at])
            delta = delta_tile[:, j * depth : j * depth + 1]
            weights = weights_ref[t * heads + j].astype(F32)
            score_grad = (weights * (weight_grad - delta)).astype(BF16)
            dq = jnp.where(mask, dot_nn(score_grad, keys_ref[:, at]), dq)
        out_ref[:, at] = (dq * (inverse_ref[:, at] * depth ** (-0.5))).astype(BF16)
        dk_ref[:, at], dv_ref[:, at] = key_tile(
            depth,
            t,
            values_ref[:count, at],
            flipped_ref,
            slice(0, count),
            q_ref[:, at],
            g_tile,
            lines,
        )
        return carry

    lax.fori_loop(0, width // LANES, tile_step, 0)


def key_grad_body(peers, depth, *refs):
    flipped_ref, v_ref, queries_ref, dq_ref, dk_ref, dv_ref = refs[:6]
    x_ref, gain_ref, w_ref, moved_ref = refs[6:10]
    others = refs[10 : 10 + peers]
    out_ref, packed_grad, grads, lines = refs[10 + peers :]
    count, width = x_ref.shape
    packed_grad[:, :width] = dq_ref[...]
    for i, other in enumerate(others):
        rows = slice(i * count, (i + 1) * count)
        grads[rows] = other[:count]
        high, low = halves(other[count:])
        lines[:, rows] = high.astype(F32) + low.astype(F32)

    def tile_step(t, carry):
        at = tile_at(t)
        dk, dv = key_tile(
            depth,
            t,
            v_ref[:, at],
            flipped_ref,
            slice(count, (peers + 1) * count),
            queries_ref[count:, at],
            grads[:, at],
            lines,
        )
        dk = (dk + dk_ref[:, at]) * depth ** (-0.5)
        packed_grad[:, tile_at(t + width // LANES)] = dk.astype(BF16)
        packed_grad[:, tile_at(t + 2 * (width // LANES))] = (dv + dv_ref[:, at]).astype(BF16)
        return carry

    lax.fori_loop(0, width // LANES, tile_step, 0)
    normed_grad = dot_nt(packed_grad[...], w_ref[...]).astype(BF16)
    path = norm_pull(x_ref[...], gain_ref[...], normed_grad)
    out_ref[...] = (moved_ref[...].astype(F32) + path.astype(F32)).astype(BF16)


def by_xor(array, axis, step, label):
    size = lax.axis_size(axis)
    with jax.named_scope(f"{label}_{step}"):
        return lax.ppermute(array, axis, [(i, i ^ step) for i in range(size)])


def exchange(pieces, axis, label):
    if len(pieces) == 1:
        size = lax.axis_size(axis)
        stacked = pieces[0].reshape((size, -1) + pieces[0].shape[1:])
        got = lax.all_to_all(stacked, axis, split_axis=0, concat_axis=0, tiled=True)
        return [got.reshape(pieces[0].shape)]
    return [pieces[0]] + [by_xor(pieces[m], axis, m, label) for m in range(1, len(pieces))]


def shards(
    points, gain_one, qkv_one, out_one, hilbert_pos, gain_two, qkv_two, out_two, segments, out_grad
):
    count, width = points.shape[2:]
    depth = width // HEADS
    tiles = width // LANES
    per_tile = LANES // depth
    patch_size = lax.axis_size("patch")
    curve_size = lax.axis_size("curve")
    peers = patch_size - 1
    total = patch_size * count
    slots = 2 * count
    capacity = slots // curve_size
    chunks = curve_size if curve_size <= 16 else 1
    rows_bf16 = jax.ShapeDtypeStruct((count, width), BF16)
    all_bf16 = jax.ShapeDtypeStruct((total, width), BF16)
    chunk_bf16 = jax.ShapeDtypeStruct((slots // chunks, width), BF16)

    x = points.reshape(count, width)
    others = [by_xor(x, "patch", m, "points") for m in range(1, patch_size)]
    gain_one = gain_one.reshape(1, width)
    gain_two = gain_two.reshape(1, width)

    def shape(kind, *dims):
        return jax.ShapeDtypeStruct(dims, kind)

    me = lax.axis_index("curve").astype(jnp.int32).reshape(1)
    at_shape = (1, slots) if chunks == 1 else (chunks, 1, capacity)
    slot, outgoing_at = vmem_call(
        functools.partial(route_body, chunks, capacity),
        (shape(jnp.int32, 1, count), shape(jnp.int32, *at_shape)),
        name="route",
        flops=1 << 20,
        moved=1 << 12,
        in_specs=[SMEM_SPEC, VMEM_SPEC],
    )(me, hilbert_pos.reshape(1, count))
    with jax.named_scope("index_0"):
        landing = lax.all_to_all(
            outgoing_at.reshape(curve_size, 1, capacity),
            "curve",
            split_axis=0,
            concat_axis=0,
            tiled=True,
        ).reshape(at_shape)
    x_then, landing = lax.optimization_barrier((x, landing))

    rows_f32 = shape(F32, count, width)
    lines_f32 = shape(F32, HEADS, count)
    dma = pltpu.SemaphoreType.DMA
    q, k, v, own_weights, own_mixed, own_sums = vmem_call(
        functools.partial(prep_body, depth),
        (rows_bf16,) * 3 + (shape(BF16, HEADS, count, count),) + (rows_f32,) * 2,
        name="prep",
        flops=2 << 30,
        moved=4 << 20,
    )(x_then, gain_one, qkv_one)
    stack = shape(BF16, HEADS, count, total)
    results = vmem_call(
        functools.partial(forward_body, peers, chunks, depth),
        (all_bf16, all_bf16, stack, rows_bf16, rows_f32, lines_f32) + (chunk_bf16,) * chunks,
        [pltpu.VMEM((slots, width), BF16), dma((chunks,))],
        name="forward",
        flops=8 << 30,
        moved=8 << 20,
        in_specs=[VMEM_SPEC] * (11 + peers),
        out_specs=(VMEM_SPEC,) * 6 + (HBM_SPEC,) * chunks,
    )(x_then, gain_one, qkv_one, out_one, slot, q, k, v, own_weights, own_mixed, own_sums, *others)
    keys_all, values_all, weights, mixed, inverse, lse = results[:6]
    arrived = exchange(results[6:], "curve", "out")
    lse_all = [lse] + [by_xor(lse, "patch", m, "lse") for m in range(1, patch_size)]

    queries_all = vmem_call(
        functools.partial(queries_body, peers),
        all_bf16,
        name="queries",
        flops=1 << 29,
        moved=3 << 20,
        in_specs=[VMEM_SPEC] * (3 + peers),
    )(gain_one, qkv_one, q, *others)
    flipped = vmem_call(
        functools.partial(weights_flipped_body, peers, depth),
        stack,
        name="weights_flipped",
        flops=4 << 30,
        moved=10 << 20,
    )(k, queries_all, *lse_all)

    returning = vmem_call(
        functools.partial(second_body, chunks, depth),
        (chunk_bf16,) * chunks,
        [
            pltpu.VMEM((slots, width), BF16),
            pltpu.VMEM((count, 3 * width), BF16),
            pltpu.VMEM((count, 3 * width), BF16),
            pltpu.VMEM((count, width), BF16),
            pltpu.VMEM((count, count), F32),
            dma((chunks,)),
        ],
        name="second",
        flops=8 << 30,
        moved=4 << 20,
        in_specs=[SMEM_SPEC] + [VMEM_SPEC] * (6 + chunks),
        out_specs=(HBM_SPEC,) * chunks,
    )(
        me,
        landing,
        segments.reshape(1, count),
        gain_two,
        qkv_two,
        out_two,
        out_grad.reshape(count, width),
        *arrived,
    )
    home = exchange(returning, "curve", "back")

    grad_shape = shape(BF16, count + HEADS, width)
    moved_grad, grad_own, grad_send = vmem_call(
        functools.partial(home_body, chunks, depth),
        (rows_bf16, grad_shape, grad_shape),
        [dma(())],
        name="home",
        flops=1 << 29,
        moved=2 << 20,
        in_specs=[VMEM_SPEC] * (3 + chunks),
        out_specs=(VMEM_SPEC,) * 2 + (HBM_SPEC,),
    )(slot, mixed, out_one, *home)
    grads = [by_xor(grad_send, "patch", m, "grad") for m in range(1, patch_size)]

    query_grad, key_own, value_own = vmem_call(
        functools.partial(query_grad_body, depth),
        (rows_bf16, rows_f32, rows_f32),
        [pltpu.VMEM((HEADS, count), F32), pltpu.VMEM((count, width), F32)],
        name="query_grad",
        flops=8 << 30,
        moved=10 << 20,
    )(weights, inverse, flipped, grad_own, keys_all, values_all, q)
    result = vmem_call(
        functools.partial(key_grad_body, peers, depth),
        rows_bf16,
        [
            pltpu.VMEM((count, 3 * width), BF16),
            pltpu.VMEM((peers * count, width), BF16),
            pltpu.VMEM((HEADS, peers * count), F32),
        ],
        name="key_grad",
        flops=8 << 30,
        moved=14 << 20,
        in_specs=[VMEM_SPEC] * (10 + peers),
    )(
        flipped,
        v,
        queries_all,
        query_grad,
        key_own,
        value_own,
        x,
        gain_one,
        qkv_one,
        moved_grad,
        *grads,
    )
    return result.reshape(points.shape)


def solution(mesh):
    in_specs = (
        P("curve", "patch", None, None),
        P(),
        P(),
        P(),
        P("curve", "patch", None),
        P(),
        P(),
        P(),
        P("patch", "curve", None),
        P("patch", "curve", None, None),
    )
    out_specs = P("curve", "patch", None, None)
    return jax.shard_map(shards, mesh=mesh, in_specs=in_specs, out_specs=out_specs, check_vma=False)
```

```python
import functools
import math

import jax
import jax.numpy as jnp
from jax import lax
from jax.experimental import pallas as pl
from jax.experimental.pallas import tpu as pltpu
from jax.sharding import PartitionSpec as P

HEADS = 16
EPS = 1e-06
LANES = 128
MASKED = -1e30
F32 = jnp.float32
BF16 = jnp.bfloat16
LOG2E = math.log2(math.e)


def dot_nn(left, right):
    return lax.dot_general(left, right, (((1,), (0,)), ((), ())), preferred_element_type=F32)


def dot_nt(left, right):
    return lax.dot_general(left, right, (((1,), (1,)), ((), ())), preferred_element_type=F32)


def dot_tn(left, right):
    return lax.dot_general(left, right, (((0,), (0,)), ((), ())), preferred_element_type=F32)


def norm_rows(rows, gain):
    wide = rows.astype(F32)
    power = jnp.mean(wide * wide, axis=-1, keepdims=True)
    return (wide * lax.rsqrt(power + EPS) * gain).astype(BF16)


def norm_pull(rows, gain, cotangent):
    wide = rows.astype(F32)
    power = jnp.mean(wide * wide, axis=-1, keepdims=True)
    inverse = lax.rsqrt(power + EPS)
    scaled = cotangent.astype(F32) * gain
    along = jnp.mean(scaled * wide, axis=-1, keepdims=True)
    return (inverse * scaled - wide * (inverse * inverse * inverse * along)).astype(BF16)


def head_mask(rows, index, depth):
    return lax.broadcasted_iota(jnp.int32, (rows, LANES), 1) // depth == index


def only(mask, tile):
    return jnp.where(mask, tile, jnp.zeros_like(tile))


def tile_at(t):
    return pl.ds(pl.multiple_of(t * LANES, LANES), LANES)


def vmem_call(body, outs, scratch=(), name=None, flops=0, moved=0, **more):
    params = pltpu.CompilerParams(vmem_limit_bytes=24 << 20, **more.pop("params", {}))
    return pl.pallas_call(
        body,
        out_shape=outs,
        scratch_shapes=scratch,
        compiler_params=params,
        name=name,
        cost_estimate=pl.CostEstimate(flops=flops, bytes_accessed=moved, transcendentals=0),
        **more,
    )


HBM_SPEC = pl.BlockSpec(memory_space=pltpu.MemorySpace.HBM)
SMEM_SPEC = pl.BlockSpec(memory_space=pltpu.MemorySpace.SMEM)
VMEM_SPEC = pl.BlockSpec(memory_space=pltpu.MemorySpace.VMEM)
LOW, HIGH = 2.0**-60, 2.0**100


def column(row):
    return jnp.transpose(jnp.broadcast_to(row.astype(F32), (LANES, row.shape[1])))[:, :1]


def start_all(pairs, sems):
    copies = [pltpu.make_async_copy(src, dst, sems.at[i]) for i, (src, dst) in enumerate(pairs)]
    for copy in copies:
        copy.start()
    return copies


def flip_tile(tile):
    return jnp.transpose(tile)


def with_ones(tile):
    return jnp.concatenate([tile, jnp.ones_like(tile)], axis=1)


def unshifted(depth, t, q_tile, k_tile, v_tile, weights_ref):
    count = q_tile.shape[0]
    scale = depth ** (-0.5) * LOG2E
    right = with_ones(v_tile)
    mixed = jnp.zeros((count, LANES), F32)
    sums = jnp.zeros((count, LANES), F32)
    for j in range(LANES // depth):
        mask = head_mask(count, j, depth)
        scores = dot_nt(only(mask, q_tile), k_tile)
        shifted = jnp.exp2(scores * scale).astype(BF16)
        weights_ref[t * (LANES // depth) + j] = shifted
        both = dot_nn(shifted, right)
        mixed = jnp.where(mask, both[:, :LANES], mixed)
        sums = jnp.where(mask, both[:, LANES:], sums)
    return mixed, sums


def route_body(chunks, capacity, me_ref, target_ref, slot_ref, at_ref):
    count = target_ref.shape[1]
    slots = 2 * count
    target = target_ref[...]
    shift = count.bit_length() - 1
    owner = lax.shift_right_logical(target, jnp.full_like(target, shift))
    offset = target - lax.shift_left(owner, jnp.full_like(target, shift))
    same = column(owner) == owner.astype(F32)
    earlier = lax.broadcasted_iota(jnp.int32, (count, count), 0) < (
        lax.broadcasted_iota(jnp.int32, (count, count), 1)
    )
    ranking = jnp.sum(jnp.where(same & earlier, 1.0, 0.0), axis=0, keepdims=True).astype(jnp.int32)
    lane = owner if chunks == 1 else lax.bitwise_xor(owner, jnp.full_like(owner, me_ref[0]))
    slot_ref[...] = lane * capacity + ranking
    hit = column(lane * capacity + ranking) == (
        lax.broadcasted_iota(jnp.int32, (count, slots), 1).astype(F32)
    )
    at = jnp.sum(jnp.where(hit, column(offset) - count, 0.0), axis=0, keepdims=True) + count
    at_ref[...] = at.astype(at_ref.dtype)


def prep_body(depth, *refs):
    x_ref, gain_ref, w_ref = refs[:3]
    q_ref, k_ref, v_ref, weights_ref, mixed_ref, sums_ref = refs[3:]
    width = x_ref.shape[1]
    normed = norm_rows(x_ref[...], gain_ref[...])
    q_ref[...] = dot_nn(normed, w_ref[:, :width]).astype(BF16)
    k_ref[...] = dot_nn(normed, w_ref[:, width : 2 * width]).astype(BF16)
    v_ref[...] = dot_nn(normed, w_ref[:, 2 * width :]).astype(BF16)

    def tile_step(t, carry):
        at = tile_at(t)
        mixed_ref[:, at], sums_ref[:, at] = unshifted(
            depth, t, q_ref[:, at], k_ref[:, at], v_ref[:, at], weights_ref
        )
        return carry

    lax.fori_loop(0, width // LANES, tile_step, 0)


def middle_body(depth, *refs):
    x_ref, gain_ref, w_ref, q_ref, mixed_in_ref, sums_in_ref = refs[:6]
    k_ref, v_ref, weights_ref, mixed_ref, sums_ref = refs[6:]
    width = x_ref.shape[1]
    normed = norm_rows(x_ref[...], gain_ref[...])
    k_ref[...] = dot_nn(normed, w_ref[:, width : 2 * width]).astype(BF16)
    v_ref[...] = dot_nn(normed, w_ref[:, 2 * width :]).astype(BF16)

    def tile_step(t, carry):
        at = tile_at(t)
        mixed, sums = unshifted(depth, t, q_ref[:, at], k_ref[:, at], v_ref[:, at], weights_ref)
        mixed_ref[:, at] = mixed + mixed_in_ref[:, at]
        sums_ref[:, at] = sums + sums_in_ref[:, at]
        return carry

    lax.fori_loop(0, width // LANES, tile_step, 0)


def forward_body(early, peers, chunks, capacity, depth, *refs):
    x_ref, gain_ref, w_ref, out_w_ref, slot_ref, at_ref, q_ref, mixed_in_ref, sums_in_ref = refs[:9]
    refs = refs[9:]
    early_keys, early_values, refs = refs[:early], refs[early : 2 * early], refs[2 * early :]
    others, refs = refs[: peers + 1 - early], refs[peers + 1 - early + early :]
    keys_ref, values_ref, weights_ref, mixed_ref, inverse_ref, lse_ref = refs[:6]
    early_weights, refs = refs[6 : 6 + early], refs[6 + early :]
    sends, (outgoing, safe, out_sems) = refs[:chunks], refs[chunks:]
    count, width = x_ref.shape
    heads = LANES // depth
    for index, other in enumerate(others):
        rows = slice(index * count, (index + 1) * count)
        normed = norm_rows(other[...], gain_ref[...])
        keys_ref[rows] = dot_nn(normed, w_ref[:, width : 2 * width]).astype(BF16)
        values_ref[rows] = dot_nn(normed, w_ref[:, 2 * width :]).astype(BF16)

    def finish_tile(t, at, mixed, sums, tops):
        inverse = 1.0 / sums
        mixed_ref[:, at] = (mixed * inverse).astype(BF16)
        inverse_ref[:, at] = inverse
        flipped = flip_tile(tops + jnp.log(sums) * LOG2E)
        for j in range(heads):
            lse_ref[pl.ds(t * heads + j, 1)] = flipped[j * depth : j * depth + 1]

    def fast_step(t, bad):
        at = tile_at(t)
        mixed, sums = unshifted(
            depth, t, q_ref[:, at], keys_ref[:, at], values_ref[:, at], weights_ref
        )
        mixed += mixed_in_ref[:, at]
        sums += sums_in_ref[:, at]
        finish_tile(t, at, mixed, sums, 0.0)
        return jnp.where((sums >= LOW) & (sums <= HIGH), bad, 1.0)

    bad = lax.fori_loop(0, width // LANES, fast_step, jnp.zeros((count, LANES), F32))

    @pl.when(jnp.max(bad) > 0.0)
    def _():
        scale = depth ** (-0.5) * LOG2E

        def safe_step(t, carry):
            at = tile_at(t)
            keys = jnp.concatenate([ref[:, at] for ref in early_keys + (keys_ref,)], axis=0)
            values = jnp.concatenate([ref[:, at] for ref in early_values + (values_ref,)], axis=0)
            right = with_ones(values)
            mixed = jnp.zeros((count, LANES), F32)
            sums = jnp.ones((count, LANES), F32)
            tops = jnp.zeros((count, LANES), F32)
            for j in range(heads):
                mask = head_mask(count, j, depth)
                scores = dot_nt(only(mask, q_ref[:, at]), keys)
                top = jnp.max(scores, axis=-1, keepdims=True) * scale
                shifted = jnp.exp2(scores * scale - top).astype(BF16)
                weights_ref[t * heads + j] = shifted[:, early * count :]
                for index in range(early):
                    part = shifted[:, index * count : (index + 1) * count]
                    safe[index, t * heads + j] = part
                both = dot_nn(shifted, right)
                mixed = jnp.where(mask, both[:, :LANES], mixed)
                sums = jnp.where(mask, both[:, LANES:], sums)
                tops = jnp.where(mask, top, tops)
            finish_tile(t, at, mixed, sums, tops)
            return carry

        lax.fori_loop(0, width // LANES, safe_step, 0)
        pairs = [(safe.at[index], early_weights[index]) for index in range(early)]
        for copy in start_all(pairs, out_sems):
            copy.wait()

    moved = (x_ref[...].astype(F32) + dot_nn(mixed_ref[...], out_w_ref[...])).astype(BF16)
    slots = 2 * count
    picked = (lax.broadcasted_iota(jnp.int32, (slots, count), 0) == slot_ref[...]).astype(F32)
    leaving = dot_nn(picked.astype(BF16), moved).astype(BF16)
    if chunks == 1:
        outgoing[0] = leaving
    else:
        line = jnp.broadcast_to(at_ref[...], (outgoing.shape[1], slots)).astype(BF16)
        for m in range(chunks):
            part = slice(m * capacity, (m + 1) * capacity)
            for t in range(width // LANES):
                tile = leaving[part, t * LANES : (t + 1) * LANES]
                outgoing[m, t * capacity : (t + 1) * capacity] = tile
            tail = outgoing.shape[1] - capacity * (width // LANES)
            outgoing[m, outgoing.shape[1] - tail :, :capacity] = line[:tail, part]
    pairs = [(outgoing.at[i], send) for i, send in enumerate(sends)]
    for copy in start_all(pairs, out_sems):
        copy.wait()


def second_body(chunks, depth, *refs):
    land_ref, seg_ref, gain_ref, w_ref, out_w_ref, grad_ref = refs[:6]
    arrived = refs[6 : 6 + chunks]
    sends = refs[6 + chunks : 6 + 2 * chunks]
    staged, packed, packed_grad, mixed_grad, bias, out_sems = refs[6 + 2 * chunks :]
    count, width = grad_ref.shape
    slots = staged.shape[0]
    size = slots // chunks
    parts = [slice(i * size, (i + 1) * size) for i in range(chunks)]
    mixed_grad[...] = dot_nt(grad_ref[...], out_w_ref[...]).astype(BF16)
    bias[...] = jnp.where(column(seg_ref[...]) == seg_ref[...].astype(F32), 0.0, MASKED)
    if chunks == 1:
        landing = land_ref[...].astype(F32)
        rows = arrived[0][...]
    else:
        ends = [piece[size * (width // LANES) :].astype(F32)[:1, :size] for piece in arrived]
        landing = jnp.concatenate(ends, axis=1)
        rows = []
        for piece in arrived:
            tiles = [piece[t * size : (t + 1) * size] for t in range(width // LANES)]
            rows.append(jnp.concatenate(tiles, axis=1))
        rows = jnp.concatenate(rows, axis=0)
    place = lax.broadcasted_iota(jnp.int32, (count, slots), 0).astype(F32) == landing
    place = place.astype(F32)
    hilbert = dot_nn(place.astype(BF16), rows).astype(BF16)
    normed = norm_rows(hilbert, gain_ref[...])
    packed[...] = dot_nn(normed, w_ref[...]).astype(BF16)
    scale = depth ** (-0.5)

    def tile_step(t, carry):
        at = tile_at(t)
        k_at = tile_at(t + width // LANES)
        v_at = tile_at(t + 2 * (width // LANES))
        q_tile = packed[:, at]
        k_tile = packed[:, k_at]
        v_tile = packed[:, v_at]
        g_tile = mixed_grad[:, at]
        k_flipped = flip_tile(k_tile)
        heads = LANES // depth
        masks = [head_mask(count, j, depth) for j in range(heads)]
        stacked = (heads, count, count)
        k_heads = jnp.concatenate([only(mask, k_tile) for mask in masks], axis=0)
        v_heads = jnp.concatenate([only(mask, v_tile) for mask in masks], axis=0)
        scores = dot_nt(k_heads, q_tile).reshape(stacked) * (scale * LOG2E) + bias[...][None]
        weight_grad = dot_nt(v_heads, g_tile).reshape(stacked)
        shifted = jnp.exp2(scores - jnp.max(scores, axis=1, keepdims=True))
        weights = shifted * (1.0 / jnp.sum(shifted, axis=1, keepdims=True))
        carried = jnp.sum(weights * weight_grad, axis=1, keepdims=True)
        score_grad = (weights * (weight_grad - carried)).astype(BF16)
        dk_heads = dot_nn(score_grad.reshape(heads * count, count), q_tile)
        dv_heads = dot_nn(weights.astype(BF16).reshape(heads * count, count), g_tile)
        dk, dv, dq = dk_heads[:count], dv_heads[:count], []
        for j in range(heads):
            part = slice(j * count, (j + 1) * count)
            dk = jnp.where(masks[j], dk_heads[part], dk)
            dv = jnp.where(masks[j], dv_heads[part], dv)
            dq.append(dot_nn(k_flipped[j * depth : (j + 1) * depth], score_grad[j]))
        dq = jnp.transpose(jnp.concatenate(dq, axis=0))
        packed_grad[:, at] = (dq * scale).astype(BF16)
        packed_grad[:, k_at] = (dk * scale).astype(BF16)
        packed_grad[:, v_at] = dv.astype(BF16)
        return carry

    lax.fori_loop(0, width // LANES, tile_step, 0)
    normed_grad = dot_nt(packed_grad[...], w_ref[...]).astype(BF16)
    total = grad_ref[...].astype(F32) + norm_pull(hilbert, gain_ref[...], normed_grad).astype(F32)
    back = lax.broadcasted_iota(jnp.int32, (slots, count), 1).astype(F32) == column(landing)
    staged[...] = dot_nn(back.astype(F32).astype(BF16), total.astype(BF16)).astype(BF16)
    pairs = [(staged.at[parts[i]], send) for i, send in enumerate(sends)]
    for copy in start_all(pairs, out_sems):
        copy.wait()


def queries_body(peers, *refs):
    gain_ref, w_ref, q_ref = refs[:3]
    others = refs[3 : 3 + peers]
    out_ref = refs[3 + peers]
    count, width = q_ref.shape
    out_ref[:count] = q_ref[...]
    for index, other in enumerate(others):
        rows = slice((index + 1) * count, (index + 2) * count)
        normed = norm_rows(other[...], gain_ref[...])
        out_ref[rows] = dot_nn(normed, w_ref[:, :width]).astype(BF16)


def spread(rows, width):
    heads = rows.shape[0]
    pick = lax.broadcasted_iota(jnp.int32, (heads, width), 1) // (width // heads) == (
        lax.broadcasted_iota(jnp.int32, (heads, width), 0)
    )
    return dot_tn(rows, pick.astype(F32).astype(BF16))


def weights_flipped_body(peers, depth, *refs):
    k_ref, queries_ref = refs[:2]
    lse_refs = refs[2 : 3 + peers]
    out_ref = refs[3 + peers]
    scale = depth ** (-0.5) * LOG2E
    heads = LANES // depth
    count = k_ref.shape[0]

    def tile_step(t, carry):
        at = tile_at(t)
        for j in range(heads):
            mask = head_mask(count, j, depth)
            scores = dot_nt(only(mask, k_ref[:, at]), queries_ref[:, at])
            h = t * heads + j
            line = jnp.concatenate([ref[pl.ds(h, 1)] for ref in lse_refs], axis=1)
            out_ref[h] = jnp.exp2(scores * scale - line).astype(BF16)
        return carry

    lax.fori_loop(0, k_ref.shape[1] // LANES, tile_step, 0)


def home_body(chunks, depth, *refs):
    slot_ref, mixed_ref, out_w_ref = refs[:3]
    home = refs[3 : 3 + chunks]
    moved_ref, grad_ref, send_ref, send_sem = refs[3 + chunks :]
    count, width = moved_ref.shape
    slots = 2 * count
    take = lax.broadcasted_iota(jnp.int32, (count, slots), 1).astype(F32) == column(slot_ref[...])
    take = take.astype(F32).astype(BF16)
    moved = dot_nn(take, jnp.concatenate([piece[...] for piece in home], axis=0)).astype(BF16)
    moved_ref[...] = moved
    grad = dot_nt(moved, out_w_ref[...]).astype(BF16)
    grad_ref[:count] = grad
    product = grad.astype(F32) * mixed_ref[...].astype(F32)
    high = product.astype(BF16)
    low = (product - high.astype(F32)).astype(BF16)
    heads = width // depth
    pick = lax.broadcasted_iota(jnp.int32, (heads, width), 1) // depth == (
        lax.broadcasted_iota(jnp.int32, (heads, width), 0)
    )
    pick = pick.astype(F32).astype(BF16)
    rows = dot_nt(pick, high) + dot_nt(pick, low)
    rows_high = rows.astype(BF16)
    grad_ref[count:, :count] = rows_high
    grad_ref[count:, count:] = (rows - rows_high.astype(F32)).astype(BF16)
    send = pltpu.make_async_copy(grad_ref, send_ref, send_sem)
    send.start()
    send.wait()


def key_tile(depth, t, v_tile, weights_ref, columns, queries, grads, deltas_ref):
    count = v_tile.shape[0]
    heads = LANES // depth
    dk = jnp.zeros((count, LANES), F32)
    dv = jnp.zeros((count, LANES), F32)
    for j in range(heads):
        h = t * heads + j
        mask = head_mask(count, j, depth)
        weights = weights_ref[h, :, columns]
        weight_grad = dot_nt(only(mask, v_tile), grads)
        delta = deltas_ref[pl.ds(h, 1)]
        score_grad = (weights.astype(F32) * (weight_grad - delta)).astype(BF16)
        dv = jnp.where(mask, dot_nn(weights, grads), dv)
        dk = jnp.where(mask, dot_nn(score_grad, queries), dk)
    return dk, dv


def halves(lines):
    half = lines.shape[1] // 2
    return lines[:, :half], lines[:, half:]


def query_grad_body(parts, depth, *refs):
    weights_refs, refs = refs[:parts], refs[parts:]
    keys_refs, refs = refs[:parts], refs[parts:]
    values_refs, refs = refs[:parts], refs[parts:]
    inverse_ref, flipped_ref, grad_ref, q_ref = refs[:4]
    out_ref, dk_ref, dv_ref, lines, wide = refs[4:]
    count, width = out_ref.shape
    heads = LANES // depth
    high, low = halves(grad_ref[count:])
    lines[...] = high.astype(F32) + low.astype(F32)
    wide[...] = spread(high, width) + spread(low, width)

    def tile_step(t, carry):
        at = tile_at(t)
        g_tile = grad_ref[:count, at]
        delta_tile = wide[:, at]
        keys = jnp.concatenate([ref[:, at] for ref in keys_refs], axis=0)
        values = jnp.concatenate([ref[:, at] for ref in values_refs], axis=0)
        dq = jnp.zeros((count, LANES), F32)
        for j in range(heads):
            mask = head_mask(count, j, depth)
            weight_grad = dot_nt(only(mask, g_tile), values)
            delta = delta_tile[:, j * depth : j * depth + 1]
            weights = jnp.concatenate([ref[t * heads + j] for ref in weights_refs], axis=1)
            score_grad = (weights.astype(F32) * (weight_grad - delta)).astype(BF16)
            dq = jnp.where(mask, dot_nn(score_grad, keys), dq)
        out_ref[:, at] = (dq * (inverse_ref[:, at] * depth ** (-0.5))).astype(BF16)
        dk_ref[:, at], dv_ref[:, at] = key_tile(
            depth,
            t,
            values_refs[0][:, at],
            flipped_ref,
            slice(0, count),
            q_ref[:, at],
            g_tile,
            lines,
        )
        return carry

    lax.fori_loop(0, width // LANES, tile_step, 0)


def key_middle_body(index, depth, *refs):
    flipped_ref, v_ref, queries_ref, dk_in_ref, dv_in_ref, grad_ref = refs[:6]
    dk_ref, dv_ref, lines = refs[6:]
    count, width = v_ref.shape
    high, low = halves(grad_ref[count:])
    lines[...] = high.astype(F32) + low.astype(F32)
    rows = slice(index * count, (index + 1) * count)

    def tile_step(t, carry):
        at = tile_at(t)
        dk, dv = key_tile(
            depth,
            t,
            v_ref[:, at],
            flipped_ref,
            rows,
            queries_ref[rows, at],
            grad_ref[:count, at],
            lines,
        )
        dk_ref[:, at] = dk + dk_in_ref[:, at]
        dv_ref[:, at] = dv + dv_in_ref[:, at]
        return carry

    lax.fori_loop(0, width // LANES, tile_step, 0)


def key_grad_body(early, peers, depth, *refs):
    flipped_ref, v_ref, queries_ref, dq_ref, dk_ref, dv_ref = refs[:6]
    x_ref, gain_ref, w_ref, moved_ref = refs[6:10]
    others = refs[10 : 11 + peers - early]
    out_ref, packed_grad, grads, lines = refs[11 + peers - early :]
    count, width = x_ref.shape
    packed_grad[:, :width] = dq_ref[...]
    for i, other in enumerate(others):
        rows = slice(i * count, (i + 1) * count)
        grads[rows] = other[:count]
        high, low = halves(other[count:])
        lines[:, rows] = high.astype(F32) + low.astype(F32)

    def tile_step(t, carry):
        at = tile_at(t)
        dk, dv = key_tile(
            depth,
            t,
            v_ref[:, at],
            flipped_ref,
            slice(early * count, (peers + 1) * count),
            queries_ref[early * count :, at],
            grads[:, at],
            lines,
        )
        dk = (dk + dk_ref[:, at]) * depth ** (-0.5)
        packed_grad[:, tile_at(t + width // LANES)] = dk.astype(BF16)
        packed_grad[:, tile_at(t + 2 * (width // LANES))] = (dv + dv_ref[:, at]).astype(BF16)
        return carry

    lax.fori_loop(0, width // LANES, tile_step, 0)
    normed_grad = dot_nt(packed_grad[...], w_ref[...]).astype(BF16)
    path = norm_pull(x_ref[...], gain_ref[...], normed_grad)
    out_ref[...] = (moved_ref[...].astype(F32) + path.astype(F32)).astype(BF16)


def by_xor(array, axis, step, label):
    size = lax.axis_size(axis)
    with jax.named_scope(f"{label}_{step}"):
        return lax.ppermute(array, axis, [(i, i ^ step) for i in range(size)])


def exchange(pieces, axis, label):
    if len(pieces) == 1:
        size = lax.axis_size(axis)
        stacked = pieces[0].reshape((size, -1) + pieces[0].shape[1:])
        got = lax.all_to_all(stacked, axis, split_axis=0, concat_axis=0, tiled=True)
        return [got.reshape(pieces[0].shape)]
    return [pieces[0]] + [by_xor(pieces[m], axis, m, label) for m in range(1, len(pieces))]


def shards(
    points, gain_one, qkv_one, out_one, hilbert_pos, gain_two, qkv_two, out_two, segments, out_grad
):
    count, width = points.shape[2:]
    depth = width // HEADS
    tiles = width // LANES
    per_tile = LANES // depth
    patch_size = lax.axis_size("patch")
    curve_size = lax.axis_size("curve")
    peers = patch_size - 1
    total = patch_size * count
    slots = 2 * count
    capacity = slots // curve_size
    chunks = curve_size if curve_size <= 16 else 1
    rows_bf16 = jax.ShapeDtypeStruct((count, width), BF16)
    all_bf16 = jax.ShapeDtypeStruct((total, width), BF16)
    chunk_bf16 = jax.ShapeDtypeStruct((slots // chunks, width), BF16)

    x = points.reshape(count, width)
    others = [by_xor(x, "patch", m, "points") for m in range(1, patch_size)]
    gain_one = gain_one.reshape(1, width)
    gain_two = gain_two.reshape(1, width)

    def shape(kind, *dims):
        return jax.ShapeDtypeStruct(dims, kind)

    me = lax.axis_index("curve").astype(jnp.int32).reshape(1)
    slot, leaving_at = vmem_call(
        functools.partial(route_body, chunks, capacity),
        (shape(jnp.int32, 1, count), shape(jnp.int32 if chunks == 1 else F32, 1, slots)),
        name="route",
        flops=1 << 20,
        moved=1 << 12,
        in_specs=[SMEM_SPEC, VMEM_SPEC],
    )(me, hilbert_pos.reshape(1, count))
    x_then, slot, leaving_at = lax.optimization_barrier((x, slot, leaving_at))
    landing = leaving_at
    if chunks == 1:
        landing = lax.all_to_all(
            leaving_at.reshape(curve_size, 1, capacity),
            "curve",
            split_axis=0,
            concat_axis=0,
            tiled=True,
        ).reshape(1, slots)

    rows_f32 = shape(F32, count, width)
    lines_f32 = shape(F32, HEADS, count)
    square = shape(BF16, HEADS, count, count)
    dma = pltpu.SemaphoreType.DMA
    q, k, v, own_weights, sum_mixed, sums = vmem_call(
        functools.partial(prep_body, depth),
        (rows_bf16,) * 3 + (square,) + (rows_f32,) * 2,
        name="prep",
        flops=2 << 30,
        moved=4 << 20,
    )(x_then, gain_one, qkv_one)
    early_keys, early_values, early_weights = [k], [v], [own_weights]
    if peers > 1:
        k_next, v_next, weights_next, sum_mixed, sums = vmem_call(
            functools.partial(middle_body, depth),
            (rows_bf16,) * 2 + (square,) + (rows_f32,) * 2,
            name="middle",
            flops=2 << 30,
            moved=4 << 20,
        )(others[0], gain_one, qkv_one, q, sum_mixed, sums)
        early_keys.append(k_next)
        early_values.append(v_next)
        early_weights.append(weights_next)
    early = len(early_keys)
    late = peers + 1 - early
    late_bf16 = shape(BF16, late * count, width)
    embedded = shape(BF16, capacity * tiles + 8, LANES)
    sent = chunk_bf16 if chunks == 1 else embedded
    first_weights = 9 + 2 * early + late
    results = vmem_call(
        functools.partial(forward_body, early, peers, chunks, capacity, depth),
        (late_bf16, late_bf16, shape(BF16, HEADS, count, late * count))
        + (rows_bf16, rows_f32, lines_f32)
        + (square,) * early
        + (sent,) * chunks,
        [
            pltpu.VMEM((chunks,) + sent.shape, BF16),
            pltpu.VMEM((early,) + square.shape, BF16),
            dma((max(chunks, early),)),
        ],
        name="forward",
        flops=8 << 30,
        moved=8 << 20,
        in_specs=[VMEM_SPEC] * first_weights + [HBM_SPEC] * early,
        out_specs=(VMEM_SPEC,) * 6 + (HBM_SPEC,) * (early + chunks),
        input_output_aliases={first_weights + index: 6 + index for index in range(early)},
    )(
        x,
        gain_one,
        qkv_one,
        out_one,
        slot,
        leaving_at,
        q,
        sum_mixed,
        sums,
        *early_keys,
        *early_values,
        *others[early - 1 :],
        *early_weights,
    )
    late_keys, late_values, late_weights, mixed, inverse, lse = results[:6]
    all_weights = list(results[6 : 6 + early]) + [late_weights]
    all_keys, all_values = early_keys + [late_keys], early_values + [late_values]
    arrived = exchange(results[6 + early :], "curve", "out")
    lse_all = [lse] + [by_xor(lse, "patch", m, "lse") for m in range(1, patch_size)]

    queries_all = vmem_call(
        functools.partial(queries_body, peers),
        all_bf16,
        name="queries",
        flops=1 << 29,
        moved=3 << 20,
        in_specs=[VMEM_SPEC] * (3 + peers),
    )(gain_one, qkv_one, q, *others)
    flipped = vmem_call(
        functools.partial(weights_flipped_body, peers, depth),
        shape(BF16, HEADS, count, total),
        name="weights_flipped",
        flops=4 << 30,
        moved=10 << 20,
    )(k, queries_all, *lse_all)

    returning = vmem_call(
        functools.partial(second_body, chunks, depth),
        (chunk_bf16,) * chunks,
        [
            pltpu.VMEM((slots, width), BF16),
            pltpu.VMEM((count, 3 * width), BF16),
            pltpu.VMEM((count, 3 * width), BF16),
            pltpu.VMEM((count, width), BF16),
            pltpu.VMEM((count, count), F32),
            dma((chunks,)),
        ],
        name="second",
        flops=8 << 30,
        moved=4 << 20,
        in_specs=[VMEM_SPEC] * (6 + chunks),
        out_specs=(HBM_SPEC,) * chunks,
    )(
        landing,
        segments.reshape(1, count),
        gain_two,
        qkv_two,
        out_two,
        out_grad.reshape(count, width),
        *arrived,
    )
    home = exchange(returning, "curve", "back")

    grad_shape = shape(BF16, count + HEADS, width)
    moved_grad, grad_own, grad_send = vmem_call(
        functools.partial(home_body, chunks, depth),
        (rows_bf16, grad_shape, grad_shape),
        [dma(())],
        name="home",
        flops=1 << 29,
        moved=2 << 20,
        in_specs=[VMEM_SPEC] * (3 + chunks),
        out_specs=(VMEM_SPEC,) * 2 + (HBM_SPEC,),
    )(slot, mixed, out_one, *home)
    grads = [by_xor(grad_send, "patch", m, "grad") for m in range(1, patch_size)]

    query_grad, key_grad, value_grad = vmem_call(
        functools.partial(query_grad_body, len(all_keys), depth),
        (rows_bf16, rows_f32, rows_f32),
        [pltpu.VMEM((HEADS, count), F32), pltpu.VMEM((count, width), F32)],
        name="query_grad",
        flops=8 << 30,
        moved=10 << 20,
    )(*all_weights, *all_keys, *all_values, inverse, flipped, grad_own, q)
    for index in range(1, early):
        key_grad, value_grad = vmem_call(
            functools.partial(key_middle_body, index, depth),
            (rows_f32, rows_f32),
            [pltpu.VMEM((HEADS, count), F32)],
            name="key_middle",
            flops=2 << 30,
            moved=4 << 20,
        )(flipped, v, queries_all, key_grad, value_grad, grads[index - 1])
    result = vmem_call(
        functools.partial(key_grad_body, early, peers, depth),
        rows_bf16,
        [
            pltpu.VMEM((count, 3 * width), BF16),
            pltpu.VMEM((late * count, width), BF16),
            pltpu.VMEM((HEADS, late * count), F32),
        ],
        name="key_grad",
        flops=8 << 30,
        moved=14 << 20,
    )(
        flipped,
        v,
        queries_all,
        query_grad,
        key_grad,
        value_grad,
        x,
        gain_one,
        qkv_one,
        moved_grad,
        *grads[early - 1 :],
    )
    return result.reshape(points.shape)


def solution(mesh):
    in_specs = (
        P("curve", "patch", None, None),
        P(),
        P(),
        P(),
        P("curve", "patch", None),
        P(),
        P(),
        P(),
        P("patch", "curve", None),
        P("patch", "curve", None, None),
    )
    out_specs = P("curve", "patch", None, None)
    return jax.shard_map(shards, mesh=mesh, in_specs=in_specs, out_specs=out_specs, check_vma=False)
```

```python
import functools
import math

import jax
import jax.numpy as jnp
from jax import lax
from jax.experimental import pallas as pl
from jax.experimental.pallas import tpu as pltpu
from jax.sharding import PartitionSpec as P


HEADS = 16
EPS = 1e-06
LANES = 128
MASKED = -1e30
MOST_PERMUTES = 16
F32 = jnp.float32
BF16 = jnp.bfloat16
LOG2E = math.log2(math.e)


def dot_nn(left, right):
    return lax.dot_general(left, right, (((1,), (0,)), ((), ())), preferred_element_type=F32)


def dot_nt(left, right):
    return lax.dot_general(left, right, (((1,), (1,)), ((), ())), preferred_element_type=F32)


def dot_tn(left, right):
    return lax.dot_general(left, right, (((0,), (0,)), ((), ())), preferred_element_type=F32)


def norm_rows(rows, gain):
    wide = rows.astype(F32)
    power = jnp.mean(wide * wide, axis=-1, keepdims=True)
    return (wide * lax.rsqrt(power + EPS) * gain).astype(BF16)


def norm_pull(rows, gain, cotangent):
    wide = rows.astype(F32)
    power = jnp.mean(wide * wide, axis=-1, keepdims=True)
    inverse = lax.rsqrt(power + EPS)
    scaled = cotangent.astype(F32) * gain
    along = jnp.mean(scaled * wide, axis=-1, keepdims=True)
    return (inverse * scaled - wide * (inverse * inverse * inverse * along)).astype(BF16)


def head_mask(rows, index, depth):
    return lax.broadcasted_iota(jnp.int32, (rows, LANES), 1) // depth == index


def only(mask, tile):
    return jnp.where(mask, tile, jnp.zeros_like(tile))


def tile_at(t):
    return pl.ds(pl.multiple_of(t * LANES, LANES), LANES)


def vmem_call(body, outs, scratch=(), flops=0, moved=0, **more):
    params = pltpu.CompilerParams(vmem_limit_bytes=24 << 20, **more.pop("params", {}))
    return pl.pallas_call(
        body,
        out_shape=outs,
        scratch_shapes=scratch,
        compiler_params=params,
        cost_estimate=pl.CostEstimate(flops=flops, bytes_accessed=moved, transcendentals=0),
        **more,
    )


HBM_SPEC = pl.BlockSpec(memory_space=pltpu.MemorySpace.HBM)
SMEM_SPEC = pl.BlockSpec(memory_space=pltpu.MemorySpace.SMEM)
VMEM_SPEC = pl.BlockSpec(memory_space=pltpu.MemorySpace.VMEM)
LOW, HIGH = 2.0**-60, 2.0**100


def column(row):
    return jnp.transpose(jnp.broadcast_to(row.astype(F32), (LANES, row.shape[1])))[:, :1]


def start_all(pairs, sems):
    copies = [pltpu.make_async_copy(src, dst, sems.at[i]) for i, (src, dst) in enumerate(pairs)]
    for copy in copies:
        copy.start()
    return copies


def flip_tile(tile):
    return jnp.transpose(tile)


def with_ones(tile):
    return jnp.concatenate([tile, jnp.ones_like(tile)], axis=1)


def unshifted(depth, t, q_tile, k_tile, v_tile, weights_ref):
    count = q_tile.shape[0]
    scale = depth ** (-0.5) * LOG2E
    right = with_ones(v_tile)
    mixed = jnp.zeros((count, LANES), F32)
    sums = jnp.zeros((count, LANES), F32)
    for j in range(LANES // depth):
        mask = head_mask(count, j, depth)
        scores = dot_nt(only(mask, q_tile), k_tile)
        shifted = jnp.exp2(scores * scale).astype(BF16)
        weights_ref[t * (LANES // depth) + j] = shifted
        both = dot_nn(shifted, right)
        mixed = jnp.where(mask, both[:, :LANES], mixed)
        sums = jnp.where(mask, both[:, LANES:], sums)
    return mixed, sums


def route_body(chunks, capacity, me_ref, target_ref, slot_ref, at_ref):
    count = target_ref.shape[1]
    slots = 2 * count
    target = target_ref[...]
    shift = count.bit_length() - 1
    owner = lax.shift_right_logical(target, jnp.full_like(target, shift))
    offset = target - lax.shift_left(owner, jnp.full_like(target, shift))
    same = column(owner) == owner.astype(F32)
    earlier = lax.broadcasted_iota(jnp.int32, (count, count), 0) < (
        lax.broadcasted_iota(jnp.int32, (count, count), 1)
    )
    ranking = jnp.sum(jnp.where(same & earlier, 1.0, 0.0), axis=0, keepdims=True).astype(jnp.int32)
    lane = owner if chunks == 1 else lax.bitwise_xor(owner, jnp.full_like(owner, me_ref[0]))
    slot_ref[...] = lane * capacity + ranking
    hit = column(lane * capacity + ranking) == (
        lax.broadcasted_iota(jnp.int32, (count, slots), 1).astype(F32)
    )
    at = jnp.sum(jnp.where(hit, column(offset) - count, 0.0), axis=0, keepdims=True) + count
    at_ref[...] = at.astype(at_ref.dtype)


def prep_body(depth, *refs):
    x_ref, gain_ref, w_ref = refs[:3]
    q_ref, k_ref, v_ref, weights_ref, mixed_ref, sums_ref = refs[3:]
    width = x_ref.shape[1]
    normed = norm_rows(x_ref[...], gain_ref[...])
    q_ref[...] = dot_nn(normed, w_ref[:, :width]).astype(BF16)
    k_ref[...] = dot_nn(normed, w_ref[:, width : 2 * width]).astype(BF16)
    v_ref[...] = dot_nn(normed, w_ref[:, 2 * width :]).astype(BF16)

    def tile_step(t, carry):
        at = tile_at(t)
        mixed_ref[:, at], sums_ref[:, at] = unshifted(
            depth, t, q_ref[:, at], k_ref[:, at], v_ref[:, at], weights_ref
        )
        return carry

    lax.fori_loop(0, width // LANES, tile_step, 0)


def middle_body(depth, *refs):
    x_ref, gain_ref, w_ref, q_ref, mixed_in_ref, sums_in_ref = refs[:6]
    k_ref, v_ref, weights_ref, mixed_ref, sums_ref = refs[6:]
    width = x_ref.shape[1]
    normed = norm_rows(x_ref[...], gain_ref[...])
    k_ref[...] = dot_nn(normed, w_ref[:, width : 2 * width]).astype(BF16)
    v_ref[...] = dot_nn(normed, w_ref[:, 2 * width :]).astype(BF16)

    def tile_step(t, carry):
        at = tile_at(t)
        mixed, sums = unshifted(depth, t, q_ref[:, at], k_ref[:, at], v_ref[:, at], weights_ref)
        mixed_ref[:, at] = mixed + mixed_in_ref[:, at]
        sums_ref[:, at] = sums + sums_in_ref[:, at]
        return carry

    lax.fori_loop(0, width // LANES, tile_step, 0)


def forward_body(early, peers, chunks, capacity, depth, *refs):
    x_ref, gain_ref, w_ref, out_w_ref, slot_ref, at_ref, q_ref, mixed_in_ref, sums_in_ref = refs[:9]
    refs = refs[9:]
    early_keys, early_values, refs = refs[:early], refs[early : 2 * early], refs[2 * early :]
    others, refs = refs[: peers + 1 - early], refs[peers + 1 - early + early :]
    keys_ref, values_ref, weights_ref, mixed_ref, inverse_ref, lse_ref = refs[:6]
    early_weights, refs = refs[6 : 6 + early], refs[6 + early :]
    sends, (safe, out_sems) = refs[:chunks], refs[chunks:]
    count, width = x_ref.shape
    heads = LANES // depth
    for index, other in enumerate(others):
        rows = slice(index * count, (index + 1) * count)
        normed = norm_rows(other[...], gain_ref[...])
        keys_ref[rows] = dot_nn(normed, w_ref[:, width : 2 * width]).astype(BF16)
        values_ref[rows] = dot_nn(normed, w_ref[:, 2 * width :]).astype(BF16)

    def finish_tile(t, at, mixed, sums, tops):
        inverse = 1.0 / sums
        mixed_ref[:, at] = (mixed * inverse).astype(BF16)
        inverse_ref[:, at] = inverse
        flipped = flip_tile(tops + jnp.log(sums) * LOG2E)
        for j in range(heads):
            lse_ref[pl.ds(t * heads + j, 1)] = flipped[j * depth : j * depth + 1]

    def fast_step(t, bad):
        at = tile_at(t)
        mixed, sums = unshifted(
            depth, t, q_ref[:, at], keys_ref[:, at], values_ref[:, at], weights_ref
        )
        mixed += mixed_in_ref[:, at]
        sums += sums_in_ref[:, at]
        finish_tile(t, at, mixed, sums, 0.0)
        return jnp.where((sums >= LOW) & (sums <= HIGH), bad, 1.0)

    bad = lax.fori_loop(0, width // LANES, fast_step, jnp.zeros((count, LANES), F32))

    @pl.when(jnp.max(bad) > 0.0)
    def _():
        scale = depth ** (-0.5) * LOG2E

        def safe_step(t, carry):
            at = tile_at(t)
            keys = jnp.concatenate([ref[:, at] for ref in early_keys + (keys_ref,)], axis=0)
            values = jnp.concatenate([ref[:, at] for ref in early_values + (values_ref,)], axis=0)
            right = with_ones(values)
            mixed = jnp.zeros((count, LANES), F32)
            sums = jnp.ones((count, LANES), F32)
            tops = jnp.zeros((count, LANES), F32)
            for j in range(heads):
                mask = head_mask(count, j, depth)
                scores = dot_nt(only(mask, q_ref[:, at]), keys)
                top = jnp.max(scores, axis=-1, keepdims=True) * scale
                shifted = jnp.exp2(scores * scale - top).astype(BF16)
                weights_ref[t * heads + j] = shifted[:, early * count :]
                for index in range(early):
                    part = shifted[:, index * count : (index + 1) * count]
                    safe[index, t * heads + j] = part
                both = dot_nn(shifted, right)
                mixed = jnp.where(mask, both[:, :LANES], mixed)
                sums = jnp.where(mask, both[:, LANES:], sums)
                tops = jnp.where(mask, top, tops)
            finish_tile(t, at, mixed, sums, tops)
            return carry

        lax.fori_loop(0, width // LANES, safe_step, 0)
        pairs = [(safe.at[index], early_weights[index]) for index in range(early)]
        for copy in start_all(pairs, out_sems):
            copy.wait()

    moved = (x_ref[...].astype(F32) + dot_nn(mixed_ref[...], out_w_ref[...])).astype(BF16)
    slots = 2 * count
    picked = (lax.broadcasted_iota(jnp.int32, (slots, count), 0) == slot_ref[...]).astype(F32)
    leaving = dot_nn(picked.astype(BF16), moved).astype(BF16)
    if chunks == 1:
        sends[0][...] = leaving
    else:
        tail = sends[0].shape[0] - capacity * (width // LANES)
        line = jnp.broadcast_to(at_ref[...], (tail, slots)).astype(BF16)
        for m, send in enumerate(sends):
            part = slice(m * capacity, (m + 1) * capacity)
            for t in range(width // LANES):
                tile = leaving[part, t * LANES : (t + 1) * LANES]
                send[t * capacity : (t + 1) * capacity] = tile
            padding = jnp.zeros((tail, LANES - capacity), BF16)
            send[send.shape[0] - tail :] = jnp.concatenate([line[:, part], padding], axis=1)


def second_body(chunks, depth, *refs):
    land_ref, seg_ref, gain_ref, w_ref, out_w_ref, grad_ref = refs[:6]
    arrived = refs[6 : 6 + chunks]
    sends = refs[6 + chunks : 6 + 2 * chunks]
    packed, packed_grad, mixed_grad, bias = refs[6 + 2 * chunks :]
    count, width = grad_ref.shape
    slots = 2 * count
    size = slots // chunks
    mixed_grad[...] = dot_nt(grad_ref[...], out_w_ref[...]).astype(BF16)
    bias[...] = jnp.where(column(seg_ref[...]) == seg_ref[...].astype(F32), 0.0, MASKED)
    if chunks == 1:
        landing = land_ref[...].astype(F32)
        rows = arrived[0][...]
    else:
        ends = [piece[size * (width // LANES) :].astype(F32)[:1, :size] for piece in arrived]
        landing = jnp.concatenate(ends, axis=1)
        rows = []
        for piece in arrived:
            tiles = [piece[t * size : (t + 1) * size] for t in range(width // LANES)]
            rows.append(jnp.concatenate(tiles, axis=1))
        rows = jnp.concatenate(rows, axis=0)
    place = lax.broadcasted_iota(jnp.int32, (count, slots), 0).astype(F32) == landing
    place = place.astype(F32)
    hilbert = dot_nn(place.astype(BF16), rows).astype(BF16)
    normed = norm_rows(hilbert, gain_ref[...])
    packed[...] = dot_nn(normed, w_ref[...]).astype(BF16)
    scale = depth ** (-0.5)

    def tile_step(t, carry):
        at = tile_at(t)
        k_at = tile_at(t + width // LANES)
        v_at = tile_at(t + 2 * (width // LANES))
        q_tile = packed[:, at]
        k_tile = packed[:, k_at]
        v_tile = packed[:, v_at]
        g_tile = mixed_grad[:, at]
        k_flipped = flip_tile(k_tile)
        heads = LANES // depth
        masks = [head_mask(count, j, depth) for j in range(heads)]
        stacked = (heads, count, count)
        k_heads = jnp.concatenate([only(mask, k_tile) for mask in masks], axis=0)
        v_heads = jnp.concatenate([only(mask, v_tile) for mask in masks], axis=0)
        scores = dot_nt(k_heads, q_tile).reshape(stacked) * (scale * LOG2E) + bias[...][None]
        weight_grad = dot_nt(v_heads, g_tile).reshape(stacked)
        shifted = jnp.exp2(scores - jnp.max(scores, axis=1, keepdims=True))
        weights = shifted * (1.0 / jnp.sum(shifted, axis=1, keepdims=True))
        carried = jnp.sum(weights * weight_grad, axis=1, keepdims=True)
        score_grad = (weights * (weight_grad - carried)).astype(BF16)
        dk_heads = dot_nn(score_grad.reshape(heads * count, count), q_tile)
        dv_heads = dot_nn(weights.astype(BF16).reshape(heads * count, count), g_tile)
        dk, dv, dq = dk_heads[:count], dv_heads[:count], []
        for j in range(heads):
            part = slice(j * count, (j + 1) * count)
            dk = jnp.where(masks[j], dk_heads[part], dk)
            dv = jnp.where(masks[j], dv_heads[part], dv)
            dq.append(dot_nn(k_flipped[j * depth : (j + 1) * depth], score_grad[j]))
        dq = jnp.transpose(jnp.concatenate(dq, axis=0))
        packed_grad[:, at] = (dq * scale).astype(BF16)
        packed_grad[:, k_at] = (dk * scale).astype(BF16)
        packed_grad[:, v_at] = dv.astype(BF16)
        return carry

    lax.fori_loop(0, width // LANES, tile_step, 0)
    normed_grad = dot_nt(packed_grad[...], w_ref[...]).astype(BF16)
    total = grad_ref[...].astype(F32) + norm_pull(hilbert, gain_ref[...], normed_grad).astype(F32)
    back = lax.broadcasted_iota(jnp.int32, (slots, count), 1).astype(F32) == column(landing)
    returning = dot_nn(back.astype(F32).astype(BF16), total.astype(BF16)).astype(BF16)
    for m, send in enumerate(sends):
        send[...] = returning[m * size : (m + 1) * size]


def queries_body(peers, *refs):
    gain_ref, w_ref, q_ref = refs[:3]
    others = refs[3 : 3 + peers]
    out_ref = refs[3 + peers]
    count, width = q_ref.shape
    out_ref[:count] = q_ref[...]
    for index, other in enumerate(others):
        rows = slice((index + 1) * count, (index + 2) * count)
        normed = norm_rows(other[...], gain_ref[...])
        out_ref[rows] = dot_nn(normed, w_ref[:, :width]).astype(BF16)


def spread(rows, width):
    heads = rows.shape[0]
    pick = lax.broadcasted_iota(jnp.int32, (heads, width), 1) // (width // heads) == (
        lax.broadcasted_iota(jnp.int32, (heads, width), 0)
    )
    return dot_tn(rows, pick.astype(F32).astype(BF16))


def weights_flipped_body(peers, depth, *refs):
    k_ref, queries_ref = refs[:2]
    lse_refs = refs[2 : 3 + peers]
    out_ref = refs[3 + peers]
    scale = depth ** (-0.5) * LOG2E
    heads = LANES // depth
    count = k_ref.shape[0]

    def tile_step(t, carry):
        at = tile_at(t)
        for j in range(heads):
            mask = head_mask(count, j, depth)
            scores = dot_nt(only(mask, k_ref[:, at]), queries_ref[:, at])
            h = t * heads + j
            line = jnp.concatenate([ref[pl.ds(h, 1)] for ref in lse_refs], axis=1)
            out_ref[h] = jnp.exp2(scores * scale - line).astype(BF16)
        return carry

    lax.fori_loop(0, k_ref.shape[1] // LANES, tile_step, 0)


def home_body(chunks, depth, *refs):
    slot_ref, mixed_ref, out_w_ref = refs[:3]
    home = refs[3 : 3 + chunks]
    moved_ref, grad_ref = refs[3 + chunks :]
    count, width = moved_ref.shape
    slots = 2 * count
    take = lax.broadcasted_iota(jnp.int32, (count, slots), 1).astype(F32) == column(slot_ref[...])
    take = take.astype(F32).astype(BF16)
    moved = dot_nn(take, jnp.concatenate([piece[...] for piece in home], axis=0)).astype(BF16)
    moved_ref[...] = moved
    grad = dot_nt(moved, out_w_ref[...]).astype(BF16)
    grad_ref[:count] = grad
    product = grad.astype(F32) * mixed_ref[...].astype(F32)
    high = product.astype(BF16)
    low = (product - high.astype(F32)).astype(BF16)
    heads = width // depth
    pick = lax.broadcasted_iota(jnp.int32, (heads, width), 1) // depth == (
        lax.broadcasted_iota(jnp.int32, (heads, width), 0)
    )
    pick = pick.astype(F32).astype(BF16)
    rows = dot_nt(pick, high) + dot_nt(pick, low)
    rows_high = rows.astype(BF16)
    grad_ref[count:, :count] = rows_high
    grad_ref[count:, count:] = (rows - rows_high.astype(F32)).astype(BF16)


def key_tile(depth, t, v_tile, weights_ref, columns, queries, grads, deltas_ref):
    count = v_tile.shape[0]
    heads = LANES // depth
    dk = jnp.zeros((count, LANES), F32)
    dv = jnp.zeros((count, LANES), F32)
    for j in range(heads):
        h = t * heads + j
        mask = head_mask(count, j, depth)
        weights = weights_ref[h, :, columns]
        weight_grad = dot_nt(only(mask, v_tile), grads)
        delta = deltas_ref[pl.ds(h, 1)]
        score_grad = (weights.astype(F32) * (weight_grad - delta)).astype(BF16)
        dv = jnp.where(mask, dot_nn(weights, grads), dv)
        dk = jnp.where(mask, dot_nn(score_grad, queries), dk)
    return dk, dv


def halves(lines):
    half = lines.shape[1] // 2
    return lines[:, :half], lines[:, half:]


def query_grad_body(parts, depth, *refs):
    weights_refs, refs = refs[:parts], refs[parts:]
    keys_refs, refs = refs[:parts], refs[parts:]
    values_refs, refs = refs[:parts], refs[parts:]
    inverse_ref, flipped_ref, grad_ref, q_ref = refs[:4]
    out_ref, dk_ref, dv_ref, lines, wide = refs[4:]
    count, width = out_ref.shape
    heads = LANES // depth
    high, low = halves(grad_ref[count:])
    lines[...] = high.astype(F32) + low.astype(F32)
    wide[...] = spread(high, width) + spread(low, width)

    def tile_step(t, carry):
        at = tile_at(t)
        g_tile = grad_ref[:count, at]
        delta_tile = wide[:, at]
        keys = jnp.concatenate([ref[:, at] for ref in keys_refs], axis=0)
        values = jnp.concatenate([ref[:, at] for ref in values_refs], axis=0)
        dq = jnp.zeros((count, LANES), F32)
        for j in range(heads):
            mask = head_mask(count, j, depth)
            weight_grad = dot_nt(only(mask, g_tile), values)
            delta = delta_tile[:, j * depth : j * depth + 1]
            weights = jnp.concatenate([ref[t * heads + j] for ref in weights_refs], axis=1)
            score_grad = (weights.astype(F32) * (weight_grad - delta)).astype(BF16)
            dq = jnp.where(mask, dot_nn(score_grad, keys), dq)
        out_ref[:, at] = (dq * (inverse_ref[:, at] * depth ** (-0.5))).astype(BF16)
        dk_ref[:, at], dv_ref[:, at] = key_tile(
            depth,
            t,
            values_refs[0][:, at],
            flipped_ref,
            slice(0, count),
            q_ref[:, at],
            g_tile,
            lines,
        )
        return carry

    lax.fori_loop(0, width // LANES, tile_step, 0)


def key_middle_body(index, depth, *refs):
    flipped_ref, v_ref, queries_ref, dk_in_ref, dv_in_ref, grad_ref = refs[:6]
    dk_ref, dv_ref, lines = refs[6:]
    count, width = v_ref.shape
    high, low = halves(grad_ref[count:])
    lines[...] = high.astype(F32) + low.astype(F32)
    rows = slice(index * count, (index + 1) * count)

    def tile_step(t, carry):
        at = tile_at(t)
        dk, dv = key_tile(
            depth,
            t,
            v_ref[:, at],
            flipped_ref,
            rows,
            queries_ref[rows, at],
            grad_ref[:count, at],
            lines,
        )
        dk_ref[:, at] = dk + dk_in_ref[:, at]
        dv_ref[:, at] = dv + dv_in_ref[:, at]
        return carry

    lax.fori_loop(0, width // LANES, tile_step, 0)


def key_grad_body(early, peers, depth, *refs):
    flipped_ref, v_ref, queries_ref, dq_ref, dk_ref, dv_ref = refs[:6]
    x_ref, gain_ref, w_ref, moved_ref = refs[6:10]
    others = refs[10 : 11 + peers - early]
    out_ref, packed_grad, grads, lines = refs[11 + peers - early :]
    count, width = x_ref.shape
    packed_grad[:, :width] = dq_ref[...]
    for i, other in enumerate(others):
        rows = slice(i * count, (i + 1) * count)
        grads[rows] = other[:count]
        high, low = halves(other[count:])
        lines[:, rows] = high.astype(F32) + low.astype(F32)

    def tile_step(t, carry):
        at = tile_at(t)
        dk, dv = key_tile(
            depth,
            t,
            v_ref[:, at],
            flipped_ref,
            slice(early * count, (peers + 1) * count),
            queries_ref[early * count :, at],
            grads[:, at],
            lines,
        )
        dk = (dk + dk_ref[:, at]) * depth ** (-0.5)
        packed_grad[:, tile_at(t + width // LANES)] = dk.astype(BF16)
        packed_grad[:, tile_at(t + 2 * (width // LANES))] = (dv + dv_ref[:, at]).astype(BF16)
        return carry

    lax.fori_loop(0, width // LANES, tile_step, 0)
    normed_grad = dot_nt(packed_grad[...], w_ref[...]).astype(BF16)
    path = norm_pull(x_ref[...], gain_ref[...], normed_grad)
    out_ref[...] = (moved_ref[...].astype(F32) + path.astype(F32)).astype(BF16)


def single_first(size):
    return sorted(range(1, size), key=lambda step: (step.bit_count(), -step))


def by_xor(array, axis, step):
    size = lax.axis_size(axis)
    return lax.ppermute(array, axis, [(i, i ^ step) for i in range(size)])


def exchange(pieces, axis):
    if len(pieces) == 1:
        size = lax.axis_size(axis)
        stacked = pieces[0].reshape((size, -1) + pieces[0].shape[1:])
        got = lax.all_to_all(stacked, axis, split_axis=0, concat_axis=0, tiled=True)
        return [got.reshape(pieces[0].shape)]
    return [pieces[0]] + [by_xor(pieces[m], axis, m) for m in range(1, len(pieces))]


def shards(
    points, gain_one, qkv_one, out_one, hilbert_pos, gain_two, qkv_two, out_two, segments, out_grad
):
    count, width = points.shape[2:]
    depth = width // HEADS
    tiles = width // LANES
    patch_size = lax.axis_size("patch")
    curve_size = lax.axis_size("curve")
    peers = patch_size - 1
    total = patch_size * count
    slots = 2 * count
    capacity = slots // curve_size
    chunks = curve_size if curve_size <= MOST_PERMUTES else 1
    rows_bf16 = jax.ShapeDtypeStruct((count, width), BF16)
    all_bf16 = jax.ShapeDtypeStruct((total, width), BF16)
    chunk_bf16 = jax.ShapeDtypeStruct((slots // chunks, width), BF16)

    x = points.reshape(count, width)
    steps = single_first(patch_size)
    others = [by_xor(x, "patch", m) for m in steps]
    gain_one = gain_one.reshape(1, width)
    gain_two = gain_two.reshape(1, width)

    def shape(kind, *dims):
        return jax.ShapeDtypeStruct(dims, kind)

    me = lax.axis_index("curve").astype(jnp.int32).reshape(1)
    slot, leaving_at = vmem_call(
        functools.partial(route_body, chunks, capacity),
        (shape(jnp.int32, 1, count), shape(jnp.int32 if chunks == 1 else F32, 1, slots)),
        flops=1 << 20,
        moved=1 << 12,
        in_specs=[SMEM_SPEC, VMEM_SPEC],
    )(me, hilbert_pos.reshape(1, count))
    x_then, slot, leaving_at = lax.optimization_barrier((x, slot, leaving_at))
    landing = leaving_at
    if chunks == 1:
        landing = lax.all_to_all(
            leaving_at.reshape(curve_size, 1, capacity),
            "curve",
            split_axis=0,
            concat_axis=0,
            tiled=True,
        ).reshape(1, slots)

    rows_f32 = shape(F32, count, width)
    lines_f32 = shape(F32, HEADS, count)
    square = shape(BF16, HEADS, count, count)
    dma = pltpu.SemaphoreType.DMA
    q, k, v, own_weights, sum_mixed, sums = vmem_call(
        functools.partial(prep_body, depth),
        (rows_bf16,) * 3 + (square,) + (rows_f32,) * 2,
        flops=2 << 30,
        moved=4 << 20,
    )(x_then, gain_one, qkv_one)
    early_keys, early_values, early_weights = [k], [v], [own_weights]
    if peers > 1:
        k_next, v_next, weights_next, sum_mixed, sums = vmem_call(
            functools.partial(middle_body, depth),
            (rows_bf16,) * 2 + (square,) + (rows_f32,) * 2,
            flops=2 << 30,
            moved=4 << 20,
        )(others[0], gain_one, qkv_one, q, sum_mixed, sums)
        early_keys.append(k_next)
        early_values.append(v_next)
        early_weights.append(weights_next)
    early = len(early_keys)
    late = peers + 1 - early
    late_bf16 = shape(BF16, late * count, width)
    embedded = shape(BF16, capacity * tiles + 8, LANES)
    sent = chunk_bf16 if chunks == 1 else embedded
    first_weights = 9 + 2 * early + late
    results = vmem_call(
        functools.partial(forward_body, early, peers, chunks, capacity, depth),
        (late_bf16, late_bf16, shape(BF16, HEADS, count, late * count))
        + (rows_bf16, rows_f32, lines_f32)
        + (square,) * early
        + (sent,) * chunks,
        [
            pltpu.VMEM((early,) + square.shape, BF16),
            dma((early,)),
        ],
        flops=8 << 30,
        moved=8 << 20,
        in_specs=[VMEM_SPEC] * first_weights + [HBM_SPEC] * early,
        out_specs=(VMEM_SPEC,) * 6 + (HBM_SPEC,) * early + (VMEM_SPEC,) * chunks,
        input_output_aliases={first_weights + index: 6 + index for index in range(early)},
    )(
        x,
        gain_one,
        qkv_one,
        out_one,
        slot,
        leaving_at,
        q,
        sum_mixed,
        sums,
        *early_keys,
        *early_values,
        *others[early - 1 :],
        *early_weights,
    )
    late_keys, late_values, late_weights, mixed, inverse, lse = results[:6]
    all_weights = list(results[6 : 6 + early]) + [late_weights]
    all_keys, all_values = early_keys + [late_keys], early_values + [late_values]
    arrived = exchange(results[6 + early :], "curve")
    lse_all = [lse] + [by_xor(lse, "patch", m) for m in steps]

    queries_all = vmem_call(
        functools.partial(queries_body, peers),
        all_bf16,
        flops=1 << 29,
        moved=3 << 20,
        in_specs=[VMEM_SPEC] * (3 + peers),
    )(gain_one, qkv_one, q, *others)
    flipped = vmem_call(
        functools.partial(weights_flipped_body, peers, depth),
        shape(BF16, HEADS, count, total),
        flops=4 << 30,
        moved=10 << 20,
    )(k, queries_all, *lse_all)

    returning = vmem_call(
        functools.partial(second_body, chunks, depth),
        (chunk_bf16,) * chunks,
        [
            pltpu.VMEM((count, 3 * width), BF16),
            pltpu.VMEM((count, 3 * width), BF16),
            pltpu.VMEM((count, width), BF16),
            pltpu.VMEM((count, count), F32),
        ],
        flops=8 << 30,
        moved=4 << 20,
    )(
        landing,
        segments.reshape(1, count),
        gain_two,
        qkv_two,
        out_two,
        out_grad.reshape(count, width),
        *arrived,
    )
    home = exchange(returning, "curve")

    moved_grad, grad_own = vmem_call(
        functools.partial(home_body, chunks, depth),
        (rows_bf16, shape(BF16, count + HEADS, width)),
        flops=1 << 29,
        moved=2 << 20,
    )(slot, mixed, out_one, *home)
    grads = [by_xor(grad_own, "patch", m) for m in steps]

    query_grad, key_grad, value_grad = vmem_call(
        functools.partial(query_grad_body, len(all_keys), depth),
        (rows_bf16, rows_f32, rows_f32),
        [pltpu.VMEM((HEADS, count), F32), pltpu.VMEM((count, width), F32)],
        flops=8 << 30,
        moved=10 << 20,
    )(*all_weights, *all_keys, *all_values, inverse, flipped, grad_own, q)
    for index in range(1, early):
        key_grad, value_grad = vmem_call(
            functools.partial(key_middle_body, index, depth),
            (rows_f32, rows_f32),
            [pltpu.VMEM((HEADS, count), F32)],
            flops=2 << 30,
            moved=4 << 20,
        )(flipped, v, queries_all, key_grad, value_grad, grads[index - 1])
    result = vmem_call(
        functools.partial(key_grad_body, early, peers, depth),
        rows_bf16,
        [
            pltpu.VMEM((count, 3 * width), BF16),
            pltpu.VMEM((late * count, width), BF16),
            pltpu.VMEM((HEADS, late * count), F32),
        ],
        flops=8 << 30,
        moved=14 << 20,
    )(
        flipped,
        v,
        queries_all,
        query_grad,
        key_grad,
        value_grad,
        x,
        gain_one,
        qkv_one,
        moved_grad,
        *grads[early - 1 :],
    )
    return result.reshape(points.shape)


def solution(mesh):
    in_specs = (
        P("curve", "patch", None, None),
        P(),
        P(),
        P(),
        P("curve", "patch", None),
        P(),
        P(),
        P(),
        P("patch", "curve", None),
        P("patch", "curve", None, None),
    )
    out_specs = P("curve", "patch", None, None)

    return jax.shard_map(shards, mesh=mesh, in_specs=in_specs, out_specs=out_specs, check_vma=False)
```

```python
import functools
import math

import jax
import jax.numpy as jnp
from jax import lax
from jax.experimental import pallas as pl
from jax.experimental.pallas import tpu as pltpu
from jax.sharding import PartitionSpec as P


HEADS = 16
EPS = 1e-06
LANES = 128
MASKED = -1e30
MOST_PERMUTES = 16
F32 = jnp.float32
BF16 = jnp.bfloat16
LOG2E = math.log2(math.e)


def dot_nn(left, right):
    return lax.dot_general(left, right, (((1,), (0,)), ((), ())), preferred_element_type=F32)


def dot_nt(left, right):
    return lax.dot_general(left, right, (((1,), (1,)), ((), ())), preferred_element_type=F32)


def dot_tn(left, right):
    return lax.dot_general(left, right, (((0,), (0,)), ((), ())), preferred_element_type=F32)


def norm_rows(rows, gain):
    wide = rows.astype(F32)
    power = jnp.mean(wide * wide, axis=-1, keepdims=True)
    return (wide * lax.rsqrt(power + EPS) * gain).astype(BF16)


def norm_pull(rows, gain, cotangent):
    wide = rows.astype(F32)
    power = jnp.mean(wide * wide, axis=-1, keepdims=True)
    inverse = lax.rsqrt(power + EPS)
    scaled = cotangent.astype(F32) * gain
    along = jnp.mean(scaled * wide, axis=-1, keepdims=True)
    return (inverse * scaled - wide * (inverse * inverse * inverse * along)).astype(BF16)


def head_mask(rows, index, depth):
    return lax.broadcasted_iota(jnp.int32, (rows, LANES), 1) // depth == index


def only(mask, tile):
    return jnp.where(mask, tile, jnp.zeros_like(tile))


def tile_at(t):
    if isinstance(t, int):
        return slice(t * LANES, (t + 1) * LANES)
    return pl.ds(pl.multiple_of(t * LANES, LANES), LANES)


def tile_loop(tiles, step, carry):
    for t in range(tiles):
        carry = step(t, carry)
    return carry


def vmem_call(body, outs, scratch=(), flops=0, moved=0, **more):
    params = pltpu.CompilerParams(vmem_limit_bytes=24 << 20, **more.pop("params", {}))
    return pl.pallas_call(
        body,
        out_shape=outs,
        scratch_shapes=scratch,
        compiler_params=params,
        cost_estimate=pl.CostEstimate(flops=flops, bytes_accessed=moved, transcendentals=0),
        **more,
    )


HBM_SPEC = pl.BlockSpec(memory_space=pltpu.MemorySpace.HBM)
SMEM_SPEC = pl.BlockSpec(memory_space=pltpu.MemorySpace.SMEM)
VMEM_SPEC = pl.BlockSpec(memory_space=pltpu.MemorySpace.VMEM)
LOW, HIGH = 2.0**-60, 2.0**100


def column(row):
    return jnp.transpose(jnp.broadcast_to(row.astype(F32), (LANES, row.shape[1])))[:, :1]


def start_all(pairs, sems):
    copies = [pltpu.make_async_copy(src, dst, sems.at[i]) for i, (src, dst) in enumerate(pairs)]
    for copy in copies:
        copy.start()
    return copies


def flip_tile(tile):
    return jnp.transpose(tile)


def with_ones(tile):
    return jnp.concatenate([tile, jnp.ones_like(tile)], axis=1)


def unshifted(depth, t, q_tile, k_tile, v_tile, weights_ref):
    count = q_tile.shape[0]
    scale = depth ** (-0.5) * LOG2E
    right = with_ones(v_tile)
    mixed = jnp.zeros((count, LANES), F32)
    sums = jnp.zeros((count, LANES), F32)
    for j in range(LANES // depth):
        mask = head_mask(count, j, depth)
        scores = dot_nt(only(mask, q_tile), k_tile)
        shifted = jnp.exp2(scores * scale).astype(BF16)
        weights_ref[t * (LANES // depth) + j] = shifted
        both = dot_nn(shifted, right)
        mixed = jnp.where(mask, both[:, :LANES], mixed)
        sums = jnp.where(mask, both[:, LANES:], sums)
    return mixed, sums


def route_body(chunks, capacity, me_ref, target_ref, slot_ref, at_ref):
    count = target_ref.shape[1]
    slots = 2 * count
    target = target_ref[...]
    shift = count.bit_length() - 1
    owner = lax.shift_right_logical(target, jnp.full_like(target, shift))
    offset = target - lax.shift_left(owner, jnp.full_like(target, shift))
    same = column(owner) == owner.astype(F32)
    earlier = lax.broadcasted_iota(jnp.int32, (count, count), 0) < (
        lax.broadcasted_iota(jnp.int32, (count, count), 1)
    )
    ranking = jnp.sum(jnp.where(same & earlier, 1.0, 0.0), axis=0, keepdims=True).astype(jnp.int32)
    lane = owner if chunks == 1 else lax.bitwise_xor(owner, jnp.full_like(owner, me_ref[0]))
    slot_ref[...] = lane * capacity + ranking
    hit = column(lane * capacity + ranking) == (
        lax.broadcasted_iota(jnp.int32, (count, slots), 1).astype(F32)
    )
    at = jnp.sum(jnp.where(hit, column(offset) - count, 0.0), axis=0, keepdims=True) + count
    at_ref[...] = at.astype(at_ref.dtype)


def prep_body(depth, *refs):
    x_ref, gain_ref, w_ref = refs[:3]
    q_ref, k_ref, v_ref, weights_ref, mixed_ref, sums_ref = refs[3:]
    width = x_ref.shape[1]
    normed = norm_rows(x_ref[...], gain_ref[...])
    q_ref[...] = dot_nn(normed, w_ref[:, :width]).astype(BF16)
    k_ref[...] = dot_nn(normed, w_ref[:, width : 2 * width]).astype(BF16)
    v_ref[...] = dot_nn(normed, w_ref[:, 2 * width :]).astype(BF16)

    def tile_step(t, carry):
        at = tile_at(t)
        mixed_ref[:, at], sums_ref[:, at] = unshifted(
            depth, t, q_ref[:, at], k_ref[:, at], v_ref[:, at], weights_ref
        )
        return carry

    tile_loop(width // LANES, tile_step, 0)


def middle_body(depth, *refs):
    x_ref, gain_ref, w_ref, q_ref, mixed_in_ref, sums_in_ref = refs[:6]
    k_ref, v_ref, weights_ref, mixed_ref, sums_ref = refs[6:]
    width = x_ref.shape[1]
    normed = norm_rows(x_ref[...], gain_ref[...])
    k_ref[...] = dot_nn(normed, w_ref[:, width : 2 * width]).astype(BF16)
    v_ref[...] = dot_nn(normed, w_ref[:, 2 * width :]).astype(BF16)

    def tile_step(t, carry):
        at = tile_at(t)
        mixed, sums = unshifted(depth, t, q_ref[:, at], k_ref[:, at], v_ref[:, at], weights_ref)
        mixed_ref[:, at] = mixed + mixed_in_ref[:, at]
        sums_ref[:, at] = sums + sums_in_ref[:, at]
        return carry

    tile_loop(width // LANES, tile_step, 0)


def forward_body(early, peers, chunks, capacity, depth, *refs):
    x_ref, gain_ref, w_ref, out_w_ref, slot_ref, at_ref, q_ref, mixed_in_ref, sums_in_ref = refs[:9]
    refs = refs[9:]
    early_keys, early_values, refs = refs[:early], refs[early : 2 * early], refs[2 * early :]
    others, refs = refs[: peers + 1 - early], refs[peers + 1 - early + early :]
    keys_ref, values_ref, weights_ref, mixed_ref, inverse_ref, lse_ref = refs[:6]
    early_weights, refs = refs[6 : 6 + early], refs[6 + early :]
    sends, (safe, out_sems) = refs[:chunks], refs[chunks:]
    count, width = x_ref.shape
    heads = LANES // depth
    for index, other in enumerate(others):
        rows = slice(index * count, (index + 1) * count)
        normed = norm_rows(other[...], gain_ref[...])
        keys_ref[rows] = dot_nn(normed, w_ref[:, width : 2 * width]).astype(BF16)
        values_ref[rows] = dot_nn(normed, w_ref[:, 2 * width :]).astype(BF16)

    def finish_tile(t, at, mixed, sums, tops):
        inverse = 1.0 / sums
        mixed_ref[:, at] = (mixed * inverse).astype(BF16)
        inverse_ref[:, at] = inverse
        flipped = flip_tile(tops + jnp.log(sums) * LOG2E)
        for j in range(heads):
            lse_ref[pl.ds(t * heads + j, 1)] = flipped[j * depth : j * depth + 1]

    def fast_step(t, bad):
        at = tile_at(t)
        mixed, sums = unshifted(
            depth, t, q_ref[:, at], keys_ref[:, at], values_ref[:, at], weights_ref
        )
        mixed += mixed_in_ref[:, at]
        sums += sums_in_ref[:, at]
        finish_tile(t, at, mixed, sums, 0.0)
        return jnp.where((sums >= LOW) & (sums <= HIGH), bad, 1.0)

    bad = tile_loop(width // LANES, fast_step, jnp.zeros((count, LANES), F32))

    @pl.when(jnp.max(bad) > 0.0)
    def _():
        scale = depth ** (-0.5) * LOG2E

        def safe_step(t, carry):
            at = tile_at(t)
            keys = jnp.concatenate([ref[:, at] for ref in early_keys + (keys_ref,)], axis=0)
            values = jnp.concatenate([ref[:, at] for ref in early_values + (values_ref,)], axis=0)
            right = with_ones(values)
            mixed = jnp.zeros((count, LANES), F32)
            sums = jnp.ones((count, LANES), F32)
            tops = jnp.zeros((count, LANES), F32)
            for j in range(heads):
                mask = head_mask(count, j, depth)
                scores = dot_nt(only(mask, q_ref[:, at]), keys)
                top = jnp.max(scores, axis=-1, keepdims=True) * scale
                shifted = jnp.exp2(scores * scale - top).astype(BF16)
                weights_ref[t * heads + j] = shifted[:, early * count :]
                for index in range(early):
                    part = shifted[:, index * count : (index + 1) * count]
                    safe[index, t * heads + j] = part
                both = dot_nn(shifted, right)
                mixed = jnp.where(mask, both[:, :LANES], mixed)
                sums = jnp.where(mask, both[:, LANES:], sums)
                tops = jnp.where(mask, top, tops)
            finish_tile(t, at, mixed, sums, tops)
            return carry

        lax.fori_loop(0, width // LANES, safe_step, 0)
        pairs = [(safe.at[index], early_weights[index]) for index in range(early)]
        for copy in start_all(pairs, out_sems):
            copy.wait()

    moved = (x_ref[...].astype(F32) + dot_nn(mixed_ref[...], out_w_ref[...])).astype(BF16)
    slots = 2 * count
    picked = (lax.broadcasted_iota(jnp.int32, (slots, count), 0) == slot_ref[...]).astype(F32)
    leaving = dot_nn(picked.astype(BF16), moved).astype(BF16)
    if chunks == 1:
        sends[0][...] = leaving
    else:
        tail = sends[0].shape[0] - capacity * (width // LANES)
        line = jnp.broadcast_to(at_ref[...], (tail, slots)).astype(BF16)
        for m, send in enumerate(sends):
            part = slice(m * capacity, (m + 1) * capacity)
            for t in range(width // LANES):
                tile = leaving[part, t * LANES : (t + 1) * LANES]
                send[t * capacity : (t + 1) * capacity] = tile
            padding = jnp.zeros((tail, LANES - capacity), BF16)
            send[send.shape[0] - tail :] = jnp.concatenate([line[:, part], padding], axis=1)


def second_body(chunks, depth, *refs):
    land_ref, seg_ref, gain_ref, w_ref, out_w_ref, grad_ref = refs[:6]
    arrived = refs[6 : 6 + chunks]
    sends = refs[6 + chunks : 6 + 2 * chunks]
    packed, packed_grad, mixed_grad, bias = refs[6 + 2 * chunks :]
    count, width = grad_ref.shape
    slots = 2 * count
    size = slots // chunks
    mixed_grad[...] = dot_nt(grad_ref[...], out_w_ref[...]).astype(BF16)
    bias[...] = jnp.where(column(seg_ref[...]) == seg_ref[...].astype(F32), 0.0, MASKED)
    if chunks == 1:
        landing = land_ref[...].astype(F32)
        rows = arrived[0][...]
    else:
        ends = [piece[size * (width // LANES) :].astype(F32)[:1, :size] for piece in arrived]
        landing = jnp.concatenate(ends, axis=1)
        rows = []
        for piece in arrived:
            tiles = [piece[t * size : (t + 1) * size] for t in range(width // LANES)]
            rows.append(jnp.concatenate(tiles, axis=1))
        rows = jnp.concatenate(rows, axis=0)
    place = lax.broadcasted_iota(jnp.int32, (count, slots), 0).astype(F32) == landing
    place = place.astype(F32)
    hilbert = dot_nn(place.astype(BF16), rows).astype(BF16)
    normed = norm_rows(hilbert, gain_ref[...])
    packed[...] = dot_nn(normed, w_ref[...]).astype(BF16)
    scale = depth ** (-0.5)

    def tile_step(t, carry):
        at = tile_at(t)
        k_at = tile_at(t + width // LANES)
        v_at = tile_at(t + 2 * (width // LANES))
        q_tile = packed[:, at]
        k_tile = packed[:, k_at]
        v_tile = packed[:, v_at]
        g_tile = mixed_grad[:, at]
        k_flipped = flip_tile(k_tile)
        heads = LANES // depth
        masks = [head_mask(count, j, depth) for j in range(heads)]
        stacked = (heads, count, count)
        k_heads = jnp.concatenate([only(mask, k_tile) for mask in masks], axis=0)
        v_heads = jnp.concatenate([only(mask, v_tile) for mask in masks], axis=0)
        scores = dot_nt(k_heads, q_tile).reshape(stacked) * (scale * LOG2E) + bias[...][None]
        weight_grad = dot_nt(v_heads, g_tile).reshape(stacked)
        shifted = jnp.exp2(scores - jnp.max(scores, axis=1, keepdims=True))
        weights = shifted * (1.0 / jnp.sum(shifted, axis=1, keepdims=True))
        carried = jnp.sum(weights * weight_grad, axis=1, keepdims=True)
        score_grad = (weights * (weight_grad - carried)).astype(BF16)
        dk_heads = dot_nn(score_grad.reshape(heads * count, count), q_tile)
        dv_heads = dot_nn(weights.astype(BF16).reshape(heads * count, count), g_tile)
        dk, dv, dq = dk_heads[:count], dv_heads[:count], []
        for j in range(heads):
            part = slice(j * count, (j + 1) * count)
            dk = jnp.where(masks[j], dk_heads[part], dk)
            dv = jnp.where(masks[j], dv_heads[part], dv)
            dq.append(dot_nn(k_flipped[j * depth : (j + 1) * depth], score_grad[j]))
        dq = jnp.transpose(jnp.concatenate(dq, axis=0))
        packed_grad[:, at] = (dq * scale).astype(BF16)
        packed_grad[:, k_at] = (dk * scale).astype(BF16)
        packed_grad[:, v_at] = dv.astype(BF16)
        return carry

    tile_loop(width // LANES, tile_step, 0)
    normed_grad = dot_nt(packed_grad[...], w_ref[...]).astype(BF16)
    total = grad_ref[...].astype(F32) + norm_pull(hilbert, gain_ref[...], normed_grad).astype(F32)
    back = lax.broadcasted_iota(jnp.int32, (slots, count), 1).astype(F32) == column(landing)
    returning = dot_nn(back.astype(F32).astype(BF16), total.astype(BF16)).astype(BF16)
    for m, send in enumerate(sends):
        send[...] = returning[m * size : (m + 1) * size]


def queries_body(peers, *refs):
    gain_ref, w_ref, q_ref = refs[:3]
    others = refs[3 : 3 + peers]
    out_ref = refs[3 + peers]
    count, width = q_ref.shape
    out_ref[:count] = q_ref[...]
    for index, other in enumerate(others):
        rows = slice((index + 1) * count, (index + 2) * count)
        normed = norm_rows(other[...], gain_ref[...])
        out_ref[rows] = dot_nn(normed, w_ref[:, :width]).astype(BF16)


def spread(rows, width):
    heads = rows.shape[0]
    pick = lax.broadcasted_iota(jnp.int32, (heads, width), 1) // (width // heads) == (
        lax.broadcasted_iota(jnp.int32, (heads, width), 0)
    )
    return dot_tn(rows, pick.astype(F32).astype(BF16))


def weights_flipped_body(peers, depth, *refs):
    k_ref, queries_ref = refs[:2]
    lse_refs = refs[2 : 3 + peers]
    out_ref = refs[3 + peers]
    scale = depth ** (-0.5) * LOG2E
    heads = LANES // depth
    count = k_ref.shape[0]

    def tile_step(t, carry):
        at = tile_at(t)
        for j in range(heads):
            mask = head_mask(count, j, depth)
            scores = dot_nt(only(mask, k_ref[:, at]), queries_ref[:, at])
            h = t * heads + j
            line = jnp.concatenate([ref[pl.ds(h, 1)] for ref in lse_refs], axis=1)
            out_ref[h] = jnp.exp2(scores * scale - line).astype(BF16)
        return carry

    tile_loop(k_ref.shape[1] // LANES, tile_step, 0)


def home_body(chunks, depth, *refs):
    slot_ref, mixed_ref, out_w_ref = refs[:3]
    home = refs[3 : 3 + chunks]
    moved_ref, grad_ref = refs[3 + chunks :]
    count, width = moved_ref.shape
    slots = 2 * count
    take = lax.broadcasted_iota(jnp.int32, (count, slots), 1).astype(F32) == column(slot_ref[...])
    take = take.astype(F32).astype(BF16)
    moved = dot_nn(take, jnp.concatenate([piece[...] for piece in home], axis=0)).astype(BF16)
    moved_ref[...] = moved
    grad = dot_nt(moved, out_w_ref[...]).astype(BF16)
    grad_ref[:count] = grad
    product = grad.astype(F32) * mixed_ref[...].astype(F32)
    high = product.astype(BF16)
    low = (product - high.astype(F32)).astype(BF16)
    heads = width // depth
    pick = lax.broadcasted_iota(jnp.int32, (heads, width), 1) // depth == (
        lax.broadcasted_iota(jnp.int32, (heads, width), 0)
    )
    pick = pick.astype(F32).astype(BF16)
    rows = dot_nt(pick, high) + dot_nt(pick, low)
    rows_high = rows.astype(BF16)
    grad_ref[count:, :count] = rows_high
    grad_ref[count:, count:] = (rows - rows_high.astype(F32)).astype(BF16)


def key_tile(depth, t, v_tile, weights_ref, columns, queries, grads, deltas_ref):
    count = v_tile.shape[0]
    heads = LANES // depth
    dk = jnp.zeros((count, LANES), F32)
    dv = jnp.zeros((count, LANES), F32)
    for j in range(heads):
        h = t * heads + j
        mask = head_mask(count, j, depth)
        weights = weights_ref[h, :, columns]
        weight_grad = dot_nt(only(mask, v_tile), grads)
        delta = deltas_ref[pl.ds(h, 1)]
        score_grad = (weights.astype(F32) * (weight_grad - delta)).astype(BF16)
        dv = jnp.where(mask, dot_nn(weights, grads), dv)
        dk = jnp.where(mask, dot_nn(score_grad, queries), dk)
    return dk, dv


def halves(lines):
    half = lines.shape[1] // 2
    return lines[:, :half], lines[:, half:]


def query_grad_body(parts, depth, *refs):
    weights_refs, refs = refs[:parts], refs[parts:]
    keys_refs, refs = refs[:parts], refs[parts:]
    values_refs, refs = refs[:parts], refs[parts:]
    inverse_ref, flipped_ref, grad_ref, q_ref = refs[:4]
    out_ref, dk_ref, dv_ref, lines, wide = refs[4:]
    count, width = out_ref.shape
    heads = LANES // depth
    high, low = halves(grad_ref[count:])
    lines[...] = high.astype(F32) + low.astype(F32)
    wide[...] = spread(high, width) + spread(low, width)

    def tile_step(t, carry):
        at = tile_at(t)
        g_tile = grad_ref[:count, at]
        delta_tile = wide[:, at]
        keys = jnp.concatenate([ref[:, at] for ref in keys_refs], axis=0)
        values = jnp.concatenate([ref[:, at] for ref in values_refs], axis=0)
        dq = jnp.zeros((count, LANES), F32)
        for j in range(heads):
            mask = head_mask(count, j, depth)
            weight_grad = dot_nt(only(mask, g_tile), values)
            delta = delta_tile[:, j * depth : j * depth + 1]
            weights = jnp.concatenate([ref[t * heads + j] for ref in weights_refs], axis=1)
            score_grad = (weights.astype(F32) * (weight_grad - delta)).astype(BF16)
            dq = jnp.where(mask, dot_nn(score_grad, keys), dq)
        out_ref[:, at] = (dq * (inverse_ref[:, at] * depth ** (-0.5))).astype(BF16)
        dk_ref[:, at], dv_ref[:, at] = key_tile(
            depth,
            t,
            values_refs[0][:, at],
            flipped_ref,
            slice(0, count),
            q_ref[:, at],
            g_tile,
            lines,
        )
        return carry

    tile_loop(width // LANES, tile_step, 0)


def key_middle_body(index, depth, *refs):
    flipped_ref, v_ref, queries_ref, dk_in_ref, dv_in_ref, grad_ref = refs[:6]
    dk_ref, dv_ref, lines = refs[6:]
    count, width = v_ref.shape
    high, low = halves(grad_ref[count:])
    lines[...] = high.astype(F32) + low.astype(F32)
    rows = slice(index * count, (index + 1) * count)

    def tile_step(t, carry):
        at = tile_at(t)
        dk, dv = key_tile(
            depth,
            t,
            v_ref[:, at],
            flipped_ref,
            rows,
            queries_ref[rows, at],
            grad_ref[:count, at],
            lines,
        )
        dk_ref[:, at] = dk + dk_in_ref[:, at]
        dv_ref[:, at] = dv + dv_in_ref[:, at]
        return carry

    tile_loop(width // LANES, tile_step, 0)


def key_grad_body(early, peers, depth, *refs):
    flipped_ref, v_ref, queries_ref, dq_ref, dk_ref, dv_ref = refs[:6]
    x_ref, gain_ref, w_ref, moved_ref = refs[6:10]
    others = refs[10 : 11 + peers - early]
    out_ref, packed_grad, grads, lines = refs[11 + peers - early :]
    count, width = x_ref.shape
    packed_grad[:, :width] = dq_ref[...]
    for i, other in enumerate(others):
        rows = slice(i * count, (i + 1) * count)
        grads[rows] = other[:count]
        high, low = halves(other[count:])
        lines[:, rows] = high.astype(F32) + low.astype(F32)

    def tile_step(t, carry):
        at = tile_at(t)
        dk, dv = key_tile(
            depth,
            t,
            v_ref[:, at],
            flipped_ref,
            slice(early * count, (peers + 1) * count),
            queries_ref[early * count :, at],
            grads[:, at],
            lines,
        )
        dk = (dk + dk_ref[:, at]) * depth ** (-0.5)
        packed_grad[:, tile_at(t + width // LANES)] = dk.astype(BF16)
        packed_grad[:, tile_at(t + 2 * (width // LANES))] = (dv + dv_ref[:, at]).astype(BF16)
        return carry

    tile_loop(width // LANES, tile_step, 0)
    normed_grad = dot_nt(packed_grad[...], w_ref[...]).astype(BF16)
    path = norm_pull(x_ref[...], gain_ref[...], normed_grad)
    out_ref[...] = (moved_ref[...].astype(F32) + path.astype(F32)).astype(BF16)


def single_first(size):
    return sorted(range(1, size), key=lambda step: (step.bit_count(), -step))


def by_xor(array, axis, step):
    size = lax.axis_size(axis)
    return lax.ppermute(array, axis, [(i, i ^ step) for i in range(size)])


def exchange(pieces, axis):
    if len(pieces) == 1:
        size = lax.axis_size(axis)
        stacked = pieces[0].reshape((size, -1) + pieces[0].shape[1:])
        got = lax.all_to_all(stacked, axis, split_axis=0, concat_axis=0, tiled=True)
        return [got.reshape(pieces[0].shape)]
    return [pieces[0]] + [by_xor(pieces[m], axis, m) for m in range(1, len(pieces))]


def shards(
    points, gain_one, qkv_one, out_one, hilbert_pos, gain_two, qkv_two, out_two, segments, out_grad
):
    count, width = points.shape[2:]
    depth = width // HEADS
    tiles = width // LANES
    patch_size = lax.axis_size("patch")
    curve_size = lax.axis_size("curve")
    peers = patch_size - 1
    total = patch_size * count
    slots = 2 * count
    capacity = slots // curve_size
    chunks = curve_size if curve_size <= MOST_PERMUTES else 1
    rows_bf16 = jax.ShapeDtypeStruct((count, width), BF16)
    all_bf16 = jax.ShapeDtypeStruct((total, width), BF16)
    chunk_bf16 = jax.ShapeDtypeStruct((slots // chunks, width), BF16)

    x = points.reshape(count, width)
    steps = single_first(patch_size)
    others = [by_xor(x, "patch", m) for m in steps]
    gain_one = gain_one.reshape(1, width)
    gain_two = gain_two.reshape(1, width)

    def shape(kind, *dims):
        return jax.ShapeDtypeStruct(dims, kind)

    me = lax.axis_index("curve").astype(jnp.int32).reshape(1)
    slot, leaving_at = vmem_call(
        functools.partial(route_body, chunks, capacity),
        (shape(jnp.int32, 1, count), shape(jnp.int32 if chunks == 1 else F32, 1, slots)),
        flops=1 << 20,
        moved=1 << 12,
        in_specs=[SMEM_SPEC, VMEM_SPEC],
    )(me, hilbert_pos.reshape(1, count))
    x_then, slot, leaving_at = lax.optimization_barrier((x, slot, leaving_at))
    landing = leaving_at
    if chunks == 1:
        landing = lax.all_to_all(
            leaving_at.reshape(curve_size, 1, capacity),
            "curve",
            split_axis=0,
            concat_axis=0,
            tiled=True,
        ).reshape(1, slots)

    rows_f32 = shape(F32, count, width)
    lines_f32 = shape(F32, HEADS, count)
    square = shape(BF16, HEADS, count, count)
    dma = pltpu.SemaphoreType.DMA
    q, k, v, own_weights, sum_mixed, sums = vmem_call(
        functools.partial(prep_body, depth),
        (rows_bf16,) * 3 + (square,) + (rows_f32,) * 2,
        flops=2 << 30,
        moved=4 << 20,
    )(x_then, gain_one, qkv_one)
    early_keys, early_values, early_weights = [k], [v], [own_weights]
    for other in others[: peers - 1]:
        k_next, v_next, weights_next, sum_mixed, sums = vmem_call(
            functools.partial(middle_body, depth),
            (rows_bf16,) * 2 + (square,) + (rows_f32,) * 2,
            flops=2 << 30,
            moved=4 << 20,
        )(other, gain_one, qkv_one, q, sum_mixed, sums)
        early_keys.append(k_next)
        early_values.append(v_next)
        early_weights.append(weights_next)
    early = len(early_keys)
    late = peers + 1 - early
    late_bf16 = shape(BF16, late * count, width)
    embedded = shape(BF16, capacity * tiles + 8, LANES)
    sent = chunk_bf16 if chunks == 1 else embedded
    first_weights = 9 + 2 * early + late
    results = vmem_call(
        functools.partial(forward_body, early, peers, chunks, capacity, depth),
        (late_bf16, late_bf16, shape(BF16, HEADS, count, late * count))
        + (rows_bf16, rows_f32, lines_f32)
        + (square,) * early
        + (sent,) * chunks,
        [
            pltpu.VMEM((early,) + square.shape, BF16),
            dma((early,)),
        ],
        flops=8 << 30,
        moved=8 << 20,
        in_specs=[VMEM_SPEC] * first_weights + [HBM_SPEC] * early,
        out_specs=(VMEM_SPEC,) * 6 + (HBM_SPEC,) * early + (VMEM_SPEC,) * chunks,
        input_output_aliases={first_weights + index: 6 + index for index in range(early)},
    )(
        x,
        gain_one,
        qkv_one,
        out_one,
        slot,
        leaving_at,
        q,
        sum_mixed,
        sums,
        *early_keys,
        *early_values,
        *others[early - 1 :],
        *early_weights,
    )
    late_keys, late_values, late_weights, mixed, inverse, lse = results[:6]
    all_weights = list(results[6 : 6 + early]) + [late_weights]
    all_keys, all_values = early_keys + [late_keys], early_values + [late_values]
    arrived = exchange(results[6 + early :], "curve")
    lse_all = [lse] + [by_xor(lse, "patch", m) for m in steps]

    queries_all = vmem_call(
        functools.partial(queries_body, peers),
        all_bf16,
        flops=1 << 29,
        moved=3 << 20,
        in_specs=[VMEM_SPEC] * (3 + peers),
    )(gain_one, qkv_one, q, *others)
    flipped = vmem_call(
        functools.partial(weights_flipped_body, peers, depth),
        shape(BF16, HEADS, count, total),
        flops=4 << 30,
        moved=10 << 20,
    )(k, queries_all, *lse_all)

    returning = vmem_call(
        functools.partial(second_body, chunks, depth),
        (chunk_bf16,) * chunks,
        [
            pltpu.VMEM((count, 3 * width), BF16),
            pltpu.VMEM((count, 3 * width), BF16),
            pltpu.VMEM((count, width), BF16),
            pltpu.VMEM((count, count), F32),
        ],
        flops=8 << 30,
        moved=4 << 20,
    )(
        landing,
        segments.reshape(1, count),
        gain_two,
        qkv_two,
        out_two,
        out_grad.reshape(count, width),
        *arrived,
    )
    home = exchange(returning, "curve")

    moved_grad, grad_own = vmem_call(
        functools.partial(home_body, chunks, depth),
        (rows_bf16, shape(BF16, count + HEADS, width)),
        flops=1 << 29,
        moved=2 << 20,
    )(slot, mixed, out_one, *home)
    grads = [by_xor(grad_own, "patch", m) for m in steps]

    query_grad, key_grad, value_grad = vmem_call(
        functools.partial(query_grad_body, len(all_keys), depth),
        (rows_bf16, rows_f32, rows_f32),
        [pltpu.VMEM((HEADS, count), F32), pltpu.VMEM((count, width), F32)],
        flops=8 << 30,
        moved=10 << 20,
    )(*all_weights, *all_keys, *all_values, inverse, flipped, grad_own, q)
    for index in range(1, early):
        key_grad, value_grad = vmem_call(
            functools.partial(key_middle_body, index, depth),
            (rows_f32, rows_f32),
            [pltpu.VMEM((HEADS, count), F32)],
            flops=2 << 30,
            moved=4 << 20,
        )(flipped, v, queries_all, key_grad, value_grad, grads[index - 1])
    result = vmem_call(
        functools.partial(key_grad_body, early, peers, depth),
        rows_bf16,
        [
            pltpu.VMEM((count, 3 * width), BF16),
            pltpu.VMEM((late * count, width), BF16),
            pltpu.VMEM((HEADS, late * count), F32),
        ],
        flops=8 << 30,
        moved=14 << 20,
    )(
        flipped,
        v,
        queries_all,
        query_grad,
        key_grad,
        value_grad,
        x,
        gain_one,
        qkv_one,
        moved_grad,
        *grads[early - 1 :],
    )
    return result.reshape(points.shape)


def solution(mesh):
    in_specs = (
        P("curve", "patch", None, None),
        P(),
        P(),
        P(),
        P("curve", "patch", None),
        P(),
        P(),
        P(),
        P("patch", "curve", None),
        P("patch", "curve", None, None),
    )
    out_specs = P("curve", "patch", None, None)

    return jax.shard_map(shards, mesh=mesh, in_specs=in_specs, out_specs=out_specs, check_vma=False)
```

```python
import functools
import math

import jax
import jax.numpy as jnp
from jax import lax
from jax.experimental import pallas as pl
from jax.experimental.pallas import tpu as pltpu
from jax.sharding import PartitionSpec as P


HEADS = 16
EPS = 1e-06
LANES = 128
MASKED = -1e30
MOST_PERMUTES = 16
F32 = jnp.float32
BF16 = jnp.bfloat16
LOG2E = math.log2(math.e)


def dot_nn(left, right):
    return lax.dot_general(left, right, (((1,), (0,)), ((), ())), preferred_element_type=F32)


def dot_nt(left, right):
    return lax.dot_general(left, right, (((1,), (1,)), ((), ())), preferred_element_type=F32)


def dot_tn(left, right):
    return lax.dot_general(left, right, (((0,), (0,)), ((), ())), preferred_element_type=F32)


def norm_parts(rows):
    wide = rows.astype(F32)
    power = jnp.mean(wide * wide, axis=-1, keepdims=True)
    inverse = lax.rsqrt(power + EPS)
    return wide * inverse, inverse


def norm_rows(rows, gain):
    return (norm_parts(rows)[0] * gain).astype(BF16)


def norm_pull(unit, slope, cotangent):
    scaled = cotangent.astype(F32) * slope
    along = jnp.mean(scaled * unit, axis=-1, keepdims=True)
    return (scaled - unit * along).astype(BF16)


def head_mask(rows, index, depth):
    return lax.broadcasted_iota(jnp.int32, (rows, LANES), 1) // depth == index


def only(mask, tile):
    return jnp.where(mask, tile, jnp.zeros_like(tile))


def tile_at(t):
    if isinstance(t, int):
        return slice(t * LANES, (t + 1) * LANES)
    return pl.ds(pl.multiple_of(t * LANES, LANES), LANES)


def tile_loop(tiles, step, carry):
    for t in range(tiles):
        carry = step(t, carry)
    return carry


def vmem_call(body, outs, scratch=(), flops=0, moved=0, **more):
    params = pltpu.CompilerParams(vmem_limit_bytes=24 << 20, **more.pop("params", {}))
    return pl.pallas_call(
        body,
        out_shape=outs,
        scratch_shapes=scratch,
        compiler_params=params,
        cost_estimate=pl.CostEstimate(flops=flops, bytes_accessed=moved, transcendentals=0),
        **more,
    )


HBM_SPEC = pl.BlockSpec(memory_space=pltpu.MemorySpace.HBM)
SMEM_SPEC = pl.BlockSpec(memory_space=pltpu.MemorySpace.SMEM)
VMEM_SPEC = pl.BlockSpec(memory_space=pltpu.MemorySpace.VMEM)
LOW, HIGH = 2.0**-60, 2.0**100


def column(row):
    return jnp.transpose(jnp.broadcast_to(row.astype(F32), (LANES, row.shape[1])))[:, :1]


def start_all(pairs, sems):
    copies = [pltpu.make_async_copy(src, dst, sems.at[i]) for i, (src, dst) in enumerate(pairs)]
    for copy in copies:
        copy.start()
    return copies


def flip_tile(tile):
    return jnp.transpose(tile)


def with_ones(tile):
    return jnp.concatenate([tile, jnp.ones_like(tile)], axis=1)


def unshifted(depth, t, q_tile, k_tile, v_tile, weights_ref):
    count = q_tile.shape[0]
    scale = depth ** (-0.5) * LOG2E
    right = with_ones(v_tile)
    mixed = jnp.zeros((count, LANES), F32)
    sums = jnp.zeros((count, LANES), F32)
    for j in range(LANES // depth):
        mask = head_mask(count, j, depth)
        scores = dot_nt(only(mask, q_tile), k_tile)
        shifted = jnp.exp2(scores * scale).astype(BF16)
        weights_ref[t * (LANES // depth) + j] = shifted
        both = dot_nn(shifted, right)
        mixed = jnp.where(mask, both[:, :LANES], mixed)
        sums = jnp.where(mask, both[:, LANES:], sums)
    return mixed, sums


def route_body(chunks, capacity, me_ref, target_ref, put_ref, take_ref, at_ref):
    count = target_ref.shape[1]
    slots = 2 * count
    target = target_ref[...]
    shift = count.bit_length() - 1
    owner = lax.shift_right_logical(target, jnp.full_like(target, shift))
    offset = target - lax.shift_left(owner, jnp.full_like(target, shift))
    same = column(owner) == owner.astype(F32)
    earlier = lax.broadcasted_iota(jnp.int32, (count, count), 0) < (
        lax.broadcasted_iota(jnp.int32, (count, count), 1)
    )
    ranking = jnp.sum(jnp.where(same & earlier, 1.0, 0.0), axis=0, keepdims=True).astype(jnp.int32)
    lane = owner if chunks == 1 else lax.bitwise_xor(owner, jnp.full_like(owner, me_ref[0]))
    slot = lane * capacity + ranking
    put = lax.broadcasted_iota(jnp.int32, (slots, count), 0) == slot
    put_ref[...] = put.astype(F32).astype(BF16)
    hit = column(slot) == lax.broadcasted_iota(jnp.int32, (count, slots), 1).astype(F32)
    take_ref[...] = hit.astype(F32).astype(BF16)
    at = jnp.sum(jnp.where(hit, column(offset) - count, 0.0), axis=0, keepdims=True) + count
    at_ref[...] = at.astype(at_ref.dtype)


def prep_body(depth, *refs):
    x_ref, gain_ref, w_ref = refs[:3]
    q_ref, k_ref, v_ref, weights_ref, mixed_ref, sums_ref, unit_ref, slope_ref = refs[3:]
    width = x_ref.shape[1]
    unit, inverse = norm_parts(x_ref[...])
    unit_ref[...] = unit
    slope_ref[...] = inverse * gain_ref[...]
    normed = (unit * gain_ref[...]).astype(BF16)
    q_ref[...] = dot_nn(normed, w_ref[:, :width]).astype(BF16)
    k_ref[...] = dot_nn(normed, w_ref[:, width : 2 * width]).astype(BF16)
    v_ref[...] = dot_nn(normed, w_ref[:, 2 * width :]).astype(BF16)

    def tile_step(t, carry):
        at = tile_at(t)
        mixed_ref[:, at], sums_ref[:, at] = unshifted(
            depth, t, q_ref[:, at], k_ref[:, at], v_ref[:, at], weights_ref
        )
        return carry

    tile_loop(width // LANES, tile_step, 0)


def middle_body(depth, *refs):
    x_ref, gain_ref, w_ref, q_ref, mixed_in_ref, sums_in_ref = refs[:6]
    k_ref, v_ref, weights_ref, mixed_ref, sums_ref = refs[6:]
    width = x_ref.shape[1]
    normed = norm_rows(x_ref[...], gain_ref[...])
    k_ref[...] = dot_nn(normed, w_ref[:, width : 2 * width]).astype(BF16)
    v_ref[...] = dot_nn(normed, w_ref[:, 2 * width :]).astype(BF16)

    def tile_step(t, carry):
        at = tile_at(t)
        mixed, sums = unshifted(depth, t, q_ref[:, at], k_ref[:, at], v_ref[:, at], weights_ref)
        mixed_ref[:, at] = mixed + mixed_in_ref[:, at]
        sums_ref[:, at] = sums + sums_in_ref[:, at]
        return carry

    tile_loop(width // LANES, tile_step, 0)


def forward_body(early, peers, chunks, capacity, depth, *refs):
    x_ref, gain_ref, w_ref, out_w_ref, put_ref, at_ref, q_ref, mixed_in_ref, sums_in_ref = refs[:9]
    refs = refs[9:]
    early_keys, early_values, refs = refs[:early], refs[early : 2 * early], refs[2 * early :]
    others, refs = refs[: peers + 1 - early], refs[peers + 1 - early + early :]
    keys_ref, values_ref, weights_ref, mixed_ref, inverse_ref, lse_ref = refs[:6]
    early_weights, refs = refs[6 : 6 + early], refs[6 + early :]
    sends, (safe, out_sems) = refs[:chunks], refs[chunks:]
    count, width = x_ref.shape
    heads = LANES // depth
    for index, other in enumerate(others):
        rows = slice(index * count, (index + 1) * count)
        normed = norm_rows(other[...], gain_ref[...])
        keys_ref[rows] = dot_nn(normed, w_ref[:, width : 2 * width]).astype(BF16)
        values_ref[rows] = dot_nn(normed, w_ref[:, 2 * width :]).astype(BF16)

    def finish_tile(t, at, mixed, sums, tops):
        inverse = 1.0 / sums
        mixed_ref[:, at] = (mixed * inverse).astype(BF16)
        inverse_ref[:, at] = inverse
        flipped = flip_tile(tops + jnp.log(sums) * LOG2E)
        for j in range(heads):
            lse_ref[pl.ds(t * heads + j, 1)] = flipped[j * depth : j * depth + 1]

    def fast_step(t, bad):
        at = tile_at(t)
        mixed, sums = unshifted(
            depth, t, q_ref[:, at], keys_ref[:, at], values_ref[:, at], weights_ref
        )
        mixed += mixed_in_ref[:, at]
        sums += sums_in_ref[:, at]
        finish_tile(t, at, mixed, sums, 0.0)
        return jnp.where((sums >= LOW) & (sums <= HIGH), bad, 1.0)

    bad = tile_loop(width // LANES, fast_step, jnp.zeros((count, LANES), F32))

    @pl.when(jnp.max(bad) > 0.0)
    def _():
        scale = depth ** (-0.5) * LOG2E

        def safe_step(t, carry):
            at = tile_at(t)
            keys = jnp.concatenate([ref[:, at] for ref in early_keys + (keys_ref,)], axis=0)
            values = jnp.concatenate([ref[:, at] for ref in early_values + (values_ref,)], axis=0)
            right = with_ones(values)
            mixed = jnp.zeros((count, LANES), F32)
            sums = jnp.ones((count, LANES), F32)
            tops = jnp.zeros((count, LANES), F32)
            for j in range(heads):
                mask = head_mask(count, j, depth)
                scores = dot_nt(only(mask, q_ref[:, at]), keys)
                top = jnp.max(scores, axis=-1, keepdims=True) * scale
                shifted = jnp.exp2(scores * scale - top).astype(BF16)
                weights_ref[t * heads + j] = shifted[:, early * count :]
                for index in range(early):
                    part = shifted[:, index * count : (index + 1) * count]
                    safe[index, t * heads + j] = part
                both = dot_nn(shifted, right)
                mixed = jnp.where(mask, both[:, :LANES], mixed)
                sums = jnp.where(mask, both[:, LANES:], sums)
                tops = jnp.where(mask, top, tops)
            finish_tile(t, at, mixed, sums, tops)
            return carry

        lax.fori_loop(0, width // LANES, safe_step, 0)
        pairs = [(safe.at[index], early_weights[index]) for index in range(early)]
        for copy in start_all(pairs, out_sems):
            copy.wait()

    moved = (x_ref[...].astype(F32) + dot_nn(mixed_ref[...], out_w_ref[...])).astype(BF16)
    slots = 2 * count
    leaving = dot_nn(put_ref[...], moved).astype(BF16)
    if chunks == 1:
        sends[0][...] = leaving
    else:
        tail = sends[0].shape[0] - capacity * (width // LANES)
        line = jnp.broadcast_to(at_ref[...], (tail, slots)).astype(BF16)
        for m, send in enumerate(sends):
            part = slice(m * capacity, (m + 1) * capacity)
            for t in range(width // LANES):
                tile = leaving[part, t * LANES : (t + 1) * LANES]
                send[t * capacity : (t + 1) * capacity] = tile
            padding = jnp.zeros((tail, LANES - capacity), BF16)
            send[send.shape[0] - tail :] = jnp.concatenate([line[:, part], padding], axis=1)


def second_early_body(seg_ref, out_w_ref, grad_ref, mixed_grad_ref, bias_ref):
    mixed_grad_ref[...] = dot_nt(grad_ref[...], out_w_ref[...]).astype(BF16)
    bias_ref[...] = jnp.where(column(seg_ref[...]) == seg_ref[...].astype(F32), 0.0, MASKED)


def second_body(chunks, depth, *refs):
    land_ref, gain_ref, w_ref, grad_ref, mixed_grad, bias = refs[:6]
    arrived = refs[6 : 6 + chunks]
    sends = refs[6 + chunks : 6 + 2 * chunks]
    packed, packed_grad = refs[6 + 2 * chunks :]
    count, width = grad_ref.shape
    slots = 2 * count
    size = slots // chunks
    if chunks == 1:
        landing = land_ref[...].astype(F32)
        rows = arrived[0][...]
    else:
        ends = [piece[size * (width // LANES) :].astype(F32)[:1, :size] for piece in arrived]
        landing = jnp.concatenate(ends, axis=1)
        rows = []
        for piece in arrived:
            tiles = [piece[t * size : (t + 1) * size] for t in range(width // LANES)]
            rows.append(jnp.concatenate(tiles, axis=1))
        rows = jnp.concatenate(rows, axis=0)
    place = lax.broadcasted_iota(jnp.int32, (count, slots), 0).astype(F32) == landing
    place = place.astype(F32)
    hilbert = dot_nn(place.astype(BF16), rows).astype(BF16)
    unit, inverse = norm_parts(hilbert)
    packed[...] = dot_nn((unit * gain_ref[...]).astype(BF16), w_ref[...]).astype(BF16)
    scale = depth ** (-0.5)

    tiles = width // LANES
    heads = LANES // depth
    masks = [head_mask(count, j, depth) for j in range(heads)]
    stacked = (heads, count, count)

    def products(t):
        k_tile = packed[:, tile_at(t + tiles)]
        v_tile = packed[:, tile_at(t + 2 * tiles)]
        k_heads = jnp.concatenate([only(mask, k_tile) for mask in masks], axis=0)
        v_heads = jnp.concatenate([only(mask, v_tile) for mask in masks], axis=0)
        scores = dot_nt(k_heads, packed[:, tile_at(t)])
        return scores, dot_nt(v_heads, mixed_grad[:, tile_at(t)])

    def softmax(scores, weight_grad):
        scores = scores.reshape(stacked) * (scale * LOG2E) + bias[...][None]
        weight_grad = weight_grad.reshape(stacked)
        shifted = jnp.exp2(scores - jnp.max(scores, axis=1, keepdims=True))
        inverse = 1.0 / jnp.sum(shifted, axis=1, keepdims=True)
        carried = jnp.sum(shifted * weight_grad, axis=1, keepdims=True) * inverse
        weights = shifted * inverse
        score_grad = (weights * (weight_grad - carried)).astype(BF16)
        return weights.astype(BF16), score_grad

    def gradients(t, weights, score_grad):
        at = tile_at(t)
        k_at, v_at = tile_at(t + tiles), tile_at(t + 2 * tiles)
        k_flipped = flip_tile(packed[:, k_at])
        dk_heads = dot_nn(score_grad.reshape(heads * count, count), packed[:, at])
        dv_heads = dot_nn(weights.reshape(heads * count, count), mixed_grad[:, at])
        dk, dv, dq = dk_heads[:count], dv_heads[:count], []
        for j in range(heads):
            part = slice(j * count, (j + 1) * count)
            dk = jnp.where(masks[j], dk_heads[part], dk)
            dv = jnp.where(masks[j], dv_heads[part], dv)
            dq.append(dot_nn(k_flipped[j * depth : (j + 1) * depth], score_grad[j]))
        dq = jnp.transpose(jnp.concatenate(dq, axis=0))
        packed_grad[:, at] = (dq * scale).astype(BF16)
        packed_grad[:, k_at] = (dk * scale).astype(BF16)
        packed_grad[:, v_at] = dv.astype(BF16)

    ahead = products(0)
    for t in range(tiles):
        now, ahead = ahead, products(t + 1) if t + 1 < tiles else None
        gradients(t, *softmax(*now))
    normed_grad = dot_nt(packed_grad[...], w_ref[...]).astype(BF16)
    path = norm_pull(unit, inverse * gain_ref[...], normed_grad)
    total = grad_ref[...].astype(F32) + path.astype(F32)
    back = lax.broadcasted_iota(jnp.int32, (slots, count), 1).astype(F32) == column(landing)
    returning = dot_nn(back.astype(F32).astype(BF16), total.astype(BF16)).astype(BF16)
    for m, send in enumerate(sends):
        send[...] = returning[m * size : (m + 1) * size]


def queries_body(peers, *refs):
    gain_ref, w_ref, q_ref = refs[:3]
    others = refs[3 : 3 + peers]
    out_ref = refs[3 + peers]
    count, width = q_ref.shape
    out_ref[:count] = q_ref[...]
    for index, other in enumerate(others):
        rows = slice((index + 1) * count, (index + 2) * count)
        normed = norm_rows(other[...], gain_ref[...])
        out_ref[rows] = dot_nn(normed, w_ref[:, :width]).astype(BF16)


def spread(rows, width):
    heads = rows.shape[0]
    pick = lax.broadcasted_iota(jnp.int32, (heads, width), 1) // (width // heads) == (
        lax.broadcasted_iota(jnp.int32, (heads, width), 0)
    )
    return dot_tn(rows, pick.astype(F32).astype(BF16))


def weights_flipped_body(peers, depth, *refs):
    k_ref, queries_ref = refs[:2]
    lse_refs = refs[2 : 3 + peers]
    out_ref = refs[3 + peers]
    scale = depth ** (-0.5) * LOG2E
    heads = LANES // depth
    count = k_ref.shape[0]

    def tile_step(t, carry):
        at = tile_at(t)
        for j in range(heads):
            mask = head_mask(count, j, depth)
            scores = dot_nt(only(mask, k_ref[:, at]), queries_ref[:, at])
            h = t * heads + j
            line = jnp.concatenate([ref[pl.ds(h, 1)] for ref in lse_refs], axis=1)
            out_ref[h] = jnp.exp2(scores * scale - line).astype(BF16)
        return carry

    tile_loop(k_ref.shape[1] // LANES, tile_step, 0)


def home_body(chunks, depth, *refs):
    take_ref, mixed_ref, out_w_ref = refs[:3]
    home = refs[3 : 3 + chunks]
    moved_ref, grad_ref = refs[3 + chunks :]
    count, width = moved_ref.shape
    rows = jnp.concatenate([piece[...] for piece in home], axis=0)
    moved = dot_nn(take_ref[...], rows).astype(BF16)
    moved_ref[...] = moved
    grad = dot_nt(moved, out_w_ref[...]).astype(BF16)
    grad_ref[:count] = grad
    product = grad.astype(F32) * mixed_ref[...].astype(F32)
    high = product.astype(BF16)
    low = (product - high.astype(F32)).astype(BF16)
    heads = width // depth
    pick = lax.broadcasted_iota(jnp.int32, (heads, width), 1) // depth == (
        lax.broadcasted_iota(jnp.int32, (heads, width), 0)
    )
    pick = pick.astype(F32).astype(BF16)
    rows = dot_nt(pick, high) + dot_nt(pick, low)
    rows_high = rows.astype(BF16)
    grad_ref[count:, :count] = rows_high
    grad_ref[count:, count:] = (rows - rows_high.astype(F32)).astype(BF16)


def key_tile(depth, t, v_tile, weights_ref, columns, queries, grads, deltas_ref):
    count = v_tile.shape[0]
    heads = LANES // depth
    dk = jnp.zeros((count, LANES), F32)
    dv = jnp.zeros((count, LANES), F32)
    for j in range(heads):
        h = t * heads + j
        mask = head_mask(count, j, depth)
        weights = weights_ref[h, :, columns]
        weight_grad = dot_nt(only(mask, v_tile), grads)
        delta = deltas_ref[pl.ds(h, 1)]
        score_grad = (weights.astype(F32) * (weight_grad - delta)).astype(BF16)
        dv = jnp.where(mask, dot_nn(weights, grads), dv)
        dk = jnp.where(mask, dot_nn(score_grad, queries), dk)
    return dk, dv


def halves(lines):
    half = lines.shape[1] // 2
    return lines[:, :half], lines[:, half:]


def query_grad_body(parts, depth, *refs):
    weights_refs, refs = refs[:parts], refs[parts:]
    keys_refs, refs = refs[:parts], refs[parts:]
    values_refs, refs = refs[:parts], refs[parts:]
    inverse_ref, flipped_ref, grad_ref, q_ref, w_ref = refs[:5]
    normed_ref, dk_ref, dv_ref, dq_all, lines, wide = refs[5:]
    count, width = q_ref.shape
    heads = LANES // depth
    high, low = halves(grad_ref[count:])
    lines[...] = high.astype(F32) + low.astype(F32)
    wide[...] = spread(high, width) + spread(low, width)

    def tile_step(t, carry):
        at = tile_at(t)
        g_tile = grad_ref[:count, at]
        delta_tile = wide[:, at]
        keys = jnp.concatenate([ref[:, at] for ref in keys_refs], axis=0)
        values = jnp.concatenate([ref[:, at] for ref in values_refs], axis=0)
        dq = jnp.zeros((count, LANES), F32)
        for j in range(heads):
            mask = head_mask(count, j, depth)
            weight_grad = dot_nt(only(mask, g_tile), values)
            delta = delta_tile[:, j * depth : j * depth + 1]
            weights = jnp.concatenate([ref[t * heads + j] for ref in weights_refs], axis=1)
            score_grad = (weights.astype(F32) * (weight_grad - delta)).astype(BF16)
            dq = jnp.where(mask, dot_nn(score_grad, keys), dq)
        dq_all[:, at] = (dq * (inverse_ref[:, at] * depth ** (-0.5))).astype(BF16)
        dk_ref[:, at], dv_ref[:, at] = key_tile(
            depth,
            t,
            values_refs[0][:, at],
            flipped_ref,
            slice(0, count),
            q_ref[:, at],
            g_tile,
            lines,
        )
        return carry

    tile_loop(width // LANES, tile_step, 0)
    normed_ref[...] = dot_nt(dq_all[...], w_ref[:, :width])


def key_middle_body(index, depth, *refs):
    flipped_ref, v_ref, queries_ref, dk_in_ref, dv_in_ref, grad_ref = refs[:6]
    dk_ref, dv_ref, lines = refs[6:]
    count, width = v_ref.shape
    high, low = halves(grad_ref[count:])
    lines[...] = high.astype(F32) + low.astype(F32)
    rows = slice(index * count, (index + 1) * count)

    def tile_step(t, carry):
        at = tile_at(t)
        dk, dv = key_tile(
            depth,
            t,
            v_ref[:, at],
            flipped_ref,
            rows,
            queries_ref[rows, at],
            grad_ref[:count, at],
            lines,
        )
        dk_ref[:, at] = dk + dk_in_ref[:, at]
        dv_ref[:, at] = dv + dv_in_ref[:, at]
        return carry

    tile_loop(width // LANES, tile_step, 0)


def key_grad_body(early, peers, depth, *refs):
    flipped_ref, v_ref, queries_ref, normed_ref, dk_ref, dv_ref = refs[:6]
    unit_ref, slope_ref, w_ref, moved_ref = refs[6:10]
    others = refs[10 : 11 + peers - early]
    out_ref, packed_grad, grads, lines = refs[11 + peers - early :]
    count, width = unit_ref.shape
    for i, other in enumerate(others):
        rows = slice(i * count, (i + 1) * count)
        grads[rows] = other[:count]
        high, low = halves(other[count:])
        lines[:, rows] = high.astype(F32) + low.astype(F32)

    def tile_step(t, carry):
        at = tile_at(t)
        dk, dv = key_tile(
            depth,
            t,
            v_ref[:, at],
            flipped_ref,
            slice(early * count, (peers + 1) * count),
            queries_ref[early * count :, at],
            grads[:, at],
            lines,
        )
        dk = (dk + dk_ref[:, at]) * depth ** (-0.5)
        packed_grad[:, at] = dk.astype(BF16)
        packed_grad[:, tile_at(t + width // LANES)] = (dv + dv_ref[:, at]).astype(BF16)
        return carry

    tile_loop(width // LANES, tile_step, 0)
    normed_grad = normed_ref[...] + dot_nt(packed_grad[...], w_ref[:, width:])
    path = norm_pull(unit_ref[...], slope_ref[...], normed_grad.astype(BF16))
    out_ref[...] = (moved_ref[...].astype(F32) + path.astype(F32)).astype(BF16)


def single_first(size):
    return sorted(range(1, size), key=lambda step: (step.bit_count(), -step))


def by_xor(array, axis, step):
    size = lax.axis_size(axis)
    return lax.ppermute(array, axis, [(i, i ^ step) for i in range(size)])


def exchange(pieces, axis):
    if len(pieces) == 1:
        size = lax.axis_size(axis)
        stacked = pieces[0].reshape((size, -1) + pieces[0].shape[1:])
        got = lax.all_to_all(stacked, axis, split_axis=0, concat_axis=0, tiled=True)
        return [got.reshape(pieces[0].shape)]
    return [pieces[0]] + [by_xor(pieces[m], axis, m) for m in range(1, len(pieces))]


def shards(
    points, gain_one, qkv_one, out_one, hilbert_pos, gain_two, qkv_two, out_two, segments, out_grad
):
    count, width = points.shape[2:]
    depth = width // HEADS
    tiles = width // LANES
    patch_size = lax.axis_size("patch")
    curve_size = lax.axis_size("curve")
    peers = patch_size - 1
    total = patch_size * count
    slots = 2 * count
    capacity = slots // curve_size
    chunks = curve_size if curve_size <= MOST_PERMUTES else 1
    rows_bf16 = jax.ShapeDtypeStruct((count, width), BF16)
    all_bf16 = jax.ShapeDtypeStruct((total, width), BF16)
    chunk_bf16 = jax.ShapeDtypeStruct((slots // chunks, width), BF16)

    x = points.reshape(count, width)
    steps = single_first(patch_size)
    others = [by_xor(x, "patch", m) for m in steps]
    gain_one = gain_one.reshape(1, width)
    gain_two = gain_two.reshape(1, width)

    def shape(kind, *dims):
        return jax.ShapeDtypeStruct(dims, kind)

    me = lax.axis_index("curve").astype(jnp.int32).reshape(1)
    put, take, leaving_at = vmem_call(
        functools.partial(route_body, chunks, capacity),
        (shape(BF16, slots, count), shape(BF16, count, slots))
        + (shape(jnp.int32 if chunks == 1 else F32, 1, slots),),
        flops=8 << 30,
        moved=16 << 20,
        in_specs=[SMEM_SPEC, VMEM_SPEC],
    )(me, hilbert_pos.reshape(1, count))
    x_then, put, take, leaving_at = lax.optimization_barrier((x, put, take, leaving_at))
    landing = leaving_at
    if chunks == 1:
        landing = lax.all_to_all(
            leaving_at.reshape(curve_size, 1, capacity),
            "curve",
            split_axis=0,
            concat_axis=0,
            tiled=True,
        ).reshape(1, slots)

    rows_f32 = shape(F32, count, width)
    lines_f32 = shape(F32, HEADS, count)
    square = shape(BF16, HEADS, count, count)
    dma = pltpu.SemaphoreType.DMA
    q, k, v, own_weights, sum_mixed, sums, unit, slope = vmem_call(
        functools.partial(prep_body, depth),
        (rows_bf16,) * 3 + (square,) + (rows_f32,) * 4,
        flops=2 << 30,
        moved=4 << 20,
    )(x_then, gain_one, qkv_one)
    early_keys, early_values, early_weights = [k], [v], [own_weights]
    for other in others[: peers - 1]:
        k_next, v_next, weights_next, sum_mixed, sums = vmem_call(
            functools.partial(middle_body, depth),
            (rows_bf16,) * 2 + (square,) + (rows_f32,) * 2,
            flops=2 << 30,
            moved=4 << 20,
        )(other, gain_one, qkv_one, q, sum_mixed, sums)
        early_keys.append(k_next)
        early_values.append(v_next)
        early_weights.append(weights_next)
    early = len(early_keys)
    late = peers + 1 - early
    late_bf16 = shape(BF16, late * count, width)
    embedded = shape(BF16, capacity * tiles + 8, LANES)
    sent = chunk_bf16 if chunks == 1 else embedded
    first_weights = 9 + 2 * early + late
    results = vmem_call(
        functools.partial(forward_body, early, peers, chunks, capacity, depth),
        (late_bf16, late_bf16, shape(BF16, HEADS, count, late * count))
        + (rows_bf16, rows_f32, lines_f32)
        + (square,) * early
        + (sent,) * chunks,
        [
            pltpu.VMEM((early,) + square.shape, BF16),
            dma((early,)),
        ],
        flops=8 << 30,
        moved=8 << 20,
        in_specs=[VMEM_SPEC] * first_weights + [HBM_SPEC] * early,
        out_specs=(VMEM_SPEC,) * 6 + (HBM_SPEC,) * early + (VMEM_SPEC,) * chunks,
        input_output_aliases={first_weights + index: 6 + index for index in range(early)},
    )(
        x,
        gain_one,
        qkv_one,
        out_one,
        put,
        leaving_at,
        q,
        sum_mixed,
        sums,
        *early_keys,
        *early_values,
        *others[early - 1 :],
        *early_weights,
    )
    late_keys, late_values, late_weights, mixed, inverse, lse = results[:6]
    all_weights = list(results[6 : 6 + early]) + [late_weights]
    all_keys, all_values = early_keys + [late_keys], early_values + [late_values]
    arrived = exchange(results[6 + early :], "curve")
    lse_all = [lse] + [by_xor(lse, "patch", m) for m in steps]

    out_grad_then, inverse = lax.optimization_barrier((out_grad, inverse))
    queries_all = vmem_call(
        functools.partial(queries_body, peers),
        all_bf16,
        flops=1 << 29,
        moved=3 << 20,
        in_specs=[VMEM_SPEC] * (3 + peers),
    )(gain_one, qkv_one, q, *others)
    flipped = vmem_call(
        functools.partial(weights_flipped_body, peers, depth),
        shape(BF16, HEADS, count, total),
        flops=4 << 30,
        moved=10 << 20,
    )(k, queries_all, *lse_all)

    second_mixed, bias = vmem_call(
        second_early_body, (rows_bf16, shape(F32, count, count)), flops=1 << 29, moved=1 << 20
    )(segments.reshape(1, count), out_two, out_grad_then.reshape(count, width))
    returning = vmem_call(
        functools.partial(second_body, chunks, depth),
        (chunk_bf16,) * chunks,
        [pltpu.VMEM((count, 3 * width), BF16), pltpu.VMEM((count, 3 * width), BF16)],
        flops=8 << 30,
        moved=4 << 20,
    )(
        landing,
        gain_two,
        qkv_two,
        out_grad_then.reshape(count, width),
        second_mixed,
        bias,
        *arrived,
    )
    home = exchange(returning, "curve")

    moved_grad, grad_own = vmem_call(
        functools.partial(home_body, chunks, depth),
        (rows_bf16, shape(BF16, count + HEADS, width)),
        flops=1 << 29,
        moved=2 << 20,
    )(take, mixed, out_one, *home)
    grads = [by_xor(grad_own, "patch", m) for m in steps]

    normed_grad, key_grad, value_grad = vmem_call(
        functools.partial(query_grad_body, len(all_keys), depth),
        (rows_f32, rows_f32, rows_f32),
        [
            pltpu.VMEM((count, width), BF16),
            pltpu.VMEM((HEADS, count), F32),
            pltpu.VMEM((count, width), F32),
        ],
        flops=8 << 30,
        moved=10 << 20,
    )(*all_weights, *all_keys, *all_values, inverse, flipped, grad_own, q, qkv_one)
    for index in range(1, early):
        key_grad, value_grad = vmem_call(
            functools.partial(key_middle_body, index, depth),
            (rows_f32, rows_f32),
            [pltpu.VMEM((HEADS, count), F32)],
            flops=2 << 30,
            moved=4 << 20,
        )(flipped, v, queries_all, key_grad, value_grad, grads[index - 1])
    result = vmem_call(
        functools.partial(key_grad_body, early, peers, depth),
        rows_bf16,
        [
            pltpu.VMEM((count, 2 * width), BF16),
            pltpu.VMEM((late * count, width), BF16),
            pltpu.VMEM((HEADS, late * count), F32),
        ],
        flops=8 << 30,
        moved=14 << 20,
    )(
        flipped,
        v,
        queries_all,
        normed_grad,
        key_grad,
        value_grad,
        unit,
        slope,
        qkv_one,
        moved_grad,
        *grads[early - 1 :],
    )
    return result.reshape(points.shape)


def solution(mesh):
    in_specs = (
        P("curve", "patch", None, None),
        P(),
        P(),
        P(),
        P("curve", "patch", None),
        P(),
        P(),
        P(),
        P("patch", "curve", None),
        P("patch", "curve", None, None),
    )
    out_specs = P("curve", "patch", None, None)

    return jax.shard_map(shards, mesh=mesh, in_specs=in_specs, out_specs=out_specs, check_vma=False)
```

```python
import functools
import math

import jax
import jax.numpy as jnp
from jax import lax
from jax.experimental import pallas as pl
from jax.experimental.pallas import tpu as pltpu
from jax.sharding import PartitionSpec as P


HEADS = 16
EPS = 1e-06
LANES = 128
MASKED = -1e30
MOST_PERMUTES = 16
F32 = jnp.float32
BF16 = jnp.bfloat16
LOG2E = math.log2(math.e)


def dot_nn(left, right):
    return lax.dot_general(left, right, (((1,), (0,)), ((), ())), preferred_element_type=F32)


def dot_nt(left, right):
    return lax.dot_general(left, right, (((1,), (1,)), ((), ())), preferred_element_type=F32)


def dot_tn(left, right):
    return lax.dot_general(left, right, (((0,), (0,)), ((), ())), preferred_element_type=F32)


def norm_parts(rows):
    wide = rows.astype(F32)
    power = jnp.mean(wide * wide, axis=-1, keepdims=True)
    inverse = lax.rsqrt(power + EPS)
    return wide * inverse, inverse


def norm_rows(rows, gain):
    return (norm_parts(rows)[0] * gain).astype(BF16)


def norm_pull(unit, slope, cotangent):
    scaled = cotangent.astype(F32) * slope
    along = jnp.mean(scaled * unit, axis=-1, keepdims=True)
    return (scaled - unit * along).astype(BF16)


def head_mask(rows, index, depth):
    return lax.broadcasted_iota(jnp.int32, (rows, LANES), 1) // depth == index


def only(mask, tile):
    return jnp.where(mask, tile, jnp.zeros_like(tile))


def tile_at(t):
    if isinstance(t, int):
        return slice(t * LANES, (t + 1) * LANES)
    return pl.ds(pl.multiple_of(t * LANES, LANES), LANES)


def tile_loop(tiles, step, carry):
    for t in range(tiles):
        carry = step(t, carry)
    return carry


def vmem_call(body, outs, scratch=(), flops=0, moved=0, **more):
    params = pltpu.CompilerParams(vmem_limit_bytes=24 << 20, **more.pop("params", {}))
    return pl.pallas_call(
        body,
        out_shape=outs,
        scratch_shapes=scratch,
        compiler_params=params,
        cost_estimate=pl.CostEstimate(flops=flops, bytes_accessed=moved, transcendentals=0),
        **more,
    )


HBM_SPEC = pl.BlockSpec(memory_space=pltpu.MemorySpace.HBM)
SMEM_SPEC = pl.BlockSpec(memory_space=pltpu.MemorySpace.SMEM)
VMEM_SPEC = pl.BlockSpec(memory_space=pltpu.MemorySpace.VMEM)
LOW, HIGH = 2.0**-60, 2.0**100


def column(row):
    return jnp.transpose(jnp.broadcast_to(row.astype(F32), (LANES, row.shape[1])))[:, :1]


def start_all(pairs, sems):
    copies = [pltpu.make_async_copy(src, dst, sems.at[i]) for i, (src, dst) in enumerate(pairs)]
    for copy in copies:
        copy.start()
    return copies


def flip_tile(tile):
    return jnp.transpose(tile)


def with_ones(tile):
    return jnp.concatenate([tile, jnp.ones_like(tile)], axis=1)


def unshifted(depth, t, q_tile, k_tile, v_tile, weights_ref):
    count = q_tile.shape[0]
    scale = depth ** (-0.5) * LOG2E
    right = with_ones(v_tile)
    mixed = jnp.zeros((count, LANES), F32)
    sums = jnp.zeros((count, LANES), F32)
    for j in range(LANES // depth):
        mask = head_mask(count, j, depth)
        scores = dot_nt(only(mask, q_tile), k_tile)
        shifted = jnp.exp2(scores * scale).astype(BF16)
        weights_ref[t * (LANES // depth) + j] = shifted
        both = dot_nn(shifted, right)
        mixed = jnp.where(mask, both[:, :LANES], mixed)
        sums = jnp.where(mask, both[:, LANES:], sums)
    return mixed, sums


def route_body(chunks, capacity, me_ref, target_ref, put_ref, take_ref, at_ref):
    count = target_ref.shape[1]
    slots = 2 * count
    target = target_ref[...]
    shift = count.bit_length() - 1
    owner = lax.shift_right_logical(target, jnp.full_like(target, shift))
    offset = target - lax.shift_left(owner, jnp.full_like(target, shift))
    same = column(owner) == owner.astype(F32)
    earlier = lax.broadcasted_iota(jnp.int32, (count, count), 0) < (
        lax.broadcasted_iota(jnp.int32, (count, count), 1)
    )
    ranking = jnp.sum(jnp.where(same & earlier, 1.0, 0.0), axis=0, keepdims=True).astype(jnp.int32)
    lane = owner if chunks == 1 else lax.bitwise_xor(owner, jnp.full_like(owner, me_ref[0]))
    slot = lane * capacity + ranking
    put = lax.broadcasted_iota(jnp.int32, (slots, count), 0) == slot
    put_ref[...] = put.astype(F32).astype(BF16)
    hit = column(slot) == lax.broadcasted_iota(jnp.int32, (count, slots), 1).astype(F32)
    take_ref[...] = hit.astype(F32).astype(BF16)
    at = jnp.sum(jnp.where(hit, column(offset) - count, 0.0), axis=0, keepdims=True) + count
    at_ref[...] = at.astype(at_ref.dtype)


def prep_body(depth, *refs):
    x_ref, gain_ref, w_ref = refs[:3]
    q_ref, k_ref, v_ref, weights_ref, mixed_ref, sums_ref, unit_ref, slope_ref = refs[3:]
    width = x_ref.shape[1]
    unit, inverse = norm_parts(x_ref[...])
    unit_ref[...] = unit
    slope_ref[...] = inverse * gain_ref[...]
    normed = (unit * gain_ref[...]).astype(BF16)
    q_ref[...] = dot_nn(normed, w_ref[:, :width]).astype(BF16)
    k_ref[...] = dot_nn(normed, w_ref[:, width : 2 * width]).astype(BF16)
    v_ref[...] = dot_nn(normed, w_ref[:, 2 * width :]).astype(BF16)

    def tile_step(t, carry):
        at = tile_at(t)
        mixed_ref[:, at], sums_ref[:, at] = unshifted(
            depth, t, q_ref[:, at], k_ref[:, at], v_ref[:, at], weights_ref
        )
        return carry

    tile_loop(width // LANES, tile_step, 0)


def middle_body(depth, *refs):
    x_ref, gain_ref, w_ref, q_ref, mixed_in_ref, sums_in_ref = refs[:6]
    k_ref, v_ref, weights_ref, mixed_ref, sums_ref = refs[6:]
    width = x_ref.shape[1]
    normed = norm_rows(x_ref[...], gain_ref[...])
    k_ref[...] = dot_nn(normed, w_ref[:, width : 2 * width]).astype(BF16)
    v_ref[...] = dot_nn(normed, w_ref[:, 2 * width :]).astype(BF16)

    def tile_step(t, carry):
        at = tile_at(t)
        mixed, sums = unshifted(depth, t, q_ref[:, at], k_ref[:, at], v_ref[:, at], weights_ref)
        mixed_ref[:, at] = mixed + mixed_in_ref[:, at]
        sums_ref[:, at] = sums + sums_in_ref[:, at]
        return carry

    tile_loop(width // LANES, tile_step, 0)


def forward_body(early, peers, chunks, capacity, depth, *refs):
    x_ref, gain_ref, w_ref, out_w_ref, put_ref, at_ref, q_ref, mixed_in_ref, sums_in_ref = refs[:9]
    refs = refs[9:]
    early_keys, early_values, refs = refs[:early], refs[early : 2 * early], refs[2 * early :]
    others, refs = refs[: peers + 1 - early], refs[peers + 1 - early + early :]
    keys_ref, values_ref, weights_ref, mixed_ref, inverse_ref, lse_ref = refs[:6]
    early_weights, refs = refs[6 : 6 + early], refs[6 + early :]
    sends, (safe, out_sems) = refs[:chunks], refs[chunks:]
    count, width = x_ref.shape
    heads = LANES // depth
    for index, other in enumerate(others):
        rows = slice(index * count, (index + 1) * count)
        normed = norm_rows(other[...], gain_ref[...])
        keys_ref[rows] = dot_nn(normed, w_ref[:, width : 2 * width]).astype(BF16)
        values_ref[rows] = dot_nn(normed, w_ref[:, 2 * width :]).astype(BF16)

    def finish_tile(t, at, mixed, sums, tops):
        inverse = 1.0 / sums
        mixed_ref[:, at] = (mixed * inverse).astype(BF16)
        inverse_ref[:, at] = inverse
        flipped = flip_tile(tops + jnp.log(sums) * LOG2E)
        for j in range(heads):
            lse_ref[pl.ds(t * heads + j, 1)] = flipped[j * depth : j * depth + 1]

    def fast_step(t, bad):
        at = tile_at(t)
        mixed, sums = unshifted(
            depth, t, q_ref[:, at], keys_ref[:, at], values_ref[:, at], weights_ref
        )
        mixed += mixed_in_ref[:, at]
        sums += sums_in_ref[:, at]
        finish_tile(t, at, mixed, sums, 0.0)
        return jnp.where((sums >= LOW) & (sums <= HIGH), bad, 1.0)

    bad = tile_loop(width // LANES, fast_step, jnp.zeros((count, LANES), F32))

    @pl.when(jnp.max(bad) > 0.0)
    def _():
        scale = depth ** (-0.5) * LOG2E

        def safe_step(t, carry):
            at = tile_at(t)
            keys = jnp.concatenate([ref[:, at] for ref in early_keys + (keys_ref,)], axis=0)
            values = jnp.concatenate([ref[:, at] for ref in early_values + (values_ref,)], axis=0)
            right = with_ones(values)
            mixed = jnp.zeros((count, LANES), F32)
            sums = jnp.ones((count, LANES), F32)
            tops = jnp.zeros((count, LANES), F32)
            for j in range(heads):
                mask = head_mask(count, j, depth)
                scores = dot_nt(only(mask, q_ref[:, at]), keys)
                top = jnp.max(scores, axis=-1, keepdims=True) * scale
                shifted = jnp.exp2(scores * scale - top).astype(BF16)
                weights_ref[t * heads + j] = shifted[:, early * count :]
                for index in range(early):
                    part = shifted[:, index * count : (index + 1) * count]
                    safe[index, t * heads + j] = part
                both = dot_nn(shifted, right)
                mixed = jnp.where(mask, both[:, :LANES], mixed)
                sums = jnp.where(mask, both[:, LANES:], sums)
                tops = jnp.where(mask, top, tops)
            finish_tile(t, at, mixed, sums, tops)
            return carry

        lax.fori_loop(0, width // LANES, safe_step, 0)
        pairs = [(safe.at[index], early_weights[index]) for index in range(early)]
        for copy in start_all(pairs, out_sems):
            copy.wait()

    moved = (x_ref[...].astype(F32) + dot_nn(mixed_ref[...], out_w_ref[...])).astype(BF16)
    slots = 2 * count
    leaving = dot_nn(put_ref[...], moved).astype(BF16)
    if chunks == 1:
        sends[0][...] = leaving
    else:
        tail = sends[0].shape[0] - capacity * (width // LANES)
        line = jnp.broadcast_to(at_ref[...], (tail, slots)).astype(BF16)
        for m, send in enumerate(sends):
            part = slice(m * capacity, (m + 1) * capacity)
            for t in range(width // LANES):
                tile = leaving[part, t * LANES : (t + 1) * LANES]
                send[t * capacity : (t + 1) * capacity] = tile
            padding = jnp.zeros((tail, LANES - capacity), BF16)
            send[send.shape[0] - tail :] = jnp.concatenate([line[:, part], padding], axis=1)


def second_early_body(seg_ref, out_w_ref, grad_ref, mixed_grad_ref, bias_ref):
    mixed_grad_ref[...] = dot_nt(grad_ref[...], out_w_ref[...]).astype(BF16)
    bias_ref[...] = jnp.where(column(seg_ref[...]) == seg_ref[...].astype(F32), 0.0, MASKED)


def second_body(chunks, depth, *refs):
    land_ref, gain_ref, w_ref, grad_ref, mixed_grad, bias = refs[:6]
    arrived = refs[6 : 6 + chunks]
    sends = refs[6 + chunks : 6 + 2 * chunks]
    packed, packed_grad = refs[6 + 2 * chunks :]
    count, width = grad_ref.shape
    slots = 2 * count
    size = slots // chunks
    if chunks == 1:
        landing = land_ref[...].astype(F32)
        rows = arrived[0][...]
    else:
        ends = [piece[size * (width // LANES) :].astype(F32)[:1, :size] for piece in arrived]
        landing = jnp.concatenate(ends, axis=1)
        rows = []
        for piece in arrived:
            tiles = [piece[t * size : (t + 1) * size] for t in range(width // LANES)]
            rows.append(jnp.concatenate(tiles, axis=1))
        rows = jnp.concatenate(rows, axis=0)
    place = lax.broadcasted_iota(jnp.int32, (count, slots), 0).astype(F32) == landing
    place = place.astype(F32)
    hilbert = dot_nn(place.astype(BF16), rows).astype(BF16)
    unit, inverse = norm_parts(hilbert)
    packed[...] = dot_nn((unit * gain_ref[...]).astype(BF16), w_ref[...]).astype(BF16)
    scale = depth ** (-0.5)

    tiles = width // LANES
    heads = LANES // depth
    masks = [head_mask(count, j, depth) for j in range(heads)]
    stacked = (heads, count, count)

    def products(t):
        k_tile = packed[:, tile_at(t + tiles)]
        v_tile = packed[:, tile_at(t + 2 * tiles)]
        k_heads = jnp.concatenate([only(mask, k_tile) for mask in masks], axis=0)
        v_heads = jnp.concatenate([only(mask, v_tile) for mask in masks], axis=0)
        scores = dot_nt(k_heads, packed[:, tile_at(t)])
        return scores, dot_nt(v_heads, mixed_grad[:, tile_at(t)])

    def softmax(scores, weight_grad):
        scores = scores.reshape(stacked) * (scale * LOG2E) + bias[...][None]
        weight_grad = weight_grad.reshape(stacked)
        shifted = jnp.exp2(scores - jnp.max(scores, axis=1, keepdims=True))
        inverse = 1.0 / jnp.sum(shifted, axis=1, keepdims=True)
        carried = jnp.sum(shifted * weight_grad, axis=1, keepdims=True) * inverse
        weights = shifted * inverse
        score_grad = (weights * (weight_grad - carried)).astype(BF16)
        return weights.astype(BF16), score_grad

    def gradients(t, weights, score_grad):
        at = tile_at(t)
        k_at, v_at = tile_at(t + tiles), tile_at(t + 2 * tiles)
        k_flipped = flip_tile(packed[:, k_at])
        dk_heads = dot_nn(score_grad.reshape(heads * count, count), packed[:, at])
        dv_heads = dot_nn(weights.reshape(heads * count, count), mixed_grad[:, at])
        dk, dv, dq = dk_heads[:count], dv_heads[:count], []
        for j in range(heads):
            part = slice(j * count, (j + 1) * count)
            dk = jnp.where(masks[j], dk_heads[part], dk)
            dv = jnp.where(masks[j], dv_heads[part], dv)
            dq.append(dot_nn(k_flipped[j * depth : (j + 1) * depth], score_grad[j]))
        dq = jnp.transpose(jnp.concatenate(dq, axis=0))
        packed_grad[:, at] = (dq * scale).astype(BF16)
        packed_grad[:, k_at] = (dk * scale).astype(BF16)
        packed_grad[:, v_at] = dv.astype(BF16)

    ahead = products(0)
    for t in range(tiles):
        now, ahead = ahead, products(t + 1) if t + 1 < tiles else None
        gradients(t, *softmax(*now))
    normed_grad = dot_nt(packed_grad[...], w_ref[...]).astype(BF16)
    path = norm_pull(unit, inverse * gain_ref[...], normed_grad)
    total = grad_ref[...].astype(F32) + path.astype(F32)
    back = lax.broadcasted_iota(jnp.int32, (slots, count), 1).astype(F32) == column(landing)
    returning = dot_nn(back.astype(F32).astype(BF16), total.astype(BF16)).astype(BF16)
    for m, send in enumerate(sends):
        send[...] = returning[m * size : (m + 1) * size]


def queries_body(peers, *refs):
    gain_ref, w_ref, q_ref = refs[:3]
    others = refs[3 : 3 + peers]
    out_ref = refs[3 + peers]
    count, width = q_ref.shape
    out_ref[:count] = q_ref[...]
    for index, other in enumerate(others):
        rows = slice((index + 1) * count, (index + 2) * count)
        normed = norm_rows(other[...], gain_ref[...])
        out_ref[rows] = dot_nn(normed, w_ref[:, :width]).astype(BF16)


def spread(rows, width):
    heads = rows.shape[0]
    pick = lax.broadcasted_iota(jnp.int32, (heads, width), 1) // (width // heads) == (
        lax.broadcasted_iota(jnp.int32, (heads, width), 0)
    )
    return dot_tn(rows, pick.astype(F32).astype(BF16))


def weights_flipped_body(peers, depth, *refs):
    k_ref, queries_ref = refs[:2]
    lse_refs = refs[2 : 3 + peers]
    out_ref = refs[3 + peers]
    scale = depth ** (-0.5) * LOG2E
    heads = LANES // depth
    count = k_ref.shape[0]

    def tile_step(t, carry):
        at = tile_at(t)
        for j in range(heads):
            mask = head_mask(count, j, depth)
            scores = dot_nt(only(mask, k_ref[:, at]), queries_ref[:, at])
            h = t * heads + j
            line = jnp.concatenate([ref[pl.ds(h, 1)] for ref in lse_refs], axis=1)
            out_ref[h] = jnp.exp2(scores * scale - line).astype(BF16)
        return carry

    tile_loop(k_ref.shape[1] // LANES, tile_step, 0)


def home_body(chunks, depth, *refs):
    take_ref, mixed_ref, out_w_ref = refs[:3]
    home = refs[3 : 3 + chunks]
    moved_ref, grad_ref, delta_ref = refs[3 + chunks :]
    count, width = moved_ref.shape
    rows = jnp.concatenate([piece[...] for piece in home], axis=0)
    moved = dot_nn(take_ref[...], rows).astype(BF16)
    moved_ref[...] = moved
    grad = dot_nt(moved, out_w_ref[...]).astype(BF16)
    grad_ref[:count] = grad
    product = grad.astype(F32) * mixed_ref[...].astype(F32)
    high = product.astype(BF16)
    low = (product - high.astype(F32)).astype(BF16)
    heads = width // depth
    pick = lax.broadcasted_iota(jnp.int32, (heads, width), 1) // depth == (
        lax.broadcasted_iota(jnp.int32, (heads, width), 0)
    )
    pick = pick.astype(F32).astype(BF16)
    delta = dot_nt(pick, high) + dot_nt(pick, low)
    delta_ref[...] = delta
    beside = width // count
    tail = heads // beside
    for part in range(beside):
        lines = delta[part * tail : (part + 1) * tail].astype(BF16)
        grad_ref[count:, part * count : (part + 1) * count] = lines


def key_tile(depth, t, v_tile, weights_ref, columns, queries, grads, deltas_ref):
    count = v_tile.shape[0]
    heads = LANES // depth
    dk = jnp.zeros((count, LANES), F32)
    dv = jnp.zeros((count, LANES), F32)
    for j in range(heads):
        h = t * heads + j
        mask = head_mask(count, j, depth)
        weights = weights_ref[h, :, columns]
        weight_grad = dot_nt(only(mask, v_tile), grads)
        delta = deltas_ref[pl.ds(h, 1)]
        score_grad = (weights.astype(F32) * (weight_grad - delta)).astype(BF16)
        dv = jnp.where(mask, dot_nn(weights, grads), dv)
        dk = jnp.where(mask, dot_nn(score_grad, queries), dk)
    return dk, dv


def heads_apart(lines, count):
    wide = lines.astype(F32)
    parts = [wide[:, i * count : (i + 1) * count] for i in range(lines.shape[1] // count)]
    return jnp.concatenate(parts, axis=0)


def query_grad_body(parts, depth, *refs):
    weights_refs, refs = refs[:parts], refs[parts:]
    keys_refs, refs = refs[:parts], refs[parts:]
    values_refs, refs = refs[:parts], refs[parts:]
    inverse_ref, flipped_ref, grad_ref, lines, q_ref, w_ref = refs[:6]
    normed_ref, dk_ref, dv_ref, dq_all, wide = refs[6:]
    count, width = q_ref.shape
    heads = LANES // depth
    high = lines[...].astype(BF16)
    low = (lines[...] - high.astype(F32)).astype(BF16)
    wide[...] = spread(high, width) + spread(low, width)

    def tile_step(t, carry):
        at = tile_at(t)
        g_tile = grad_ref[:count, at]
        delta_tile = wide[:, at]
        keys = jnp.concatenate([ref[:, at] for ref in keys_refs], axis=0)
        values = jnp.concatenate([ref[:, at] for ref in values_refs], axis=0)
        dq = jnp.zeros((count, LANES), F32)
        for j in range(heads):
            mask = head_mask(count, j, depth)
            weight_grad = dot_nt(only(mask, g_tile), values)
            delta = delta_tile[:, j * depth : j * depth + 1]
            weights = jnp.concatenate([ref[t * heads + j] for ref in weights_refs], axis=1)
            score_grad = (weights.astype(F32) * (weight_grad - delta)).astype(BF16)
            dq = jnp.where(mask, dot_nn(score_grad, keys), dq)
        dq_all[:, at] = (dq * (inverse_ref[:, at] * depth ** (-0.5))).astype(BF16)
        dk_ref[:, at], dv_ref[:, at] = key_tile(
            depth,
            t,
            values_refs[0][:, at],
            flipped_ref,
            slice(0, count),
            q_ref[:, at],
            g_tile,
            lines,
        )
        return carry

    tile_loop(width // LANES, tile_step, 0)
    normed_ref[...] = dot_nt(dq_all[...], w_ref[:, :width])


def key_middle_body(index, depth, *refs):
    flipped_ref, v_ref, queries_ref, dk_in_ref, dv_in_ref, grad_ref = refs[:6]
    dk_ref, dv_ref, lines = refs[6:]
    count, width = v_ref.shape
    lines[...] = heads_apart(grad_ref[count:], count)
    rows = slice(index * count, (index + 1) * count)

    def tile_step(t, carry):
        at = tile_at(t)
        dk, dv = key_tile(
            depth,
            t,
            v_ref[:, at],
            flipped_ref,
            rows,
            queries_ref[rows, at],
            grad_ref[:count, at],
            lines,
        )
        dk_ref[:, at] = dk + dk_in_ref[:, at]
        dv_ref[:, at] = dv + dv_in_ref[:, at]
        return carry

    tile_loop(width // LANES, tile_step, 0)


def key_grad_body(early, peers, depth, *refs):
    flipped_ref, v_ref, queries_ref, normed_ref, dk_ref, dv_ref = refs[:6]
    unit_ref, slope_ref, w_ref, moved_ref = refs[6:10]
    others = refs[10 : 11 + peers - early]
    out_ref, packed_grad, grads, lines = refs[11 + peers - early :]
    count, width = unit_ref.shape
    for i, other in enumerate(others):
        rows = slice(i * count, (i + 1) * count)
        grads[rows] = other[:count]
        lines[:, rows] = heads_apart(other[count:], count)

    def tile_step(t, carry):
        at = tile_at(t)
        dk, dv = key_tile(
            depth,
            t,
            v_ref[:, at],
            flipped_ref,
            slice(early * count, (peers + 1) * count),
            queries_ref[early * count :, at],
            grads[:, at],
            lines,
        )
        dk = (dk + dk_ref[:, at]) * depth ** (-0.5)
        packed_grad[:, at] = dk.astype(BF16)
        packed_grad[:, tile_at(t + width // LANES)] = (dv + dv_ref[:, at]).astype(BF16)
        return carry

    tile_loop(width // LANES, tile_step, 0)
    normed_grad = normed_ref[...] + dot_nt(packed_grad[...], w_ref[:, width:])
    path = norm_pull(unit_ref[...], slope_ref[...], normed_grad.astype(BF16))
    out_ref[...] = (moved_ref[...].astype(F32) + path.astype(F32)).astype(BF16)


def single_first(size):
    return sorted(range(1, size), key=lambda step: (step.bit_count(), -step))


def by_xor(array, axis, step):
    size = lax.axis_size(axis)
    return lax.ppermute(array, axis, [(i, i ^ step) for i in range(size)])


def exchange(pieces, axis):
    if len(pieces) == 1:
        size = lax.axis_size(axis)
        stacked = pieces[0].reshape((size, -1) + pieces[0].shape[1:])
        got = lax.all_to_all(stacked, axis, split_axis=0, concat_axis=0, tiled=True)
        return [got.reshape(pieces[0].shape)]
    return [pieces[0]] + [by_xor(pieces[m], axis, m) for m in range(1, len(pieces))]


def shards(
    points, gain_one, qkv_one, out_one, hilbert_pos, gain_two, qkv_two, out_two, segments, out_grad
):
    count, width = points.shape[2:]
    depth = width // HEADS
    tiles = width // LANES
    patch_size = lax.axis_size("patch")
    curve_size = lax.axis_size("curve")
    peers = patch_size - 1
    total = patch_size * count
    slots = 2 * count
    capacity = slots // curve_size
    chunks = curve_size if curve_size <= MOST_PERMUTES else 1
    rows_bf16 = jax.ShapeDtypeStruct((count, width), BF16)
    all_bf16 = jax.ShapeDtypeStruct((total, width), BF16)
    chunk_bf16 = jax.ShapeDtypeStruct((slots // chunks, width), BF16)

    x = points.reshape(count, width)
    steps = single_first(patch_size)
    others = [by_xor(x, "patch", m) for m in steps]
    gain_one = gain_one.reshape(1, width)
    gain_two = gain_two.reshape(1, width)

    def shape(kind, *dims):
        return jax.ShapeDtypeStruct(dims, kind)

    me = lax.axis_index("curve").astype(jnp.int32).reshape(1)
    put, take, leaving_at = vmem_call(
        functools.partial(route_body, chunks, capacity),
        (shape(BF16, slots, count), shape(BF16, count, slots))
        + (shape(jnp.int32 if chunks == 1 else F32, 1, slots),),
        flops=8 << 30,
        moved=16 << 20,
        in_specs=[SMEM_SPEC, VMEM_SPEC],
    )(me, hilbert_pos.reshape(1, count))
    x_then, put, take, leaving_at = lax.optimization_barrier((x, put, take, leaving_at))
    landing = leaving_at
    if chunks == 1:
        landing = lax.all_to_all(
            leaving_at.reshape(curve_size, 1, capacity),
            "curve",
            split_axis=0,
            concat_axis=0,
            tiled=True,
        ).reshape(1, slots)

    rows_f32 = shape(F32, count, width)
    lines_f32 = shape(F32, HEADS, count)
    square = shape(BF16, HEADS, count, count)
    dma = pltpu.SemaphoreType.DMA
    q, k, v, own_weights, sum_mixed, sums, unit, slope = vmem_call(
        functools.partial(prep_body, depth),
        (rows_bf16,) * 3 + (square,) + (rows_f32,) * 4,
        flops=2 << 30,
        moved=4 << 20,
    )(x_then, gain_one, qkv_one)
    early_keys, early_values, early_weights = [k], [v], [own_weights]
    for other in others[: peers - 1]:
        k_next, v_next, weights_next, sum_mixed, sums = vmem_call(
            functools.partial(middle_body, depth),
            (rows_bf16,) * 2 + (square,) + (rows_f32,) * 2,
            flops=2 << 30,
            moved=4 << 20,
        )(other, gain_one, qkv_one, q, sum_mixed, sums)
        early_keys.append(k_next)
        early_values.append(v_next)
        early_weights.append(weights_next)
    early = len(early_keys)
    late = peers + 1 - early
    late_bf16 = shape(BF16, late * count, width)
    embedded = shape(BF16, capacity * tiles + 8, LANES)
    sent = chunk_bf16 if chunks == 1 else embedded
    first_weights = 9 + 2 * early + late
    results = vmem_call(
        functools.partial(forward_body, early, peers, chunks, capacity, depth),
        (late_bf16, late_bf16, shape(BF16, HEADS, count, late * count))
        + (rows_bf16, rows_f32, lines_f32)
        + (square,) * early
        + (sent,) * chunks,
        [
            pltpu.VMEM((early,) + square.shape, BF16),
            dma((early,)),
        ],
        flops=8 << 30,
        moved=8 << 20,
        in_specs=[VMEM_SPEC] * first_weights + [HBM_SPEC] * early,
        out_specs=(VMEM_SPEC,) * 6 + (HBM_SPEC,) * early + (VMEM_SPEC,) * chunks,
        input_output_aliases={first_weights + index: 6 + index for index in range(early)},
    )(
        x,
        gain_one,
        qkv_one,
        out_one,
        put,
        leaving_at,
        q,
        sum_mixed,
        sums,
        *early_keys,
        *early_values,
        *others[early - 1 :],
        *early_weights,
    )
    late_keys, late_values, late_weights, mixed, inverse, lse = results[:6]
    all_weights = list(results[6 : 6 + early]) + [late_weights]
    all_keys, all_values = early_keys + [late_keys], early_values + [late_values]
    arrived = exchange(results[6 + early :], "curve")
    lse_all = [lse] + [by_xor(lse, "patch", m) for m in steps]

    out_grad_then, inverse = lax.optimization_barrier((out_grad, inverse))
    queries_all = vmem_call(
        functools.partial(queries_body, peers),
        all_bf16,
        flops=1 << 29,
        moved=3 << 20,
        in_specs=[VMEM_SPEC] * (3 + peers),
    )(gain_one, qkv_one, q, *others)
    flipped = vmem_call(
        functools.partial(weights_flipped_body, peers, depth),
        shape(BF16, HEADS, count, total),
        flops=4 << 30,
        moved=10 << 20,
    )(k, queries_all, *lse_all)

    second_mixed, bias = vmem_call(
        second_early_body, (rows_bf16, shape(F32, count, count)), flops=1 << 29, moved=1 << 20
    )(segments.reshape(1, count), out_two, out_grad_then.reshape(count, width))
    returning = vmem_call(
        functools.partial(second_body, chunks, depth),
        (chunk_bf16,) * chunks,
        [pltpu.VMEM((count, 3 * width), BF16), pltpu.VMEM((count, 3 * width), BF16)],
        flops=8 << 30,
        moved=4 << 20,
    )(
        landing,
        gain_two,
        qkv_two,
        out_grad_then.reshape(count, width),
        second_mixed,
        bias,
        *arrived,
    )
    home = exchange(returning, "curve")

    moved_grad, grad_own, delta = vmem_call(
        functools.partial(home_body, chunks, depth),
        (rows_bf16, shape(BF16, count + HEADS * count // width, width), lines_f32),
        flops=1 << 29,
        moved=2 << 20,
    )(take, mixed, out_one, *home)
    grads = [by_xor(grad_own, "patch", m) for m in steps]

    normed_grad, key_grad, value_grad = vmem_call(
        functools.partial(query_grad_body, len(all_keys), depth),
        (rows_f32, rows_f32, rows_f32),
        [
            pltpu.VMEM((count, width), BF16),
            pltpu.VMEM((count, width), F32),
        ],
        flops=8 << 30,
        moved=10 << 20,
    )(*all_weights, *all_keys, *all_values, inverse, flipped, grad_own, delta, q, qkv_one)
    for index in range(1, early):
        key_grad, value_grad = vmem_call(
            functools.partial(key_middle_body, index, depth),
            (rows_f32, rows_f32),
            [pltpu.VMEM((HEADS, count), F32)],
            flops=2 << 30,
            moved=4 << 20,
        )(flipped, v, queries_all, key_grad, value_grad, grads[index - 1])
    result = vmem_call(
        functools.partial(key_grad_body, early, peers, depth),
        rows_bf16,
        [
            pltpu.VMEM((count, 2 * width), BF16),
            pltpu.VMEM((late * count, width), BF16),
            pltpu.VMEM((HEADS, late * count), F32),
        ],
        flops=8 << 30,
        moved=14 << 20,
    )(
        flipped,
        v,
        queries_all,
        normed_grad,
        key_grad,
        value_grad,
        unit,
        slope,
        qkv_one,
        moved_grad,
        *grads[early - 1 :],
    )
    return result.reshape(points.shape)


def solution(mesh):
    in_specs = (
        P("curve", "patch", None, None),
        P(),
        P(),
        P(),
        P("curve", "patch", None),
        P(),
        P(),
        P(),
        P("patch", "curve", None),
        P("patch", "curve", None, None),
    )
    out_specs = P("curve", "patch", None, None)

    return jax.shard_map(shards, mesh=mesh, in_specs=in_specs, out_specs=out_specs, check_vma=False)
```

```python
import functools
import math

import jax
import jax.numpy as jnp
from jax import lax
from jax.experimental import pallas as pl
from jax.experimental.pallas import tpu as pltpu
from jax.sharding import PartitionSpec as P


HEADS = 16
EPS = 1e-06
LANES = 128
MASKED = -1e30
MOST_PERMUTES = 16
F32 = jnp.float32
BF16 = jnp.bfloat16
LOG2E = math.log2(math.e)


def dot_nn(left, right):
    return lax.dot_general(left, right, (((1,), (0,)), ((), ())), preferred_element_type=F32)


def dot_nt(left, right):
    return lax.dot_general(left, right, (((1,), (1,)), ((), ())), preferred_element_type=F32)


def dot_tn(left, right):
    return lax.dot_general(left, right, (((0,), (0,)), ((), ())), preferred_element_type=F32)


def norm_parts(rows):
    wide = rows.astype(F32)
    power = jnp.mean(wide * wide, axis=-1, keepdims=True)
    inverse = lax.rsqrt(power + EPS)
    return wide * inverse, inverse


def norm_rows(rows, gain):
    return (norm_parts(rows)[0] * gain).astype(BF16)


def norm_pull(unit, slope, cotangent):
    scaled = cotangent.astype(F32) * slope
    along = jnp.mean(scaled * unit, axis=-1, keepdims=True)
    return (scaled - unit * along).astype(BF16)


def head_mask(rows, index, depth):
    return lax.broadcasted_iota(jnp.int32, (rows, LANES), 1) // depth == index


def only(mask, tile):
    return jnp.where(mask, tile, jnp.zeros_like(tile))


def tile_at(t):
    if isinstance(t, int):
        return slice(t * LANES, (t + 1) * LANES)
    return pl.ds(pl.multiple_of(t * LANES, LANES), LANES)


def tile_loop(tiles, step, carry):
    for t in range(tiles):
        carry = step(t, carry)
    return carry


def vmem_call(body, outs, scratch=(), flops=0, moved=0, **more):
    params = pltpu.CompilerParams(vmem_limit_bytes=24 << 20, **more.pop("params", {}))
    return pl.pallas_call(
        body,
        out_shape=outs,
        scratch_shapes=scratch,
        compiler_params=params,
        cost_estimate=pl.CostEstimate(flops=flops, bytes_accessed=moved, transcendentals=0),
        **more,
    )


HBM_SPEC = pl.BlockSpec(memory_space=pltpu.MemorySpace.HBM)
SMEM_SPEC = pl.BlockSpec(memory_space=pltpu.MemorySpace.SMEM)
VMEM_SPEC = pl.BlockSpec(memory_space=pltpu.MemorySpace.VMEM)
LOW, HIGH = 2.0**-60, 2.0**100


def column(row):
    return jnp.transpose(jnp.broadcast_to(row.astype(F32), (LANES, row.shape[1])))[:, :1]


def start_all(pairs, sems):
    copies = [pltpu.make_async_copy(src, dst, sems.at[i]) for i, (src, dst) in enumerate(pairs)]
    for copy in copies:
        copy.start()
    return copies


def flip_tile(tile):
    return jnp.transpose(tile)


def with_ones(tile):
    return jnp.concatenate([tile, jnp.ones_like(tile)], axis=1)


def unshifted(depth, t, q_tile, k_tile, v_tile, weights_ref):
    count = q_tile.shape[0]
    scale = depth ** (-0.5) * LOG2E
    right = with_ones(v_tile)
    mixed = jnp.zeros((count, LANES), F32)
    sums = jnp.zeros((count, LANES), F32)
    for j in range(LANES // depth):
        mask = head_mask(count, j, depth)
        scores = dot_nt(only(mask, q_tile), k_tile)
        shifted = jnp.exp2(scores * scale).astype(BF16)
        weights_ref[t * (LANES // depth) + j] = shifted
        both = dot_nn(shifted, right)
        mixed = jnp.where(mask, both[:, :LANES], mixed)
        sums = jnp.where(mask, both[:, LANES:], sums)
    return mixed, sums


def route_body(chunks, capacity, me_ref, target_ref, put_ref, take_ref, at_ref):
    count = target_ref.shape[1]
    slots = 2 * count
    target = target_ref[...]
    shift = count.bit_length() - 1
    owner = lax.shift_right_logical(target, jnp.full_like(target, shift))
    offset = target - lax.shift_left(owner, jnp.full_like(target, shift))
    same = column(owner) == owner.astype(F32)
    earlier = lax.broadcasted_iota(jnp.int32, (count, count), 0) < (
        lax.broadcasted_iota(jnp.int32, (count, count), 1)
    )
    ranking = jnp.sum(jnp.where(same & earlier, 1.0, 0.0), axis=0, keepdims=True).astype(jnp.int32)
    lane = owner if chunks == 1 else lax.bitwise_xor(owner, jnp.full_like(owner, me_ref[0]))
    slot = lane * capacity + ranking
    put = lax.broadcasted_iota(jnp.int32, (slots, count), 0) == slot
    put_ref[...] = put.astype(F32).astype(BF16)
    hit = column(slot) == lax.broadcasted_iota(jnp.int32, (count, slots), 1).astype(F32)
    take_ref[...] = hit.astype(F32).astype(BF16)
    at = jnp.sum(jnp.where(hit, column(offset) - count, 0.0), axis=0, keepdims=True) + count
    at_ref[...] = at.astype(at_ref.dtype)


def prep_body(depth, *refs):
    x_ref, gain_ref, w_ref = refs[:3]
    q_ref, k_ref, v_ref, weights_ref, mixed_ref, sums_ref, unit_ref, slope_ref = refs[3:]
    width = x_ref.shape[1]
    unit, inverse = norm_parts(x_ref[...])
    unit_ref[...] = unit
    slope_ref[...] = inverse * gain_ref[...]
    normed = (unit * gain_ref[...]).astype(BF16)
    q_ref[...] = dot_nn(normed, w_ref[:, :width]).astype(BF16)
    k_ref[...] = dot_nn(normed, w_ref[:, width : 2 * width]).astype(BF16)
    v_ref[...] = dot_nn(normed, w_ref[:, 2 * width :]).astype(BF16)

    def tile_step(t, carry):
        at = tile_at(t)
        mixed_ref[:, at], sums_ref[:, at] = unshifted(
            depth, t, q_ref[:, at], k_ref[:, at], v_ref[:, at], weights_ref
        )
        return carry

    tile_loop(width // LANES, tile_step, 0)


def middle_body(depth, *refs):
    x_ref, gain_ref, w_ref, q_ref, mixed_in_ref, sums_in_ref = refs[:6]
    k_ref, v_ref, weights_ref, mixed_ref, sums_ref = refs[6:]
    width = x_ref.shape[1]
    normed = norm_rows(x_ref[...], gain_ref[...])
    k_ref[...] = dot_nn(normed, w_ref[:, width : 2 * width]).astype(BF16)
    v_ref[...] = dot_nn(normed, w_ref[:, 2 * width :]).astype(BF16)

    def tile_step(t, carry):
        at = tile_at(t)
        mixed, sums = unshifted(depth, t, q_ref[:, at], k_ref[:, at], v_ref[:, at], weights_ref)
        mixed_ref[:, at] = mixed + mixed_in_ref[:, at]
        sums_ref[:, at] = sums + sums_in_ref[:, at]
        return carry

    tile_loop(width // LANES, tile_step, 0)


def forward_body(early, peers, chunks, capacity, depth, *refs):
    x_ref, gain_ref, w_ref, out_w_ref, put_ref, at_ref, q_ref, mixed_in_ref, sums_in_ref = refs[:9]
    refs = refs[9:]
    early_keys, early_values, refs = refs[:early], refs[early : 2 * early], refs[2 * early :]
    others, refs = refs[: peers + 1 - early], refs[peers + 1 - early + early :]
    keys_ref, values_ref, weights_ref, mixed_ref, inverse_ref, lse_ref = refs[:6]
    early_weights, refs = refs[6 : 6 + early], refs[6 + early :]
    sends, (mixed_low, safe, out_sems) = refs[:chunks], refs[chunks:]
    count, width = x_ref.shape
    heads = LANES // depth
    for index, other in enumerate(others):
        rows = slice(index * count, (index + 1) * count)
        normed = norm_rows(other[...], gain_ref[...])
        keys_ref[rows] = dot_nn(normed, w_ref[:, width : 2 * width]).astype(BF16)
        values_ref[rows] = dot_nn(normed, w_ref[:, 2 * width :]).astype(BF16)

    def finish_tile(t, at, mixed, sums, tops):
        inverse = 1.0 / sums
        mixed_ref[:, at] = mixed * inverse
        mixed_low[:, at] = (mixed * inverse).astype(BF16)
        inverse_ref[:, at] = inverse
        flipped = flip_tile(tops + jnp.log(sums) * LOG2E)
        for j in range(heads):
            lse_ref[pl.ds(t * heads + j, 1)] = flipped[j * depth : j * depth + 1]

    def fast_step(t, bad):
        at = tile_at(t)
        mixed, sums = unshifted(
            depth, t, q_ref[:, at], keys_ref[:, at], values_ref[:, at], weights_ref
        )
        mixed += mixed_in_ref[:, at]
        sums += sums_in_ref[:, at]
        finish_tile(t, at, mixed, sums, 0.0)
        return jnp.where((sums >= LOW) & (sums <= HIGH), bad, 1.0)

    bad = tile_loop(width // LANES, fast_step, jnp.zeros((count, LANES), F32))

    @pl.when(jnp.max(bad) > 0.0)
    def _():
        scale = depth ** (-0.5) * LOG2E

        def safe_step(t, carry):
            at = tile_at(t)
            keys = jnp.concatenate([ref[:, at] for ref in early_keys + (keys_ref,)], axis=0)
            values = jnp.concatenate([ref[:, at] for ref in early_values + (values_ref,)], axis=0)
            right = with_ones(values)
            mixed = jnp.zeros((count, LANES), F32)
            sums = jnp.ones((count, LANES), F32)
            tops = jnp.zeros((count, LANES), F32)
            for j in range(heads):
                mask = head_mask(count, j, depth)
                scores = dot_nt(only(mask, q_ref[:, at]), keys)
                top = jnp.max(scores, axis=-1, keepdims=True) * scale
                shifted = jnp.exp2(scores * scale - top).astype(BF16)
                weights_ref[t * heads + j] = shifted[:, early * count :]
                for index in range(early):
                    part = shifted[:, index * count : (index + 1) * count]
                    safe[index, t * heads + j] = part
                both = dot_nn(shifted, right)
                mixed = jnp.where(mask, both[:, :LANES], mixed)
                sums = jnp.where(mask, both[:, LANES:], sums)
                tops = jnp.where(mask, top, tops)
            finish_tile(t, at, mixed, sums, tops)
            return carry

        lax.fori_loop(0, width // LANES, safe_step, 0)
        pairs = [(safe.at[index], early_weights[index]) for index in range(early)]
        for copy in start_all(pairs, out_sems):
            copy.wait()

    moved = (x_ref[...].astype(F32) + dot_nn(mixed_low[...], out_w_ref[...])).astype(BF16)
    slots = 2 * count
    leaving = dot_nn(put_ref[...], moved).astype(BF16)
    if chunks == 1:
        sends[0][...] = leaving
    else:
        tail = sends[0].shape[0] - capacity * (width // LANES)
        line = jnp.broadcast_to(at_ref[...], (tail, slots)).astype(BF16)
        for m, send in enumerate(sends):
            part = slice(m * capacity, (m + 1) * capacity)
            for t in range(width // LANES):
                tile = leaving[part, t * LANES : (t + 1) * LANES]
                send[t * capacity : (t + 1) * capacity] = tile
            padding = jnp.zeros((tail, LANES - capacity), BF16)
            send[send.shape[0] - tail :] = jnp.concatenate([line[:, part], padding], axis=1)


def second_early_body(seg_ref, out_w_ref, grad_ref, mixed_grad_ref, bias_ref):
    mixed_grad_ref[...] = dot_nt(grad_ref[...], out_w_ref[...]).astype(BF16)
    bias_ref[...] = jnp.where(column(seg_ref[...]) == seg_ref[...].astype(F32), 0.0, MASKED)


def second_body(chunks, depth, *refs):
    land_ref, gain_ref, w_ref, grad_ref, mixed_grad, bias = refs[:6]
    arrived = refs[6 : 6 + chunks]
    sends = refs[6 + chunks : 6 + 2 * chunks]
    packed, packed_grad = refs[6 + 2 * chunks :]
    count, width = grad_ref.shape
    slots = 2 * count
    size = slots // chunks
    if chunks == 1:
        landing = land_ref[...].astype(F32)
        rows = arrived[0][...]
    else:
        ends = [piece[size * (width // LANES) :].astype(F32)[:1, :size] for piece in arrived]
        landing = jnp.concatenate(ends, axis=1)
        rows = []
        for piece in arrived:
            tiles = [piece[t * size : (t + 1) * size] for t in range(width // LANES)]
            rows.append(jnp.concatenate(tiles, axis=1))
        rows = jnp.concatenate(rows, axis=0)
    place = lax.broadcasted_iota(jnp.int32, (count, slots), 0).astype(F32) == landing
    place = place.astype(F32)
    hilbert = dot_nn(place.astype(BF16), rows).astype(BF16)
    unit, inverse = norm_parts(hilbert)
    packed[...] = dot_nn((unit * gain_ref[...]).astype(BF16), w_ref[...]).astype(BF16)
    scale = depth ** (-0.5)

    tiles = width // LANES
    heads = LANES // depth
    masks = [head_mask(count, j, depth) for j in range(heads)]
    stacked = (heads, count, count)

    def products(t):
        k_tile = packed[:, tile_at(t + tiles)]
        v_tile = packed[:, tile_at(t + 2 * tiles)]
        k_heads = jnp.concatenate([only(mask, k_tile) for mask in masks], axis=0)
        v_heads = jnp.concatenate([only(mask, v_tile) for mask in masks], axis=0)
        scores = dot_nt(k_heads, packed[:, tile_at(t)])
        return scores, dot_nt(v_heads, mixed_grad[:, tile_at(t)])

    def softmax(scores, weight_grad):
        scores = scores.reshape(stacked) * (scale * LOG2E) + bias[...][None]
        weight_grad = weight_grad.reshape(stacked)
        shifted = jnp.exp2(scores - jnp.max(scores, axis=1, keepdims=True))
        inverse = 1.0 / jnp.sum(shifted, axis=1, keepdims=True)
        carried = jnp.sum(shifted * weight_grad, axis=1, keepdims=True) * inverse
        weights = shifted * inverse
        score_grad = (weights * (weight_grad - carried)).astype(BF16)
        return weights.astype(BF16), score_grad

    def gradients(t, weights, score_grad):
        at = tile_at(t)
        k_at, v_at = tile_at(t + tiles), tile_at(t + 2 * tiles)
        k_flipped = flip_tile(packed[:, k_at])
        dk_heads = dot_nn(score_grad.reshape(heads * count, count), packed[:, at])
        dv_heads = dot_nn(weights.reshape(heads * count, count), mixed_grad[:, at])
        dk, dv, dq = dk_heads[:count], dv_heads[:count], []
        for j in range(heads):
            part = slice(j * count, (j + 1) * count)
            dk = jnp.where(masks[j], dk_heads[part], dk)
            dv = jnp.where(masks[j], dv_heads[part], dv)
            dq.append(dot_nn(k_flipped[j * depth : (j + 1) * depth], score_grad[j]))
        dq = jnp.transpose(jnp.concatenate(dq, axis=0))
        packed_grad[:, at] = (dq * scale).astype(BF16)
        packed_grad[:, k_at] = (dk * scale).astype(BF16)
        packed_grad[:, v_at] = dv.astype(BF16)

    ahead = products(0)
    for t in range(tiles):
        now, ahead = ahead, products(t + 1) if t + 1 < tiles else None
        gradients(t, *softmax(*now))
    normed_grad = dot_nt(packed_grad[...], w_ref[...]).astype(BF16)
    path = norm_pull(unit, inverse * gain_ref[...], normed_grad)
    total = grad_ref[...].astype(F32) + path.astype(F32)
    back = lax.broadcasted_iota(jnp.int32, (slots, count), 1).astype(F32) == column(landing)
    returning = dot_nn(back.astype(F32).astype(BF16), total.astype(BF16)).astype(BF16)
    for m, send in enumerate(sends):
        send[...] = returning[m * size : (m + 1) * size]


def queries_body(peers, *refs):
    gain_ref, w_ref, q_ref = refs[:3]
    others = refs[3 : 3 + peers]
    out_ref = refs[3 + peers]
    count, width = q_ref.shape
    out_ref[:count] = q_ref[...]
    for index, other in enumerate(others):
        rows = slice((index + 1) * count, (index + 2) * count)
        normed = norm_rows(other[...], gain_ref[...])
        out_ref[rows] = dot_nn(normed, w_ref[:, :width]).astype(BF16)


def spread(rows, width):
    heads = rows.shape[0]
    pick = lax.broadcasted_iota(jnp.int32, (heads, width), 1) // (width // heads) == (
        lax.broadcasted_iota(jnp.int32, (heads, width), 0)
    )
    return dot_tn(rows, pick.astype(F32).astype(BF16))


def weights_flipped_body(peers, depth, *refs):
    k_ref, queries_ref = refs[:2]
    lse_refs = refs[2 : 3 + peers]
    out_ref = refs[3 + peers]
    scale = depth ** (-0.5) * LOG2E
    heads = LANES // depth
    count = k_ref.shape[0]

    def tile_step(t, carry):
        at = tile_at(t)
        for j in range(heads):
            mask = head_mask(count, j, depth)
            scores = dot_nt(only(mask, k_ref[:, at]), queries_ref[:, at])
            h = t * heads + j
            line = jnp.concatenate([ref[pl.ds(h, 1)] for ref in lse_refs], axis=1)
            out_ref[h] = jnp.exp2(scores * scale - line).astype(BF16)
        return carry

    tile_loop(k_ref.shape[1] // LANES, tile_step, 0)


def home_body(chunks, depth, *refs):
    take_ref, mixed_ref, out_w_ref = refs[:3]
    home = refs[3 : 3 + chunks]
    moved_ref, grad_ref, delta_ref = refs[3 + chunks :]
    count, width = moved_ref.shape
    rows = jnp.concatenate([piece[...] for piece in home], axis=0)
    moved = dot_nn(take_ref[...], rows).astype(BF16)
    moved_ref[...] = moved
    grad = dot_nt(moved, out_w_ref[...]).astype(BF16)
    grad_ref[:count] = grad
    product = grad.astype(F32) * mixed_ref[...]
    high = product.astype(BF16)
    low = (product - high.astype(F32)).astype(BF16)
    heads = width // depth
    pick = lax.broadcasted_iota(jnp.int32, (heads, width), 1) // depth == (
        lax.broadcasted_iota(jnp.int32, (heads, width), 0)
    )
    pick = pick.astype(F32).astype(BF16)
    delta = dot_nt(pick, high) + dot_nt(pick, low)
    delta_ref[...] = delta
    beside = width // count
    tail = heads // beside
    rest = delta
    for term in range(2):
        rounded = rest.astype(BF16)
        rest -= rounded.astype(F32)
        rows = slice(count + term * tail, count + (term + 1) * tail)
        for part in range(beside):
            lines = rounded[part * tail : (part + 1) * tail]
            grad_ref[rows, part * count : (part + 1) * count] = lines


def key_tile(depth, t, v_tile, weights_ref, columns, queries, grads, deltas_ref):
    count = v_tile.shape[0]
    heads = LANES // depth
    dk = jnp.zeros((count, LANES), F32)
    dv = jnp.zeros((count, LANES), F32)
    for j in range(heads):
        h = t * heads + j
        mask = head_mask(count, j, depth)
        weights = weights_ref[h, :, columns]
        weight_grad = dot_nt(only(mask, v_tile), grads)
        delta = deltas_ref[pl.ds(h, 1)]
        score_grad = (weights.astype(F32) * (weight_grad - delta)).astype(BF16)
        dv = jnp.where(mask, dot_nn(weights, grads), dv)
        dk = jnp.where(mask, dot_nn(score_grad, queries), dk)
    return dk, dv


def heads_apart(lines, count):
    wide = lines.astype(F32)
    wide = wide[: wide.shape[0] // 2] + wide[wide.shape[0] // 2 :]
    parts = [wide[:, i * count : (i + 1) * count] for i in range(lines.shape[1] // count)]
    return jnp.concatenate(parts, axis=0)


def query_grad_body(parts, depth, *refs):
    weights_refs, refs = refs[:parts], refs[parts:]
    keys_refs, refs = refs[:parts], refs[parts:]
    values_refs, refs = refs[:parts], refs[parts:]
    inverse_ref, flipped_ref, grad_ref, lines, q_ref, w_ref = refs[:6]
    normed_ref, dk_ref, dv_ref, dq_all, wide = refs[6:]
    count, width = q_ref.shape
    heads = LANES // depth
    high = lines[...].astype(BF16)
    low = (lines[...] - high.astype(F32)).astype(BF16)
    wide[...] = spread(high, width) + spread(low, width)

    def tile_step(t, carry):
        at = tile_at(t)
        g_tile = grad_ref[:count, at]
        delta_tile = wide[:, at]
        keys = jnp.concatenate([ref[:, at] for ref in keys_refs], axis=0)
        values = jnp.concatenate([ref[:, at] for ref in values_refs], axis=0)
        dq = jnp.zeros((count, LANES), F32)
        for j in range(heads):
            mask = head_mask(count, j, depth)
            weight_grad = dot_nt(only(mask, g_tile), values)
            delta = delta_tile[:, j * depth : j * depth + 1]
            weights = jnp.concatenate([ref[t * heads + j] for ref in weights_refs], axis=1)
            score_grad = (weights.astype(F32) * (weight_grad - delta)).astype(BF16)
            dq = jnp.where(mask, dot_nn(score_grad, keys), dq)
        dq_all[:, at] = (dq * (inverse_ref[:, at] * depth ** (-0.5))).astype(BF16)
        dk_ref[:, at], dv_ref[:, at] = key_tile(
            depth,
            t,
            values_refs[0][:, at],
            flipped_ref,
            slice(0, count),
            q_ref[:, at],
            g_tile,
            lines,
        )
        return carry

    tile_loop(width // LANES, tile_step, 0)
    normed_ref[...] = dot_nt(dq_all[...], w_ref[:, :width])


def key_middle_body(index, depth, *refs):
    flipped_ref, v_ref, queries_ref, dk_in_ref, dv_in_ref, grad_ref = refs[:6]
    dk_ref, dv_ref, lines = refs[6:]
    count, width = v_ref.shape
    lines[...] = heads_apart(grad_ref[count:], count)
    rows = slice(index * count, (index + 1) * count)

    def tile_step(t, carry):
        at = tile_at(t)
        dk, dv = key_tile(
            depth,
            t,
            v_ref[:, at],
            flipped_ref,
            rows,
            queries_ref[rows, at],
            grad_ref[:count, at],
            lines,
        )
        dk_ref[:, at] = dk + dk_in_ref[:, at]
        dv_ref[:, at] = dv + dv_in_ref[:, at]
        return carry

    tile_loop(width // LANES, tile_step, 0)


def key_grad_body(early, peers, depth, *refs):
    flipped_ref, v_ref, queries_ref, normed_ref, dk_ref, dv_ref = refs[:6]
    unit_ref, slope_ref, w_ref, moved_ref = refs[6:10]
    others = refs[10 : 11 + peers - early]
    out_ref, packed_grad, grads, lines = refs[11 + peers - early :]
    count, width = unit_ref.shape
    for i, other in enumerate(others):
        rows = slice(i * count, (i + 1) * count)
        grads[rows] = other[:count]
        lines[:, rows] = heads_apart(other[count:], count)

    def tile_step(t, carry):
        at = tile_at(t)
        dk, dv = key_tile(
            depth,
            t,
            v_ref[:, at],
            flipped_ref,
            slice(early * count, (peers + 1) * count),
            queries_ref[early * count :, at],
            grads[:, at],
            lines,
        )
        dk = (dk + dk_ref[:, at]) * depth ** (-0.5)
        packed_grad[:, at] = dk.astype(BF16)
        packed_grad[:, tile_at(t + width // LANES)] = (dv + dv_ref[:, at]).astype(BF16)
        return carry

    tile_loop(width // LANES, tile_step, 0)
    normed_grad = normed_ref[...] + dot_nt(packed_grad[...], w_ref[:, width:])
    path = norm_pull(unit_ref[...], slope_ref[...], normed_grad.astype(BF16))
    out_ref[...] = (moved_ref[...].astype(F32) + path.astype(F32)).astype(BF16)


def single_first(size):
    return sorted(range(1, size), key=lambda step: (step.bit_count(), -step))


def by_xor(array, axis, step):
    size = lax.axis_size(axis)
    return lax.ppermute(array, axis, [(i, i ^ step) for i in range(size)])


def exchange(pieces, axis):
    if len(pieces) == 1:
        size = lax.axis_size(axis)
        stacked = pieces[0].reshape((size, -1) + pieces[0].shape[1:])
        got = lax.all_to_all(stacked, axis, split_axis=0, concat_axis=0, tiled=True)
        return [got.reshape(pieces[0].shape)]
    return [pieces[0]] + [by_xor(pieces[m], axis, m) for m in range(1, len(pieces))]


def shards(
    points, gain_one, qkv_one, out_one, hilbert_pos, gain_two, qkv_two, out_two, segments, out_grad
):
    count, width = points.shape[2:]
    depth = width // HEADS
    tiles = width // LANES
    patch_size = lax.axis_size("patch")
    curve_size = lax.axis_size("curve")
    peers = patch_size - 1
    total = patch_size * count
    slots = 2 * count
    capacity = slots // curve_size
    chunks = curve_size if curve_size <= MOST_PERMUTES else 1
    rows_bf16 = jax.ShapeDtypeStruct((count, width), BF16)
    all_bf16 = jax.ShapeDtypeStruct((total, width), BF16)
    chunk_bf16 = jax.ShapeDtypeStruct((slots // chunks, width), BF16)

    x = points.reshape(count, width)
    steps = single_first(patch_size)
    others = [by_xor(x, "patch", m) for m in steps]
    gain_one = gain_one.reshape(1, width)
    gain_two = gain_two.reshape(1, width)

    def shape(kind, *dims):
        return jax.ShapeDtypeStruct(dims, kind)

    me = lax.axis_index("curve").astype(jnp.int32).reshape(1)
    put, take, leaving_at = vmem_call(
        functools.partial(route_body, chunks, capacity),
        (shape(BF16, slots, count), shape(BF16, count, slots))
        + (shape(jnp.int32 if chunks == 1 else F32, 1, slots),),
        flops=8 << 30,
        moved=16 << 20,
        in_specs=[SMEM_SPEC, VMEM_SPEC],
    )(me, hilbert_pos.reshape(1, count))
    x_then, put, take, leaving_at = lax.optimization_barrier((x, put, take, leaving_at))
    landing = leaving_at
    if chunks == 1:
        landing = lax.all_to_all(
            leaving_at.reshape(curve_size, 1, capacity),
            "curve",
            split_axis=0,
            concat_axis=0,
            tiled=True,
        ).reshape(1, slots)

    rows_f32 = shape(F32, count, width)
    lines_f32 = shape(F32, HEADS, count)
    square = shape(BF16, HEADS, count, count)
    dma = pltpu.SemaphoreType.DMA
    q, k, v, own_weights, sum_mixed, sums, unit, slope = vmem_call(
        functools.partial(prep_body, depth),
        (rows_bf16,) * 3 + (square,) + (rows_f32,) * 4,
        flops=2 << 30,
        moved=4 << 20,
    )(x_then, gain_one, qkv_one)
    early_keys, early_values, early_weights = [k], [v], [own_weights]
    for other in others[: peers - 1]:
        k_next, v_next, weights_next, sum_mixed, sums = vmem_call(
            functools.partial(middle_body, depth),
            (rows_bf16,) * 2 + (square,) + (rows_f32,) * 2,
            flops=2 << 30,
            moved=4 << 20,
        )(other, gain_one, qkv_one, q, sum_mixed, sums)
        early_keys.append(k_next)
        early_values.append(v_next)
        early_weights.append(weights_next)
    early = len(early_keys)
    late = peers + 1 - early
    late_bf16 = shape(BF16, late * count, width)
    embedded = shape(BF16, capacity * tiles + 8, LANES)
    sent = chunk_bf16 if chunks == 1 else embedded
    first_weights = 9 + 2 * early + late
    results = vmem_call(
        functools.partial(forward_body, early, peers, chunks, capacity, depth),
        (late_bf16, late_bf16, shape(BF16, HEADS, count, late * count))
        + (rows_f32, rows_f32, lines_f32)
        + (square,) * early
        + (sent,) * chunks,
        [
            pltpu.VMEM((count, width), BF16),
            pltpu.VMEM((early,) + square.shape, BF16),
            dma((early,)),
        ],
        flops=8 << 30,
        moved=8 << 20,
        in_specs=[VMEM_SPEC] * first_weights + [HBM_SPEC] * early,
        out_specs=(VMEM_SPEC,) * 6 + (HBM_SPEC,) * early + (VMEM_SPEC,) * chunks,
        input_output_aliases={first_weights + index: 6 + index for index in range(early)},
    )(
        x,
        gain_one,
        qkv_one,
        out_one,
        put,
        leaving_at,
        q,
        sum_mixed,
        sums,
        *early_keys,
        *early_values,
        *others[early - 1 :],
        *early_weights,
    )
    late_keys, late_values, late_weights, mixed, inverse, lse = results[:6]
    all_weights = list(results[6 : 6 + early]) + [late_weights]
    all_keys, all_values = early_keys + [late_keys], early_values + [late_values]
    arrived = exchange(results[6 + early :], "curve")
    lse_all = [lse] + [by_xor(lse, "patch", m) for m in steps]

    out_grad_then, inverse = lax.optimization_barrier((out_grad, inverse))
    queries_all = vmem_call(
        functools.partial(queries_body, peers),
        all_bf16,
        flops=1 << 29,
        moved=3 << 20,
        in_specs=[VMEM_SPEC] * (3 + peers),
    )(gain_one, qkv_one, q, *others)
    flipped = vmem_call(
        functools.partial(weights_flipped_body, peers, depth),
        shape(BF16, HEADS, count, total),
        flops=4 << 30,
        moved=10 << 20,
    )(k, queries_all, *lse_all)

    second_mixed, bias = vmem_call(
        second_early_body, (rows_bf16, shape(F32, count, count)), flops=1 << 29, moved=1 << 20
    )(segments.reshape(1, count), out_two, out_grad_then.reshape(count, width))
    returning = vmem_call(
        functools.partial(second_body, chunks, depth),
        (chunk_bf16,) * chunks,
        [pltpu.VMEM((count, 3 * width), BF16), pltpu.VMEM((count, 3 * width), BF16)],
        flops=8 << 30,
        moved=4 << 20,
    )(
        landing,
        gain_two,
        qkv_two,
        out_grad_then.reshape(count, width),
        second_mixed,
        bias,
        *arrived,
    )
    home = exchange(returning, "curve")

    moved_grad, grad_own, delta = vmem_call(
        functools.partial(home_body, chunks, depth),
        (rows_bf16, shape(BF16, count + 2 * HEADS * count // width, width), lines_f32),
        flops=1 << 29,
        moved=2 << 20,
    )(take, mixed, out_one, *home)
    grads = [by_xor(grad_own, "patch", m) for m in steps]

    normed_grad, key_grad, value_grad = vmem_call(
        functools.partial(query_grad_body, len(all_keys), depth),
        (rows_f32, rows_f32, rows_f32),
        [
            pltpu.VMEM((count, width), BF16),
            pltpu.VMEM((count, width), F32),
        ],
        flops=8 << 30,
        moved=10 << 20,
    )(*all_weights, *all_keys, *all_values, inverse, flipped, grad_own, delta, q, qkv_one)
    for index in range(1, early):
        key_grad, value_grad = vmem_call(
            functools.partial(key_middle_body, index, depth),
            (rows_f32, rows_f32),
            [pltpu.VMEM((HEADS, count), F32)],
            flops=2 << 30,
            moved=4 << 20,
        )(flipped, v, queries_all, key_grad, value_grad, grads[index - 1])
    result = vmem_call(
        functools.partial(key_grad_body, early, peers, depth),
        rows_bf16,
        [
            pltpu.VMEM((count, 2 * width), BF16),
            pltpu.VMEM((late * count, width), BF16),
            pltpu.VMEM((HEADS, late * count), F32),
        ],
        flops=8 << 30,
        moved=14 << 20,
    )(
        flipped,
        v,
        queries_all,
        normed_grad,
        key_grad,
        value_grad,
        unit,
        slope,
        qkv_one,
        moved_grad,
        *grads[early - 1 :],
    )
    return result.reshape(points.shape)


def solution(mesh):
    in_specs = (
        P("curve", "patch", None, None),
        P(),
        P(),
        P(),
        P("curve", "patch", None),
        P(),
        P(),
        P(),
        P("patch", "curve", None),
        P("patch", "curve", None, None),
    )
    out_specs = P("curve", "patch", None, None)

    return jax.shard_map(shards, mesh=mesh, in_specs=in_specs, out_specs=out_specs, check_vma=False)
```

```python
import functools
import math

import jax
import jax.numpy as jnp
from jax import lax
from jax.experimental import pallas as pl
from jax.experimental.pallas import tpu as pltpu
from jax.sharding import PartitionSpec as P


HEADS = 16
EPS = 1e-06
LANES = 128
MASKED = -1e30
MOST_PERMUTES = 16
F32 = jnp.float32
BF16 = jnp.bfloat16
LOG2E = math.log2(math.e)


def dot_nn(left, right):
    return lax.dot_general(left, right, (((1,), (0,)), ((), ())), preferred_element_type=F32)


def dot_nt(left, right):
    return lax.dot_general(left, right, (((1,), (1,)), ((), ())), preferred_element_type=F32)


def dot_tn(left, right):
    return lax.dot_general(left, right, (((0,), (0,)), ((), ())), preferred_element_type=F32)


def norm_parts(rows):
    wide = rows.astype(F32)
    power = jnp.mean(wide * wide, axis=-1, keepdims=True)
    inverse = lax.rsqrt(power + EPS)
    return wide * inverse, inverse


def norm_rows(rows, gain):
    return (norm_parts(rows)[0] * gain).astype(BF16)


def norm_pull(unit, slope, cotangent):
    scaled = cotangent.astype(F32) * slope
    along = jnp.mean(scaled * unit, axis=-1, keepdims=True)
    return (scaled - unit * along).astype(BF16)


def head_mask(rows, index, depth):
    return lax.broadcasted_iota(jnp.int32, (rows, LANES), 1) // depth == index


def only(mask, tile):
    return jnp.where(mask, tile, jnp.zeros_like(tile))


def tile_at(t):
    if isinstance(t, int):
        return slice(t * LANES, (t + 1) * LANES)
    return pl.ds(pl.multiple_of(t * LANES, LANES), LANES)


def tile_loop(tiles, step, carry):
    for t in range(tiles):
        carry = step(t, carry)
    return carry


def vmem_call(body, outs, scratch=(), flops=0, moved=0, **more):
    params = pltpu.CompilerParams(vmem_limit_bytes=24 << 20, **more.pop("params", {}))
    return pl.pallas_call(
        body,
        out_shape=outs,
        scratch_shapes=scratch,
        compiler_params=params,
        cost_estimate=pl.CostEstimate(flops=flops, bytes_accessed=moved, transcendentals=0),
        **more,
    )


HBM_SPEC = pl.BlockSpec(memory_space=pltpu.MemorySpace.HBM)
SMEM_SPEC = pl.BlockSpec(memory_space=pltpu.MemorySpace.SMEM)
VMEM_SPEC = pl.BlockSpec(memory_space=pltpu.MemorySpace.VMEM)
LOW, HIGH = 2.0**-60, 2.0**100


def column(row):
    return jnp.transpose(jnp.broadcast_to(row.astype(F32), (LANES, row.shape[1])))[:, :1]


def start_all(pairs, sems):
    copies = [pltpu.make_async_copy(src, dst, sems.at[i]) for i, (src, dst) in enumerate(pairs)]
    for copy in copies:
        copy.start()
    return copies


def flip_tile(tile):
    return jnp.transpose(tile)


def with_ones(tile):
    return jnp.concatenate([tile, jnp.ones_like(tile)], axis=1)


def unshifted(depth, t, q_tile, k_tile, v_tile, weights_ref):
    count = q_tile.shape[0]
    scale = depth ** (-0.5) * LOG2E
    right = with_ones(v_tile)
    mixed = jnp.zeros((count, LANES), F32)
    sums = jnp.zeros((count, LANES), F32)
    for j in range(LANES // depth):
        mask = head_mask(count, j, depth)
        scores = dot_nt(only(mask, q_tile), k_tile)
        shifted = jnp.exp2(scores * scale).astype(BF16)
        weights_ref[t * (LANES // depth) + j] = shifted
        both = dot_nn(shifted, right)
        mixed = jnp.where(mask, both[:, :LANES], mixed)
        sums = jnp.where(mask, both[:, LANES:], sums)
    return mixed, sums


def route_body(chunks, capacity, me_ref, target_ref, put_ref, take_ref, at_ref):
    count = target_ref.shape[1]
    slots = 2 * count
    target = target_ref[...]
    shift = count.bit_length() - 1
    owner = lax.shift_right_logical(target, jnp.full_like(target, shift))
    offset = target - lax.shift_left(owner, jnp.full_like(target, shift))
    same = column(owner) == owner.astype(F32)
    earlier = lax.broadcasted_iota(jnp.int32, (count, count), 0) < (
        lax.broadcasted_iota(jnp.int32, (count, count), 1)
    )
    ranking = jnp.sum(jnp.where(same & earlier, 1.0, 0.0), axis=0, keepdims=True).astype(jnp.int32)
    lane = owner if chunks == 1 else lax.bitwise_xor(owner, jnp.full_like(owner, me_ref[0]))
    slot = lane * capacity + ranking
    put = lax.broadcasted_iota(jnp.int32, (slots, count), 0) == slot
    put_ref[...] = put.astype(F32).astype(BF16)
    hit = column(slot) == lax.broadcasted_iota(jnp.int32, (count, slots), 1).astype(F32)
    take_ref[...] = hit.astype(F32).astype(BF16)
    at = jnp.sum(jnp.where(hit, column(offset) - count, 0.0), axis=0, keepdims=True) + count
    at_ref[...] = at.astype(at_ref.dtype)


def prep_body(depth, *refs):
    x_ref, gain_ref, w_ref = refs[:3]
    q_ref, k_ref, v_ref, weights_ref, mixed_ref, sums_ref, unit_ref, slope_ref = refs[3:]
    width = x_ref.shape[1]
    unit, inverse = norm_parts(x_ref[...])
    unit_ref[...] = unit
    slope_ref[...] = inverse * gain_ref[...]
    normed = (unit * gain_ref[...]).astype(BF16)
    q_ref[...] = dot_nn(normed, w_ref[:, :width]).astype(BF16)
    k_ref[...] = dot_nn(normed, w_ref[:, width : 2 * width]).astype(BF16)
    v_ref[...] = dot_nn(normed, w_ref[:, 2 * width :]).astype(BF16)

    def tile_step(t, carry):
        at = tile_at(t)
        mixed_ref[:, at], sums_ref[:, at] = unshifted(
            depth, t, q_ref[:, at], k_ref[:, at], v_ref[:, at], weights_ref
        )
        return carry

    tile_loop(width // LANES, tile_step, 0)


def middle_body(depth, *refs):
    x_ref, gain_ref, w_ref, q_ref, mixed_in_ref, sums_in_ref = refs[:6]
    k_ref, v_ref, weights_ref, mixed_ref, sums_ref = refs[6:]
    width = x_ref.shape[1]
    normed = norm_rows(x_ref[...], gain_ref[...])
    k_ref[...] = dot_nn(normed, w_ref[:, width : 2 * width]).astype(BF16)
    v_ref[...] = dot_nn(normed, w_ref[:, 2 * width :]).astype(BF16)

    def tile_step(t, carry):
        at = tile_at(t)
        mixed, sums = unshifted(depth, t, q_ref[:, at], k_ref[:, at], v_ref[:, at], weights_ref)
        mixed_ref[:, at] = mixed + mixed_in_ref[:, at]
        sums_ref[:, at] = sums + sums_in_ref[:, at]
        return carry

    tile_loop(width // LANES, tile_step, 0)


def forward_body(early, peers, chunks, capacity, depth, *refs):
    x_ref, gain_ref, w_ref, out_w_ref, put_ref, at_ref, q_ref, mixed_in_ref, sums_in_ref = refs[:9]
    refs = refs[9:]
    early_keys, early_values, refs = refs[:early], refs[early : 2 * early], refs[2 * early :]
    others, refs = refs[: peers + 1 - early], refs[peers + 1 - early + early :]
    keys_ref, values_ref, weights_ref, mixed_ref, inverse_ref, lse_ref = refs[:6]
    early_weights, refs = refs[6 : 6 + early], refs[6 + early :]
    sends, (mixed_low, safe, out_sems) = refs[:chunks], refs[chunks:]
    count, width = x_ref.shape
    heads = LANES // depth
    for index, other in enumerate(others):
        rows = slice(index * count, (index + 1) * count)
        normed = norm_rows(other[...], gain_ref[...])
        keys_ref[rows] = dot_nn(normed, w_ref[:, width : 2 * width]).astype(BF16)
        values_ref[rows] = dot_nn(normed, w_ref[:, 2 * width :]).astype(BF16)

    def finish_tile(t, at, mixed, sums, tops):
        inverse = 1.0 / sums
        mixed_ref[:, at] = mixed * inverse
        mixed_low[:, at] = (mixed * inverse).astype(BF16)
        inverse_ref[:, at] = inverse
        flipped = flip_tile(tops + jnp.log(sums) * LOG2E)
        for j in range(heads):
            lse_ref[pl.ds(t * heads + j, 1)] = flipped[j * depth : j * depth + 1]

    def fast_step(t, bad):
        at = tile_at(t)
        mixed, sums = unshifted(
            depth, t, q_ref[:, at], keys_ref[:, at], values_ref[:, at], weights_ref
        )
        mixed += mixed_in_ref[:, at]
        sums += sums_in_ref[:, at]
        finish_tile(t, at, mixed, sums, 0.0)
        return jnp.where((sums >= LOW) & (sums <= HIGH), bad, 1.0)

    bad = tile_loop(width // LANES, fast_step, jnp.zeros((count, LANES), F32))

    @pl.when(jnp.max(bad) > 0.0)
    def _():
        scale = depth ** (-0.5) * LOG2E

        def safe_step(t, carry):
            at = tile_at(t)
            keys = jnp.concatenate([ref[:, at] for ref in early_keys + (keys_ref,)], axis=0)
            values = jnp.concatenate([ref[:, at] for ref in early_values + (values_ref,)], axis=0)
            right = with_ones(values)
            mixed = jnp.zeros((count, LANES), F32)
            sums = jnp.ones((count, LANES), F32)
            tops = jnp.zeros((count, LANES), F32)
            for j in range(heads):
                mask = head_mask(count, j, depth)
                scores = dot_nt(only(mask, q_ref[:, at]), keys)
                top = jnp.max(scores, axis=-1, keepdims=True) * scale
                shifted = jnp.exp2(scores * scale - top).astype(BF16)
                weights_ref[t * heads + j] = shifted[:, early * count :]
                for index in range(early):
                    part = shifted[:, index * count : (index + 1) * count]
                    safe[index, t * heads + j] = part
                both = dot_nn(shifted, right)
                mixed = jnp.where(mask, both[:, :LANES], mixed)
                sums = jnp.where(mask, both[:, LANES:], sums)
                tops = jnp.where(mask, top, tops)
            finish_tile(t, at, mixed, sums, tops)
            return carry

        lax.fori_loop(0, width // LANES, safe_step, 0)
        pairs = [(safe.at[index], early_weights[index]) for index in range(early)]
        for copy in start_all(pairs, out_sems):
            copy.wait()

    moved = (x_ref[...].astype(F32) + dot_nn(mixed_low[...], out_w_ref[...])).astype(BF16)
    slots = 2 * count
    leaving = dot_nn(put_ref[...], moved).astype(BF16)
    if chunks == 1:
        sends[0][...] = leaving
    else:
        tail = sends[0].shape[0] - capacity * (width // LANES)
        line = jnp.broadcast_to(at_ref[...], (tail, slots)).astype(BF16)
        for m, send in enumerate(sends):
            part = slice(m * capacity, (m + 1) * capacity)
            for t in range(width // LANES):
                tile = leaving[part, t * LANES : (t + 1) * LANES]
                send[t * capacity : (t + 1) * capacity] = tile
            padding = jnp.zeros((tail, LANES - capacity), BF16)
            send[send.shape[0] - tail :] = jnp.concatenate([line[:, part], padding], axis=1)


def second_early_body(seg_ref, out_w_ref, grad_ref, mixed_grad_ref, bias_ref):
    mixed_grad_ref[...] = dot_nt(grad_ref[...], out_w_ref[...]).astype(BF16)
    bias_ref[...] = jnp.where(column(seg_ref[...]) == seg_ref[...].astype(F32), 0.0, MASKED)


def second_body(chunks, depth, *refs):
    land_ref, gain_ref, w_ref, grad_ref, mixed_grad, bias = refs[:6]
    arrived = refs[6 : 6 + chunks]
    sends = refs[6 + chunks : 6 + 2 * chunks]
    packed, packed_grad = refs[6 + 2 * chunks :]
    count, width = grad_ref.shape
    slots = 2 * count
    size = slots // chunks
    if chunks == 1:
        landing = land_ref[...].astype(F32)
        rows = arrived[0][...]
    else:
        ends = [piece[size * (width // LANES) :].astype(F32)[:1, :size] for piece in arrived]
        landing = jnp.concatenate(ends, axis=1)
        rows = []
        for piece in arrived:
            tiles = [piece[t * size : (t + 1) * size] for t in range(width // LANES)]
            rows.append(jnp.concatenate(tiles, axis=1))
        rows = jnp.concatenate(rows, axis=0)
    place = lax.broadcasted_iota(jnp.int32, (count, slots), 0).astype(F32) == landing
    place = place.astype(F32)
    hilbert = dot_nn(place.astype(BF16), rows).astype(BF16)
    unit, inverse = norm_parts(hilbert)
    packed[...] = dot_nn((unit * gain_ref[...]).astype(BF16), w_ref[...]).astype(BF16)
    scale = depth ** (-0.5)

    tiles = width // LANES
    heads = LANES // depth
    masks = [head_mask(count, j, depth) for j in range(heads)]
    stacked = (heads, count, count)

    def products(t):
        k_tile = packed[:, tile_at(t + tiles)]
        v_tile = packed[:, tile_at(t + 2 * tiles)]
        k_heads = jnp.concatenate([only(mask, k_tile) for mask in masks], axis=0)
        v_heads = jnp.concatenate([only(mask, v_tile) for mask in masks], axis=0)
        scores = dot_nt(k_heads, packed[:, tile_at(t)])
        return scores, dot_nt(v_heads, mixed_grad[:, tile_at(t)])

    def softmax(scores, weight_grad):
        scores = scores.reshape(stacked) * (scale * LOG2E) + bias[...][None]
        weight_grad = weight_grad.reshape(stacked)
        shifted = jnp.exp2(scores - jnp.max(scores, axis=1, keepdims=True))
        inverse = 1.0 / jnp.sum(shifted, axis=1, keepdims=True)
        carried = jnp.sum(shifted * weight_grad, axis=1, keepdims=True) * inverse
        weights = shifted * inverse
        score_grad = (weights * (weight_grad - carried)).astype(BF16)
        return weights.astype(BF16), score_grad

    def gradients(t, weights, score_grad):
        at = tile_at(t)
        k_at, v_at = tile_at(t + tiles), tile_at(t + 2 * tiles)
        k_flipped = flip_tile(packed[:, k_at])
        dk_heads = dot_nn(score_grad.reshape(heads * count, count), packed[:, at])
        dv_heads = dot_nn(weights.reshape(heads * count, count), mixed_grad[:, at])
        dk, dv, dq = dk_heads[:count], dv_heads[:count], []
        for j in range(heads):
            part = slice(j * count, (j + 1) * count)
            dk = jnp.where(masks[j], dk_heads[part], dk)
            dv = jnp.where(masks[j], dv_heads[part], dv)
            dq.append(dot_nn(k_flipped[j * depth : (j + 1) * depth], score_grad[j]))
        dq = jnp.transpose(jnp.concatenate(dq, axis=0))
        packed_grad[:, at] = (dq * scale).astype(BF16)
        packed_grad[:, k_at] = (dk * scale).astype(BF16)
        packed_grad[:, v_at] = dv.astype(BF16)

    ahead = products(0)
    for t in range(tiles):
        now, ahead = ahead, products(t + 1) if t + 1 < tiles else None
        gradients(t, *softmax(*now))
    normed_grad = dot_nt(packed_grad[...], w_ref[...]).astype(BF16)
    path = norm_pull(unit, inverse * gain_ref[...], normed_grad)
    total = grad_ref[...].astype(F32) + path.astype(F32)
    back = lax.broadcasted_iota(jnp.int32, (slots, count), 1).astype(F32) == column(landing)
    returning = dot_nn(back.astype(F32).astype(BF16), total.astype(BF16)).astype(BF16)
    for m, send in enumerate(sends):
        send[...] = returning[m * size : (m + 1) * size]


def queries_body(peers, *refs):
    gain_ref, w_ref, q_ref = refs[:3]
    others = refs[3 : 3 + peers]
    out_ref = refs[3 + peers]
    count, width = q_ref.shape
    out_ref[:count] = q_ref[...]
    for index, other in enumerate(others):
        rows = slice((index + 1) * count, (index + 2) * count)
        normed = norm_rows(other[...], gain_ref[...])
        out_ref[rows] = dot_nn(normed, w_ref[:, :width]).astype(BF16)


def spread(rows, width):
    heads = rows.shape[0]
    pick = lax.broadcasted_iota(jnp.int32, (heads, width), 1) // (width // heads) == (
        lax.broadcasted_iota(jnp.int32, (heads, width), 0)
    )
    return dot_tn(rows, pick.astype(F32).astype(BF16))


def weights_flipped_body(peers, depth, *refs):
    k_ref, queries_ref = refs[:2]
    lse_refs = refs[2 : 3 + peers]
    out_ref = refs[3 + peers]
    scale = depth ** (-0.5) * LOG2E
    heads = LANES // depth
    count = k_ref.shape[0]

    def tile_step(t, carry):
        at = tile_at(t)
        for j in range(heads):
            mask = head_mask(count, j, depth)
            scores = dot_nt(only(mask, k_ref[:, at]), queries_ref[:, at])
            h = t * heads + j
            line = jnp.concatenate([ref[pl.ds(h, 1)] for ref in lse_refs], axis=1)
            out_ref[h] = jnp.exp2(scores * scale - line).astype(BF16)
        return carry

    tile_loop(k_ref.shape[1] // LANES, tile_step, 0)


def home_body(chunks, depth, *refs):
    take_ref, mixed_ref, out_w_ref = refs[:3]
    home = refs[3 : 3 + chunks]
    moved_ref, grad_ref, delta_ref = refs[3 + chunks :]
    count, width = moved_ref.shape
    rows = jnp.concatenate([piece[...] for piece in home], axis=0)
    moved = dot_nn(take_ref[...], rows).astype(BF16)
    moved_ref[...] = moved
    grad = dot_nt(moved, out_w_ref[...]).astype(BF16)
    grad_ref[:count] = grad
    product = grad.astype(F32) * mixed_ref[...]
    high = product.astype(BF16)
    low = (product - high.astype(F32)).astype(BF16)
    heads = width // depth
    pick = lax.broadcasted_iota(jnp.int32, (heads, width), 1) // depth == (
        lax.broadcasted_iota(jnp.int32, (heads, width), 0)
    )
    pick = pick.astype(F32).astype(BF16)
    delta = dot_nt(pick, high) + dot_nt(pick, low)
    delta_ref[...] = delta
    beside = width // count
    tail = heads // beside
    rest = delta
    for term in range(2):
        rounded = rest.astype(BF16)
        rest -= rounded.astype(F32)
        rows = slice(count + term * tail, count + (term + 1) * tail)
        for part in range(beside):
            lines = rounded[part * tail : (part + 1) * tail]
            grad_ref[rows, part * count : (part + 1) * count] = lines


def key_tile(depth, t, v_tile, weights_ref, columns, queries, grads, deltas_ref):
    count = v_tile.shape[0]
    heads = LANES // depth
    masks = [head_mask(count, j, depth) for j in range(heads)]
    v_heads = jnp.concatenate([only(mask, v_tile) for mask in masks], axis=0)
    weights = weights_ref[t * heads : (t + 1) * heads, :, columns]
    weight_grad = dot_nt(v_heads, grads).reshape(weights.shape)
    delta = deltas_ref[t * heads : (t + 1) * heads][:, None, :]
    score_grad = (weights.astype(F32) * (weight_grad - delta)).astype(BF16)
    dv_heads = dot_nn(weights.reshape(heads * count, -1), grads)
    dk_heads = dot_nn(score_grad.reshape(heads * count, -1), queries)
    dk, dv = dk_heads[:count], dv_heads[:count]
    for j in range(1, heads):
        part = slice(j * count, (j + 1) * count)
        dk = jnp.where(masks[j], dk_heads[part], dk)
        dv = jnp.where(masks[j], dv_heads[part], dv)
    return dk, dv


def heads_apart(lines, count):
    wide = lines.astype(F32)
    wide = wide[: wide.shape[0] // 2] + wide[wide.shape[0] // 2 :]
    parts = [wide[:, i * count : (i + 1) * count] for i in range(lines.shape[1] // count)]
    return jnp.concatenate(parts, axis=0)


def query_grad_body(parts, depth, *refs):
    weights_refs, refs = refs[:parts], refs[parts:]
    keys_refs, refs = refs[:parts], refs[parts:]
    values_refs, refs = refs[:parts], refs[parts:]
    inverse_ref, flipped_ref, grad_ref, lines, q_ref, w_ref = refs[:6]
    normed_ref, dk_ref, dv_ref, dq_all, wide = refs[6:]
    count, width = q_ref.shape
    heads = LANES // depth
    high = lines[...].astype(BF16)
    low = (lines[...] - high.astype(F32)).astype(BF16)
    wide[...] = spread(high, width) + spread(low, width)

    def tile_step(t, carry):
        at = tile_at(t)
        g_tile = grad_ref[:count, at]
        delta_tile = wide[:, at]
        keys = jnp.concatenate([ref[:, at] for ref in keys_refs], axis=0)
        values = jnp.concatenate([ref[:, at] for ref in values_refs], axis=0)
        dq = jnp.zeros((count, LANES), F32)
        for j in range(heads):
            mask = head_mask(count, j, depth)
            weight_grad = dot_nt(only(mask, g_tile), values)
            delta = delta_tile[:, j * depth : j * depth + 1]
            weights = jnp.concatenate([ref[t * heads + j] for ref in weights_refs], axis=1)
            score_grad = (weights.astype(F32) * (weight_grad - delta)).astype(BF16)
            dq = jnp.where(mask, dot_nn(score_grad, keys), dq)
        dq_all[:, at] = (dq * (inverse_ref[:, at] * depth ** (-0.5))).astype(BF16)
        dk_ref[:, at], dv_ref[:, at] = key_tile(
            depth,
            t,
            values_refs[0][:, at],
            flipped_ref,
            slice(0, count),
            q_ref[:, at],
            g_tile,
            lines,
        )
        return carry

    tile_loop(width // LANES, tile_step, 0)
    normed_ref[...] = dot_nt(dq_all[...], w_ref[:, :width])


def key_middle_body(index, depth, *refs):
    flipped_ref, v_ref, queries_ref, dk_in_ref, dv_in_ref, grad_ref = refs[:6]
    dk_ref, dv_ref, lines = refs[6:]
    count, width = v_ref.shape
    lines[...] = heads_apart(grad_ref[count:], count)
    rows = slice(index * count, (index + 1) * count)

    def tile_step(t, carry):
        at = tile_at(t)
        dk, dv = key_tile(
            depth,
            t,
            v_ref[:, at],
            flipped_ref,
            rows,
            queries_ref[rows, at],
            grad_ref[:count, at],
            lines,
        )
        dk_ref[:, at] = dk + dk_in_ref[:, at]
        dv_ref[:, at] = dv + dv_in_ref[:, at]
        return carry

    tile_loop(width // LANES, tile_step, 0)


def key_grad_body(early, peers, depth, *refs):
    flipped_ref, v_ref, queries_ref, normed_ref, dk_ref, dv_ref = refs[:6]
    unit_ref, slope_ref, w_ref, moved_ref = refs[6:10]
    others = refs[10 : 11 + peers - early]
    out_ref, packed_grad, grads, lines = refs[11 + peers - early :]
    count, width = unit_ref.shape
    for i, other in enumerate(others):
        rows = slice(i * count, (i + 1) * count)
        grads[rows] = other[:count]
        lines[:, rows] = heads_apart(other[count:], count)

    def tile_step(t, carry):
        at = tile_at(t)
        dk, dv = key_tile(
            depth,
            t,
            v_ref[:, at],
            flipped_ref,
            slice(early * count, (peers + 1) * count),
            queries_ref[early * count :, at],
            grads[:, at],
            lines,
        )
        dk = (dk + dk_ref[:, at]) * depth ** (-0.5)
        packed_grad[:, at] = dk.astype(BF16)
        packed_grad[:, tile_at(t + width // LANES)] = (dv + dv_ref[:, at]).astype(BF16)
        return carry

    tile_loop(width // LANES, tile_step, 0)
    normed_grad = normed_ref[...] + dot_nt(packed_grad[...], w_ref[:, width:])
    path = norm_pull(unit_ref[...], slope_ref[...], normed_grad.astype(BF16))
    out_ref[...] = (moved_ref[...].astype(F32) + path.astype(F32)).astype(BF16)


def single_first(size):
    return sorted(range(1, size), key=lambda step: (step.bit_count(), -step))


def by_xor(array, axis, step):
    size = lax.axis_size(axis)
    return lax.ppermute(array, axis, [(i, i ^ step) for i in range(size)])


def exchange(pieces, axis):
    if len(pieces) == 1:
        size = lax.axis_size(axis)
        stacked = pieces[0].reshape((size, -1) + pieces[0].shape[1:])
        got = lax.all_to_all(stacked, axis, split_axis=0, concat_axis=0, tiled=True)
        return [got.reshape(pieces[0].shape)]
    return [pieces[0]] + [by_xor(pieces[m], axis, m) for m in range(1, len(pieces))]


def shards(
    points, gain_one, qkv_one, out_one, hilbert_pos, gain_two, qkv_two, out_two, segments, out_grad
):
    count, width = points.shape[2:]
    depth = width // HEADS
    tiles = width // LANES
    patch_size = lax.axis_size("patch")
    curve_size = lax.axis_size("curve")
    peers = patch_size - 1
    total = patch_size * count
    slots = 2 * count
    capacity = slots // curve_size
    chunks = curve_size if curve_size <= MOST_PERMUTES else 1
    rows_bf16 = jax.ShapeDtypeStruct((count, width), BF16)
    all_bf16 = jax.ShapeDtypeStruct((total, width), BF16)
    chunk_bf16 = jax.ShapeDtypeStruct((slots // chunks, width), BF16)

    x = points.reshape(count, width)
    steps = single_first(patch_size)
    others = [by_xor(x, "patch", m) for m in steps]
    gain_one = gain_one.reshape(1, width)
    gain_two = gain_two.reshape(1, width)

    def shape(kind, *dims):
        return jax.ShapeDtypeStruct(dims, kind)

    me = lax.axis_index("curve").astype(jnp.int32).reshape(1)
    put, take, leaving_at = vmem_call(
        functools.partial(route_body, chunks, capacity),
        (shape(BF16, slots, count), shape(BF16, count, slots))
        + (shape(jnp.int32 if chunks == 1 else F32, 1, slots),),
        flops=8 << 30,
        moved=16 << 20,
        in_specs=[SMEM_SPEC, VMEM_SPEC],
    )(me, hilbert_pos.reshape(1, count))
    x_then, put, take, leaving_at = lax.optimization_barrier((x, put, take, leaving_at))
    landing = leaving_at
    if chunks == 1:
        landing = lax.all_to_all(
            leaving_at.reshape(curve_size, 1, capacity),
            "curve",
            split_axis=0,
            concat_axis=0,
            tiled=True,
        ).reshape(1, slots)

    rows_f32 = shape(F32, count, width)
    lines_f32 = shape(F32, HEADS, count)
    square = shape(BF16, HEADS, count, count)
    dma = pltpu.SemaphoreType.DMA
    q, k, v, own_weights, sum_mixed, sums, unit, slope = vmem_call(
        functools.partial(prep_body, depth),
        (rows_bf16,) * 3 + (square,) + (rows_f32,) * 4,
        flops=2 << 30,
        moved=4 << 20,
    )(x_then, gain_one, qkv_one)
    early_keys, early_values, early_weights = [k], [v], [own_weights]
    for other in others[: peers - 1]:
        k_next, v_next, weights_next, sum_mixed, sums = vmem_call(
            functools.partial(middle_body, depth),
            (rows_bf16,) * 2 + (square,) + (rows_f32,) * 2,
            flops=2 << 30,
            moved=4 << 20,
        )(other, gain_one, qkv_one, q, sum_mixed, sums)
        early_keys.append(k_next)
        early_values.append(v_next)
        early_weights.append(weights_next)
    early = len(early_keys)
    late = peers + 1 - early
    late_bf16 = shape(BF16, late * count, width)
    embedded = shape(BF16, capacity * tiles + 8, LANES)
    sent = chunk_bf16 if chunks == 1 else embedded
    first_weights = 9 + 2 * early + late
    results = vmem_call(
        functools.partial(forward_body, early, peers, chunks, capacity, depth),
        (late_bf16, late_bf16, shape(BF16, HEADS, count, late * count))
        + (rows_f32, rows_f32, lines_f32)
        + (square,) * early
        + (sent,) * chunks,
        [
            pltpu.VMEM((count, width), BF16),
            pltpu.VMEM((early,) + square.shape, BF16),
            dma((early,)),
        ],
        flops=8 << 30,
        moved=8 << 20,
        in_specs=[VMEM_SPEC] * first_weights + [HBM_SPEC] * early,
        out_specs=(VMEM_SPEC,) * 6 + (HBM_SPEC,) * early + (VMEM_SPEC,) * chunks,
        input_output_aliases={first_weights + index: 6 + index for index in range(early)},
    )(
        x,
        gain_one,
        qkv_one,
        out_one,
        put,
        leaving_at,
        q,
        sum_mixed,
        sums,
        *early_keys,
        *early_values,
        *others[early - 1 :],
        *early_weights,
    )
    late_keys, late_values, late_weights, mixed, inverse, lse = results[:6]
    all_weights = list(results[6 : 6 + early]) + [late_weights]
    all_keys, all_values = early_keys + [late_keys], early_values + [late_values]
    arrived = exchange(results[6 + early :], "curve")
    lse_all = [lse] + [by_xor(lse, "patch", m) for m in steps]

    out_grad_then, inverse = lax.optimization_barrier((out_grad, inverse))
    queries_all = vmem_call(
        functools.partial(queries_body, peers),
        all_bf16,
        flops=1 << 29,
        moved=3 << 20,
        in_specs=[VMEM_SPEC] * (3 + peers),
    )(gain_one, qkv_one, q, *others)
    flipped = vmem_call(
        functools.partial(weights_flipped_body, peers, depth),
        shape(BF16, HEADS, count, total),
        flops=4 << 30,
        moved=10 << 20,
    )(k, queries_all, *lse_all)

    second_mixed, bias = vmem_call(
        second_early_body, (rows_bf16, shape(F32, count, count)), flops=1 << 29, moved=1 << 20
    )(segments.reshape(1, count), out_two, out_grad_then.reshape(count, width))
    returning = vmem_call(
        functools.partial(second_body, chunks, depth),
        (chunk_bf16,) * chunks,
        [pltpu.VMEM((count, 3 * width), BF16), pltpu.VMEM((count, 3 * width), BF16)],
        flops=8 << 30,
        moved=4 << 20,
    )(
        landing,
        gain_two,
        qkv_two,
        out_grad_then.reshape(count, width),
        second_mixed,
        bias,
        *arrived,
    )
    home = exchange(returning, "curve")

    moved_grad, grad_own, delta = vmem_call(
        functools.partial(home_body, chunks, depth),
        (rows_bf16, shape(BF16, count + 2 * HEADS * count // width, width), lines_f32),
        flops=1 << 29,
        moved=2 << 20,
    )(take, mixed, out_one, *home)
    grads = [by_xor(grad_own, "patch", m) for m in steps]

    normed_grad, key_grad, value_grad = vmem_call(
        functools.partial(query_grad_body, len(all_keys), depth),
        (rows_f32, rows_f32, rows_f32),
        [
            pltpu.VMEM((count, width), BF16),
            pltpu.VMEM((count, width), F32),
        ],
        flops=8 << 30,
        moved=10 << 20,
    )(*all_weights, *all_keys, *all_values, inverse, flipped, grad_own, delta, q, qkv_one)
    for index in range(1, early):
        key_grad, value_grad = vmem_call(
            functools.partial(key_middle_body, index, depth),
            (rows_f32, rows_f32),
            [pltpu.VMEM((HEADS, count), F32)],
            flops=2 << 30,
            moved=4 << 20,
        )(flipped, v, queries_all, key_grad, value_grad, grads[index - 1])
    result = vmem_call(
        functools.partial(key_grad_body, early, peers, depth),
        rows_bf16,
        [
            pltpu.VMEM((count, 2 * width), BF16),
            pltpu.VMEM((late * count, width), BF16),
            pltpu.VMEM((HEADS, late * count), F32),
        ],
        flops=8 << 30,
        moved=14 << 20,
    )(
        flipped,
        v,
        queries_all,
        normed_grad,
        key_grad,
        value_grad,
        unit,
        slope,
        qkv_one,
        moved_grad,
        *grads[early - 1 :],
    )
    return result.reshape(points.shape)


def solution(mesh):
    in_specs = (
        P("curve", "patch", None, None),
        P(),
        P(),
        P(),
        P("curve", "patch", None),
        P(),
        P(),
        P(),
        P("patch", "curve", None),
        P("patch", "curve", None, None),
    )
    out_specs = P("curve", "patch", None, None)

    return jax.shard_map(shards, mesh=mesh, in_specs=in_specs, out_specs=out_specs, check_vma=False)
```

```python
import functools
import math

import jax
import jax.numpy as jnp
from jax import lax
from jax.experimental import pallas as pl
from jax.experimental.pallas import tpu as pltpu
from jax.sharding import PartitionSpec as P


HEADS = 16
EPS = 1e-06
LANES = 128
MASKED = -1e30
MOST_PERMUTES = 16
F32 = jnp.float32
BF16 = jnp.bfloat16
LOG2E = math.log2(math.e)


def dot_nn(left, right):
    return lax.dot_general(left, right, (((1,), (0,)), ((), ())), preferred_element_type=F32)


def dot_nt(left, right):
    return lax.dot_general(left, right, (((1,), (1,)), ((), ())), preferred_element_type=F32)


def dot_tn(left, right):
    return lax.dot_general(left, right, (((0,), (0,)), ((), ())), preferred_element_type=F32)


def norm_parts(rows):
    wide = rows.astype(F32)
    power = jnp.mean(wide * wide, axis=-1, keepdims=True)
    inverse = lax.rsqrt(power + EPS)
    return wide * inverse, inverse


def norm_rows(rows, gain):
    return (norm_parts(rows)[0] * gain).astype(BF16)


def norm_pull(unit, slope, cotangent):
    scaled = cotangent.astype(F32) * slope
    along = jnp.mean(scaled * unit, axis=-1, keepdims=True)
    return (scaled - unit * along).astype(BF16)


def head_mask(rows, index, depth):
    return lax.broadcasted_iota(jnp.int32, (rows, LANES), 1) // depth == index


def only(mask, tile):
    return jnp.where(mask, tile, jnp.zeros_like(tile))


def tile_at(t):
    if isinstance(t, int):
        return slice(t * LANES, (t + 1) * LANES)
    return pl.ds(pl.multiple_of(t * LANES, LANES), LANES)


def tile_loop(tiles, step, carry):
    for t in range(tiles):
        carry = step(t, carry)
    return carry


def vmem_call(body, outs, scratch=(), flops=0, moved=0, **more):
    params = pltpu.CompilerParams(vmem_limit_bytes=24 << 20, **more.pop("params", {}))
    return pl.pallas_call(
        body,
        out_shape=outs,
        scratch_shapes=scratch,
        compiler_params=params,
        cost_estimate=pl.CostEstimate(flops=flops, bytes_accessed=moved, transcendentals=0),
        **more,
    )


HBM_SPEC = pl.BlockSpec(memory_space=pltpu.MemorySpace.HBM)
SMEM_SPEC = pl.BlockSpec(memory_space=pltpu.MemorySpace.SMEM)
VMEM_SPEC = pl.BlockSpec(memory_space=pltpu.MemorySpace.VMEM)
LOW, HIGH = 2.0**-60, 2.0**100


def column(row):
    return jnp.transpose(jnp.broadcast_to(row.astype(F32), (LANES, row.shape[1])))[:, :1]


def start_all(pairs, sems):
    copies = [pltpu.make_async_copy(src, dst, sems.at[i]) for i, (src, dst) in enumerate(pairs)]
    for copy in copies:
        copy.start()
    return copies


def flip_tile(tile):
    return jnp.transpose(tile)


def with_ones(tile):
    return jnp.concatenate([tile, jnp.ones_like(tile)], axis=1)


def unshifted(depth, t, q_tile, k_tile, v_tile, weights_ref):
    count = q_tile.shape[0]
    scale = depth ** (-0.5) * LOG2E
    heads = LANES // depth
    masks = [head_mask(count, j, depth) for j in range(heads)]
    q_heads = jnp.concatenate([only(mask, q_tile) for mask in masks], axis=0)
    shifted = jnp.exp2(dot_nt(q_heads, k_tile) * scale).astype(BF16)
    weights_ref[t * heads : (t + 1) * heads] = shifted.reshape(heads, count, -1)
    both = dot_nn(shifted, with_ones(v_tile))
    mixed, sums = both[:count, :LANES], both[:count, LANES:]
    for j in range(1, heads):
        part = slice(j * count, (j + 1) * count)
        mixed = jnp.where(masks[j], both[part, :LANES], mixed)
        sums = jnp.where(masks[j], both[part, LANES:], sums)
    return mixed, sums


def route_body(chunks, capacity, me_ref, target_ref, put_ref, take_ref, at_ref):
    count = target_ref.shape[1]
    slots = 2 * count
    target = target_ref[...]
    shift = count.bit_length() - 1
    owner = lax.shift_right_logical(target, jnp.full_like(target, shift))
    offset = target - lax.shift_left(owner, jnp.full_like(target, shift))
    same = column(owner) == owner.astype(F32)
    earlier = lax.broadcasted_iota(jnp.int32, (count, count), 0) < (
        lax.broadcasted_iota(jnp.int32, (count, count), 1)
    )
    ranking = jnp.sum(jnp.where(same & earlier, 1.0, 0.0), axis=0, keepdims=True).astype(jnp.int32)
    lane = owner if chunks == 1 else lax.bitwise_xor(owner, jnp.full_like(owner, me_ref[0]))
    slot = lane * capacity + ranking
    put = lax.broadcasted_iota(jnp.int32, (slots, count), 0) == slot
    put_ref[...] = put.astype(F32).astype(BF16)
    hit = column(slot) == lax.broadcasted_iota(jnp.int32, (count, slots), 1).astype(F32)
    take_ref[...] = hit.astype(F32).astype(BF16)
    at = jnp.sum(jnp.where(hit, column(offset) - count, 0.0), axis=0, keepdims=True) + count
    at_ref[...] = at.astype(at_ref.dtype)


def prep_body(depth, *refs):
    x_ref, gain_ref, w_ref = refs[:3]
    q_ref, k_ref, v_ref, weights_ref, mixed_ref, sums_ref, unit_ref, slope_ref = refs[3:]
    width = x_ref.shape[1]
    unit, inverse = norm_parts(x_ref[...])
    unit_ref[...] = unit
    slope_ref[...] = inverse * gain_ref[...]
    normed = (unit * gain_ref[...]).astype(BF16)
    q_ref[...] = dot_nn(normed, w_ref[:, :width]).astype(BF16)
    k_ref[...] = dot_nn(normed, w_ref[:, width : 2 * width]).astype(BF16)
    v_ref[...] = dot_nn(normed, w_ref[:, 2 * width :]).astype(BF16)

    def tile_step(t, carry):
        at = tile_at(t)
        mixed_ref[:, at], sums_ref[:, at] = unshifted(
            depth, t, q_ref[:, at], k_ref[:, at], v_ref[:, at], weights_ref
        )
        return carry

    tile_loop(width // LANES, tile_step, 0)


def middle_body(depth, *refs):
    x_ref, gain_ref, w_ref, q_ref, mixed_in_ref, sums_in_ref = refs[:6]
    k_ref, v_ref, weights_ref, mixed_ref, sums_ref = refs[6:]
    width = x_ref.shape[1]
    normed = norm_rows(x_ref[...], gain_ref[...])
    k_ref[...] = dot_nn(normed, w_ref[:, width : 2 * width]).astype(BF16)
    v_ref[...] = dot_nn(normed, w_ref[:, 2 * width :]).astype(BF16)

    def tile_step(t, carry):
        at = tile_at(t)
        mixed, sums = unshifted(depth, t, q_ref[:, at], k_ref[:, at], v_ref[:, at], weights_ref)
        mixed_ref[:, at] = mixed + mixed_in_ref[:, at]
        sums_ref[:, at] = sums + sums_in_ref[:, at]
        return carry

    tile_loop(width // LANES, tile_step, 0)


def forward_body(early, peers, chunks, capacity, depth, *refs):
    x_ref, gain_ref, w_ref, out_w_ref, put_ref, at_ref, q_ref, mixed_in_ref, sums_in_ref = refs[:9]
    refs = refs[9:]
    early_keys, early_values, refs = refs[:early], refs[early : 2 * early], refs[2 * early :]
    others, refs = refs[: peers + 1 - early], refs[peers + 1 - early + early :]
    keys_ref, values_ref, weights_ref, mixed_ref, inverse_ref, lse_ref = refs[:6]
    early_weights, refs = refs[6 : 6 + early], refs[6 + early :]
    sends, (mixed_low, safe, out_sems) = refs[:chunks], refs[chunks:]
    count, width = x_ref.shape
    heads = LANES // depth
    for index, other in enumerate(others):
        rows = slice(index * count, (index + 1) * count)
        normed = norm_rows(other[...], gain_ref[...])
        keys_ref[rows] = dot_nn(normed, w_ref[:, width : 2 * width]).astype(BF16)
        values_ref[rows] = dot_nn(normed, w_ref[:, 2 * width :]).astype(BF16)

    def finish_tile(t, at, mixed, sums, tops):
        inverse = 1.0 / sums
        mixed_ref[:, at] = mixed * inverse
        mixed_low[:, at] = (mixed * inverse).astype(BF16)
        inverse_ref[:, at] = inverse
        flipped = flip_tile(tops + jnp.log(sums) * LOG2E)
        for j in range(heads):
            lse_ref[pl.ds(t * heads + j, 1)] = flipped[j * depth : j * depth + 1]

    def fast_step(t, bad):
        at = tile_at(t)
        mixed, sums = unshifted(
            depth, t, q_ref[:, at], keys_ref[:, at], values_ref[:, at], weights_ref
        )
        mixed += mixed_in_ref[:, at]
        sums += sums_in_ref[:, at]
        finish_tile(t, at, mixed, sums, 0.0)
        return jnp.where((sums >= LOW) & (sums <= HIGH), bad, 1.0)

    bad = tile_loop(width // LANES, fast_step, jnp.zeros((count, LANES), F32))

    @pl.when(jnp.max(bad) > 0.0)
    def _():
        scale = depth ** (-0.5) * LOG2E

        def safe_step(t, carry):
            at = tile_at(t)
            keys = jnp.concatenate([ref[:, at] for ref in early_keys + (keys_ref,)], axis=0)
            values = jnp.concatenate([ref[:, at] for ref in early_values + (values_ref,)], axis=0)
            right = with_ones(values)
            mixed = jnp.zeros((count, LANES), F32)
            sums = jnp.ones((count, LANES), F32)
            tops = jnp.zeros((count, LANES), F32)
            for j in range(heads):
                mask = head_mask(count, j, depth)
                scores = dot_nt(only(mask, q_ref[:, at]), keys)
                top = jnp.max(scores, axis=-1, keepdims=True) * scale
                shifted = jnp.exp2(scores * scale - top).astype(BF16)
                weights_ref[t * heads + j] = shifted[:, early * count :]
                for index in range(early):
                    part = shifted[:, index * count : (index + 1) * count]
                    safe[index, t * heads + j] = part
                both = dot_nn(shifted, right)
                mixed = jnp.where(mask, both[:, :LANES], mixed)
                sums = jnp.where(mask, both[:, LANES:], sums)
                tops = jnp.where(mask, top, tops)
            finish_tile(t, at, mixed, sums, tops)
            return carry

        lax.fori_loop(0, width // LANES, safe_step, 0)
        pairs = [(safe.at[index], early_weights[index]) for index in range(early)]
        for copy in start_all(pairs, out_sems):
            copy.wait()

    moved = (x_ref[...].astype(F32) + dot_nn(mixed_low[...], out_w_ref[...])).astype(BF16)
    slots = 2 * count
    leaving = dot_nn(put_ref[...], moved).astype(BF16)
    if chunks == 1:
        sends[0][...] = leaving
    else:
        tail = sends[0].shape[0] - capacity * (width // LANES)
        line = jnp.broadcast_to(at_ref[...], (tail, slots)).astype(BF16)
        for m, send in enumerate(sends):
            part = slice(m * capacity, (m + 1) * capacity)
            for t in range(width // LANES):
                tile = leaving[part, t * LANES : (t + 1) * LANES]
                send[t * capacity : (t + 1) * capacity] = tile
            padding = jnp.zeros((tail, LANES - capacity), BF16)
            send[send.shape[0] - tail :] = jnp.concatenate([line[:, part], padding], axis=1)


def second_early_body(seg_ref, out_w_ref, grad_ref, mixed_grad_ref, bias_ref):
    mixed_grad_ref[...] = dot_nt(grad_ref[...], out_w_ref[...]).astype(BF16)
    bias_ref[...] = jnp.where(column(seg_ref[...]) == seg_ref[...].astype(F32), 0.0, MASKED)


def second_body(chunks, depth, *refs):
    land_ref, gain_ref, w_ref, grad_ref, mixed_grad, bias = refs[:6]
    arrived = refs[6 : 6 + chunks]
    sends = refs[6 + chunks : 6 + 2 * chunks]
    packed, packed_grad = refs[6 + 2 * chunks :]
    count, width = grad_ref.shape
    slots = 2 * count
    size = slots // chunks
    if chunks == 1:
        landing = land_ref[...].astype(F32)
        rows = arrived[0][...]
    else:
        ends = [piece[size * (width // LANES) :].astype(F32)[:1, :size] for piece in arrived]
        landing = jnp.concatenate(ends, axis=1)
        rows = []
        for piece in arrived:
            tiles = [piece[t * size : (t + 1) * size] for t in range(width // LANES)]
            rows.append(jnp.concatenate(tiles, axis=1))
        rows = jnp.concatenate(rows, axis=0)
    place = lax.broadcasted_iota(jnp.int32, (count, slots), 0).astype(F32) == landing
    place = place.astype(F32)
    hilbert = dot_nn(place.astype(BF16), rows).astype(BF16)
    unit, inverse = norm_parts(hilbert)
    packed[...] = dot_nn((unit * gain_ref[...]).astype(BF16), w_ref[...]).astype(BF16)
    scale = depth ** (-0.5)

    tiles = width // LANES
    heads = LANES // depth
    masks = [head_mask(count, j, depth) for j in range(heads)]
    stacked = (heads, count, count)

    def products(t):
        k_tile = packed[:, tile_at(t + tiles)]
        v_tile = packed[:, tile_at(t + 2 * tiles)]
        k_heads = jnp.concatenate([only(mask, k_tile) for mask in masks], axis=0)
        v_heads = jnp.concatenate([only(mask, v_tile) for mask in masks], axis=0)
        scores = dot_nt(k_heads, packed[:, tile_at(t)])
        return scores, dot_nt(v_heads, mixed_grad[:, tile_at(t)])

    def softmax(scores, weight_grad):
        scores = scores.reshape(stacked) * (scale * LOG2E) + bias[...][None]
        weight_grad = weight_grad.reshape(stacked)
        shifted = jnp.exp2(scores - jnp.max(scores, axis=1, keepdims=True))
        inverse = 1.0 / jnp.sum(shifted, axis=1, keepdims=True)
        carried = jnp.sum(shifted * weight_grad, axis=1, keepdims=True) * inverse
        weights = shifted * inverse
        score_grad = (weights * (weight_grad - carried)).astype(BF16)
        return weights.astype(BF16), score_grad

    def gradients(t, weights, score_grad):
        at = tile_at(t)
        k_at, v_at = tile_at(t + tiles), tile_at(t + 2 * tiles)
        k_flipped = flip_tile(packed[:, k_at])
        dk_heads = dot_nn(score_grad.reshape(heads * count, count), packed[:, at])
        dv_heads = dot_nn(weights.reshape(heads * count, count), mixed_grad[:, at])
        dk, dv, dq = dk_heads[:count], dv_heads[:count], []
        for j in range(heads):
            part = slice(j * count, (j + 1) * count)
            dk = jnp.where(masks[j], dk_heads[part], dk)
            dv = jnp.where(masks[j], dv_heads[part], dv)
            dq.append(dot_nn(k_flipped[j * depth : (j + 1) * depth], score_grad[j]))
        dq = jnp.transpose(jnp.concatenate(dq, axis=0))
        packed_grad[:, at] = (dq * scale).astype(BF16)
        packed_grad[:, k_at] = (dk * scale).astype(BF16)
        packed_grad[:, v_at] = dv.astype(BF16)

    ahead = products(0)
    for t in range(tiles):
        now, ahead = ahead, products(t + 1) if t + 1 < tiles else None
        gradients(t, *softmax(*now))
    normed_grad = dot_nt(packed_grad[...], w_ref[...]).astype(BF16)
    path = norm_pull(unit, inverse * gain_ref[...], normed_grad)
    total = grad_ref[...].astype(F32) + path.astype(F32)
    back = lax.broadcasted_iota(jnp.int32, (slots, count), 1).astype(F32) == column(landing)
    returning = dot_nn(back.astype(F32).astype(BF16), total.astype(BF16)).astype(BF16)
    for m, send in enumerate(sends):
        send[...] = returning[m * size : (m + 1) * size]


def queries_body(peers, *refs):
    gain_ref, w_ref, q_ref = refs[:3]
    others = refs[3 : 3 + peers]
    out_ref = refs[3 + peers]
    count, width = q_ref.shape
    out_ref[:count] = q_ref[...]
    for index, other in enumerate(others):
        rows = slice((index + 1) * count, (index + 2) * count)
        normed = norm_rows(other[...], gain_ref[...])
        out_ref[rows] = dot_nn(normed, w_ref[:, :width]).astype(BF16)


def spread(rows, width):
    heads = rows.shape[0]
    pick = lax.broadcasted_iota(jnp.int32, (heads, width), 1) // (width // heads) == (
        lax.broadcasted_iota(jnp.int32, (heads, width), 0)
    )
    return dot_tn(rows, pick.astype(F32).astype(BF16))


def weights_flipped_body(peers, depth, *refs):
    k_ref, queries_ref = refs[:2]
    lse_refs = refs[2 : 3 + peers]
    out_ref = refs[3 + peers]
    scale = depth ** (-0.5) * LOG2E
    heads = LANES // depth
    count = k_ref.shape[0]

    def tile_step(t, carry):
        at = tile_at(t)
        for j in range(heads):
            mask = head_mask(count, j, depth)
            scores = dot_nt(only(mask, k_ref[:, at]), queries_ref[:, at])
            h = t * heads + j
            line = jnp.concatenate([ref[pl.ds(h, 1)] for ref in lse_refs], axis=1)
            out_ref[h] = jnp.exp2(scores * scale - line).astype(BF16)
        return carry

    tile_loop(k_ref.shape[1] // LANES, tile_step, 0)


def home_body(chunks, depth, *refs):
    take_ref, mixed_ref, out_w_ref = refs[:3]
    home = refs[3 : 3 + chunks]
    moved_ref, grad_ref, delta_ref = refs[3 + chunks :]
    count, width = moved_ref.shape
    rows = jnp.concatenate([piece[...] for piece in home], axis=0)
    moved = dot_nn(take_ref[...], rows).astype(BF16)
    moved_ref[...] = moved
    grad = dot_nt(moved, out_w_ref[...]).astype(BF16)
    grad_ref[:count] = grad
    product = grad.astype(F32) * mixed_ref[...]
    high = product.astype(BF16)
    low = (product - high.astype(F32)).astype(BF16)
    heads = width // depth
    pick = lax.broadcasted_iota(jnp.int32, (heads, width), 1) // depth == (
        lax.broadcasted_iota(jnp.int32, (heads, width), 0)
    )
    pick = pick.astype(F32).astype(BF16)
    delta = dot_nt(pick, high) + dot_nt(pick, low)
    delta_ref[...] = delta
    beside = width // count
    tail = heads // beside
    rest = delta
    for term in range(2):
        rounded = rest.astype(BF16)
        rest -= rounded.astype(F32)
        rows = slice(count + term * tail, count + (term + 1) * tail)
        for part in range(beside):
            lines = rounded[part * tail : (part + 1) * tail]
            grad_ref[rows, part * count : (part + 1) * count] = lines


def key_tile(depth, t, v_tile, weights_ref, columns, queries, grads, deltas_ref):
    count = v_tile.shape[0]
    heads = LANES // depth
    masks = [head_mask(count, j, depth) for j in range(heads)]
    v_heads = jnp.concatenate([only(mask, v_tile) for mask in masks], axis=0)
    weights = weights_ref[t * heads : (t + 1) * heads, :, columns]
    weight_grad = dot_nt(v_heads, grads).reshape(weights.shape)
    delta = deltas_ref[t * heads : (t + 1) * heads][:, None, :]
    score_grad = (weights.astype(F32) * (weight_grad - delta)).astype(BF16)
    dv_heads = dot_nn(weights.reshape(heads * count, -1), grads)
    dk_heads = dot_nn(score_grad.reshape(heads * count, -1), queries)
    dk, dv = dk_heads[:count], dv_heads[:count]
    for j in range(1, heads):
        part = slice(j * count, (j + 1) * count)
        dk = jnp.where(masks[j], dk_heads[part], dk)
        dv = jnp.where(masks[j], dv_heads[part], dv)
    return dk, dv


def heads_apart(lines, count):
    wide = lines.astype(F32)
    wide = wide[: wide.shape[0] // 2] + wide[wide.shape[0] // 2 :]
    parts = [wide[:, i * count : (i + 1) * count] for i in range(lines.shape[1] // count)]
    return jnp.concatenate(parts, axis=0)


def query_grad_body(parts, depth, *refs):
    weights_refs, refs = refs[:parts], refs[parts:]
    keys_refs, refs = refs[:parts], refs[parts:]
    values_refs, refs = refs[:parts], refs[parts:]
    inverse_ref, flipped_ref, grad_ref, lines, q_ref, w_ref = refs[:6]
    normed_ref, dk_ref, dv_ref, dq_all, wide = refs[6:]
    count, width = q_ref.shape
    heads = LANES // depth
    high = lines[...].astype(BF16)
    low = (lines[...] - high.astype(F32)).astype(BF16)
    wide[...] = spread(high, width) + spread(low, width)

    def tile_step(t, carry):
        at = tile_at(t)
        g_tile = grad_ref[:count, at]
        delta_tile = wide[:, at]
        keys = jnp.concatenate([ref[:, at] for ref in keys_refs], axis=0)
        values = jnp.concatenate([ref[:, at] for ref in values_refs], axis=0)
        dq = jnp.zeros((count, LANES), F32)
        for j in range(heads):
            mask = head_mask(count, j, depth)
            weight_grad = dot_nt(only(mask, g_tile), values)
            delta = delta_tile[:, j * depth : j * depth + 1]
            weights = jnp.concatenate([ref[t * heads + j] for ref in weights_refs], axis=1)
            score_grad = (weights.astype(F32) * (weight_grad - delta)).astype(BF16)
            dq = jnp.where(mask, dot_nn(score_grad, keys), dq)
        dq_all[:, at] = (dq * (inverse_ref[:, at] * depth ** (-0.5))).astype(BF16)
        dk_ref[:, at], dv_ref[:, at] = key_tile(
            depth,
            t,
            values_refs[0][:, at],
            flipped_ref,
            slice(0, count),
            q_ref[:, at],
            g_tile,
            lines,
        )
        return carry

    tile_loop(width // LANES, tile_step, 0)
    normed_ref[...] = dot_nt(dq_all[...], w_ref[:, :width])


def key_middle_body(index, depth, *refs):
    flipped_ref, v_ref, queries_ref, dk_in_ref, dv_in_ref, grad_ref = refs[:6]
    dk_ref, dv_ref, lines = refs[6:]
    count, width = v_ref.shape
    lines[...] = heads_apart(grad_ref[count:], count)
    rows = slice(index * count, (index + 1) * count)

    def tile_step(t, carry):
        at = tile_at(t)
        dk, dv = key_tile(
            depth,
            t,
            v_ref[:, at],
            flipped_ref,
            rows,
            queries_ref[rows, at],
            grad_ref[:count, at],
            lines,
        )
        dk_ref[:, at] = dk + dk_in_ref[:, at]
        dv_ref[:, at] = dv + dv_in_ref[:, at]
        return carry

    tile_loop(width // LANES, tile_step, 0)


def key_grad_body(early, peers, depth, *refs):
    flipped_ref, v_ref, queries_ref, normed_ref, dk_ref, dv_ref = refs[:6]
    unit_ref, slope_ref, w_ref, moved_ref = refs[6:10]
    others = refs[10 : 11 + peers - early]
    out_ref, packed_grad, grads, lines = refs[11 + peers - early :]
    count, width = unit_ref.shape
    for i, other in enumerate(others):
        rows = slice(i * count, (i + 1) * count)
        grads[rows] = other[:count]
        lines[:, rows] = heads_apart(other[count:], count)

    def tile_step(t, carry):
        at = tile_at(t)
        dk, dv = key_tile(
            depth,
            t,
            v_ref[:, at],
            flipped_ref,
            slice(early * count, (peers + 1) * count),
            queries_ref[early * count :, at],
            grads[:, at],
            lines,
        )
        dk = (dk + dk_ref[:, at]) * depth ** (-0.5)
        packed_grad[:, at] = dk.astype(BF16)
        packed_grad[:, tile_at(t + width // LANES)] = (dv + dv_ref[:, at]).astype(BF16)
        return carry

    tile_loop(width // LANES, tile_step, 0)
    normed_grad = normed_ref[...] + dot_nt(packed_grad[...], w_ref[:, width:])
    path = norm_pull(unit_ref[...], slope_ref[...], normed_grad.astype(BF16))
    out_ref[...] = (moved_ref[...].astype(F32) + path.astype(F32)).astype(BF16)


def single_first(size):
    return sorted(range(1, size), key=lambda step: (step.bit_count(), -step))


def by_xor(array, axis, step):
    size = lax.axis_size(axis)
    return lax.ppermute(array, axis, [(i, i ^ step) for i in range(size)])


def exchange(pieces, axis):
    if len(pieces) == 1:
        size = lax.axis_size(axis)
        stacked = pieces[0].reshape((size, -1) + pieces[0].shape[1:])
        got = lax.all_to_all(stacked, axis, split_axis=0, concat_axis=0, tiled=True)
        return [got.reshape(pieces[0].shape)]
    return [pieces[0]] + [by_xor(pieces[m], axis, m) for m in range(1, len(pieces))]


def shards(
    points, gain_one, qkv_one, out_one, hilbert_pos, gain_two, qkv_two, out_two, segments, out_grad
):
    count, width = points.shape[2:]
    depth = width // HEADS
    tiles = width // LANES
    patch_size = lax.axis_size("patch")
    curve_size = lax.axis_size("curve")
    peers = patch_size - 1
    total = patch_size * count
    slots = 2 * count
    capacity = slots // curve_size
    chunks = curve_size if curve_size <= MOST_PERMUTES else 1
    rows_bf16 = jax.ShapeDtypeStruct((count, width), BF16)
    all_bf16 = jax.ShapeDtypeStruct((total, width), BF16)
    chunk_bf16 = jax.ShapeDtypeStruct((slots // chunks, width), BF16)

    x = points.reshape(count, width)
    steps = single_first(patch_size)
    others = [by_xor(x, "patch", m) for m in steps]
    gain_one = gain_one.reshape(1, width)
    gain_two = gain_two.reshape(1, width)

    def shape(kind, *dims):
        return jax.ShapeDtypeStruct(dims, kind)

    me = lax.axis_index("curve").astype(jnp.int32).reshape(1)
    put, take, leaving_at = vmem_call(
        functools.partial(route_body, chunks, capacity),
        (shape(BF16, slots, count), shape(BF16, count, slots))
        + (shape(jnp.int32 if chunks == 1 else F32, 1, slots),),
        flops=8 << 30,
        moved=16 << 20,
        in_specs=[SMEM_SPEC, VMEM_SPEC],
    )(me, hilbert_pos.reshape(1, count))
    x_then, put, take, leaving_at = lax.optimization_barrier((x, put, take, leaving_at))
    landing = leaving_at
    if chunks == 1:
        landing = lax.all_to_all(
            leaving_at.reshape(curve_size, 1, capacity),
            "curve",
            split_axis=0,
            concat_axis=0,
            tiled=True,
        ).reshape(1, slots)

    rows_f32 = shape(F32, count, width)
    lines_f32 = shape(F32, HEADS, count)
    square = shape(BF16, HEADS, count, count)
    dma = pltpu.SemaphoreType.DMA
    q, k, v, own_weights, sum_mixed, sums, unit, slope = vmem_call(
        functools.partial(prep_body, depth),
        (rows_bf16,) * 3 + (square,) + (rows_f32,) * 4,
        flops=2 << 30,
        moved=4 << 20,
    )(x_then, gain_one, qkv_one)
    early_keys, early_values, early_weights = [k], [v], [own_weights]
    for other in others[: peers - 1]:
        k_next, v_next, weights_next, sum_mixed, sums = vmem_call(
            functools.partial(middle_body, depth),
            (rows_bf16,) * 2 + (square,) + (rows_f32,) * 2,
            flops=2 << 30,
            moved=4 << 20,
        )(other, gain_one, qkv_one, q, sum_mixed, sums)
        early_keys.append(k_next)
        early_values.append(v_next)
        early_weights.append(weights_next)
    early = len(early_keys)
    late = peers + 1 - early
    late_bf16 = shape(BF16, late * count, width)
    embedded = shape(BF16, capacity * tiles + 8, LANES)
    sent = chunk_bf16 if chunks == 1 else embedded
    first_weights = 9 + 2 * early + late
    results = vmem_call(
        functools.partial(forward_body, early, peers, chunks, capacity, depth),
        (late_bf16, late_bf16, shape(BF16, HEADS, count, late * count))
        + (rows_f32, rows_f32, lines_f32)
        + (square,) * early
        + (sent,) * chunks,
        [
            pltpu.VMEM((count, width), BF16),
            pltpu.VMEM((early,) + square.shape, BF16),
            dma((early,)),
        ],
        flops=8 << 30,
        moved=8 << 20,
        in_specs=[VMEM_SPEC] * first_weights + [HBM_SPEC] * early,
        out_specs=(VMEM_SPEC,) * 6 + (HBM_SPEC,) * early + (VMEM_SPEC,) * chunks,
        input_output_aliases={first_weights + index: 6 + index for index in range(early)},
    )(
        x,
        gain_one,
        qkv_one,
        out_one,
        put,
        leaving_at,
        q,
        sum_mixed,
        sums,
        *early_keys,
        *early_values,
        *others[early - 1 :],
        *early_weights,
    )
    late_keys, late_values, late_weights, mixed, inverse, lse = results[:6]
    all_weights = list(results[6 : 6 + early]) + [late_weights]
    all_keys, all_values = early_keys + [late_keys], early_values + [late_values]
    arrived = exchange(results[6 + early :], "curve")
    lse_all = [lse] + [by_xor(lse, "patch", m) for m in steps]

    out_grad_then, inverse = lax.optimization_barrier((out_grad, inverse))
    queries_all = vmem_call(
        functools.partial(queries_body, peers),
        all_bf16,
        flops=1 << 29,
        moved=3 << 20,
        in_specs=[VMEM_SPEC] * (3 + peers),
    )(gain_one, qkv_one, q, *others)
    flipped = vmem_call(
        functools.partial(weights_flipped_body, peers, depth),
        shape(BF16, HEADS, count, total),
        flops=4 << 30,
        moved=10 << 20,
    )(k, queries_all, *lse_all)

    second_mixed, bias = vmem_call(
        second_early_body, (rows_bf16, shape(F32, count, count)), flops=1 << 29, moved=1 << 20
    )(segments.reshape(1, count), out_two, out_grad_then.reshape(count, width))
    returning = vmem_call(
        functools.partial(second_body, chunks, depth),
        (chunk_bf16,) * chunks,
        [pltpu.VMEM((count, 3 * width), BF16), pltpu.VMEM((count, 3 * width), BF16)],
        flops=8 << 30,
        moved=4 << 20,
    )(
        landing,
        gain_two,
        qkv_two,
        out_grad_then.reshape(count, width),
        second_mixed,
        bias,
        *arrived,
    )
    home = exchange(returning, "curve")

    moved_grad, grad_own, delta = vmem_call(
        functools.partial(home_body, chunks, depth),
        (rows_bf16, shape(BF16, count + 2 * HEADS * count // width, width), lines_f32),
        flops=1 << 29,
        moved=2 << 20,
    )(take, mixed, out_one, *home)
    grads = [by_xor(grad_own, "patch", m) for m in steps]

    normed_grad, key_grad, value_grad = vmem_call(
        functools.partial(query_grad_body, len(all_keys), depth),
        (rows_f32, rows_f32, rows_f32),
        [
            pltpu.VMEM((count, width), BF16),
            pltpu.VMEM((count, width), F32),
        ],
        flops=8 << 30,
        moved=10 << 20,
    )(*all_weights, *all_keys, *all_values, inverse, flipped, grad_own, delta, q, qkv_one)
    for index in range(1, early):
        key_grad, value_grad = vmem_call(
            functools.partial(key_middle_body, index, depth),
            (rows_f32, rows_f32),
            [pltpu.VMEM((HEADS, count), F32)],
            flops=2 << 30,
            moved=4 << 20,
        )(flipped, v, queries_all, key_grad, value_grad, grads[index - 1])
    result = vmem_call(
        functools.partial(key_grad_body, early, peers, depth),
        rows_bf16,
        [
            pltpu.VMEM((count, 2 * width), BF16),
            pltpu.VMEM((late * count, width), BF16),
            pltpu.VMEM((HEADS, late * count), F32),
        ],
        flops=8 << 30,
        moved=14 << 20,
    )(
        flipped,
        v,
        queries_all,
        normed_grad,
        key_grad,
        value_grad,
        unit,
        slope,
        qkv_one,
        moved_grad,
        *grads[early - 1 :],
    )
    return result.reshape(points.shape)


def solution(mesh):
    in_specs = (
        P("curve", "patch", None, None),
        P(),
        P(),
        P(),
        P("curve", "patch", None),
        P(),
        P(),
        P(),
        P("patch", "curve", None),
        P("patch", "curve", None, None),
    )
    out_specs = P("curve", "patch", None, None)

    return jax.shard_map(shards, mesh=mesh, in_specs=in_specs, out_specs=out_specs, check_vma=False)
```
